32 devices in a mesh: shard: 4 (over z), context: 2 (over x), tensor: 4 (over y, core).
Axes of the slice: x: 2, y: 2, z: 4, core: 2. Of those that a mesh axis runs over, the one named last changes fastest.
Arguments:
- tokens: bfloat16 [4, 2048, 1024], P('shard', ('context', 'tensor'))
- piece_ids: int32 [4, 2048], P('shard', 'context'), may hold values from 0 to 4, as said below
- tok_qkv: bfloat16 [1024, 8, 384], P('shard', 'tensor'), may hold values from -0.1875 to 0.1875
- state_qkv: bfloat16 [1024, 8, 384], P('shard', 'tensor'), may hold values from -0.1875 to 0.1875
- tok_out: bfloat16 [8, 128, 1024], P('tensor', None, 'shard'), may hold values from -0.75 to 0.75
- state_out: bfloat16 [8, 128, 1024], P('tensor', None, 'shard'), may hold values from -0.75 to 0.75
- mlp_in: bfloat16 [1024, 4096], P('shard', 'tensor'), may hold values from -0.1875 to 0.1875
- mlp_out: bfloat16 [4096, 1024], P('tensor', 'shard'), may hold values from -0.09375 to 0.09375
- rel_bias: bfloat16 [32, 8], P('shard', 'tensor'), may hold values from -4 to 4
- init_state: bfloat16 [512, 1024], P('tensor', 'shard'), may hold values from -5 to 5
- norm_gains: bfloat16 [3, 1024], P(None, ('shard', 'tensor')), may hold values from 0.5 to 1.5
- decay_param: bfloat16 [1024], P(('shard', 'tensor')), may hold values from 1 to 4
- cotangent: bfloat16 [4, 2048, 1024], P('shard', ('context', 'tensor')), may hold values from -6 to 6
Outputs:
- output: bfloat16 [4, 2048, 1024], P('shard', ('context', 'tensor'))
- grad_tokens: bfloat16 [4, 2048, 1024], P('shard', ('context', 'tensor'))
- grad_tok_qkv: float32 [1024, 8, 384], P('shard', 'tensor')
- grad_state_qkv: float32 [1024, 8, 384], P('shard', 'tensor')
- grad_tok_out: float32 [8, 128, 1024], P('tensor', None, 'shard')
- grad_state_out: float32 [8, 128, 1024], P('tensor', None, 'shard')
- grad_mlp_in: float32 [1024, 4096], P('shard', 'tensor')
- grad_mlp_out: float32 [4096, 1024], P('tensor', 'shard')
- grad_rel_bias: float32 [32, 8], P('shard', 'tensor')
- grad_init_state: float32 [512, 1024], P('tensor', 'shard')
- grad_norm_gains: float32 [3, 1024], P(None, ('shard', 'tensor'))
- grad_decay_param: float32 [1024], P(('shard', 'tensor'))
- rms_out: float32 [3], replicated
The draws below stay inside these ranges and needn't reach their ends.
Inputs may be any that keep to these rules, and one draw needn't show every extreme that they name: `piece_ids`: in every aligned block of 512 positions of a sequence exactly 256 consecutive positions form one picture piece and hold the number of that block plus one (1 for the first block); all other positions hold 0.
All inputs are finite; a program needn't handle non-finite values.
Results may differ from the reference program's by a relative error of at most 0.024.
Values may be sent and summed in bfloat16 or wider, within the bound.
No kernel may reach another device: no remote copies, remote signals or barrier semaphores. Data moves between devices by JAX's collectives and lax.ppermute only.
A program may use at most 192 MiB of HBM per device.

```python
import jax
import jax.numpy as jnp
import numpy as np
from jax import lax

D = 1024
H = 8
HS = 128
FF = 4096
NSTATE = 512
BLK = 512
NBUCKET = 32
PIECE = 256
LEN = 2048
SEQS = 4


def draw_tokens(key, part):
    seq_pos = jnp.arange(SEQS, dtype=jnp.float32)[:, None, None] / max(SEQS - 1, 1)
    tok_pos = jnp.arange(LEN, dtype=jnp.float32)[None, :, None] / (LEN - 1)
    rising = 0.3 * jnp.exp(jnp.log(3.0) * (seq_pos + tok_pos))
    key_base, key_rows = jax.random.split(key)
    normal_part = jax.random.normal(key_base, (SEQS, LEN, D), jnp.float32)
    roughness = jnp.exp(jax.random.uniform(key_rows, (SEQS, LEN, 1), jnp.float32, 0.0, 0.7))
    return (normal_part * rising * roughness).astype(jnp.bfloat16)


def draw_piece_ids(key, part):
    block_count = LEN // BLK
    starts = jax.random.randint(key, (SEQS, block_count, 1), 0, BLK - PIECE + 1)
    offset = jnp.arange(BLK, dtype=jnp.int32)[None, None, :]
    inside = (offset >= starts) & (offset < starts + PIECE)
    labels = jnp.arange(1, block_count + 1, dtype=jnp.int32)[None, :, None]
    return jnp.where(inside, labels, 0).reshape(SEQS, LEN).astype(jnp.int32)


def shard_levels(key, extent, shards, least, high):
    level = 1.0
    for position, parts in shards:
        draws = jax.random.uniform(jax.random.fold_in(jax.random.fold_in(key, 6), position), (parts,), jnp.float32, least / len(shards), high / len(shards))
        level = level * jnp.repeat(jnp.exp(draws), extent[position] // parts).reshape((-1,) + (1,) * (len(extent) - 1 - position))
    return level


def bell_draw(own_key, dims, deviation, reach, pieces=(), kind=jnp.bfloat16):
    result = jax.random.normal(own_key, dims, jnp.float32) * deviation
    if len(pieces) > 0:
        result = shard_levels(own_key, dims, pieces, -0.22, 0.18) * result
    return jnp.clip(result, min=-reach, max=reach).astype(kind)


def setup_inputs(seed: int = 0) -> dict:
    key_of = jax.random.split(jax.random.key(seed), 14)
    return {
        "tokens": draw_tokens(jax.random.fold_in(key_of[13], 71), 0),
        "piece_ids": draw_piece_ids(jax.random.fold_in(key_of[13], 71), 0),
        "tok_qkv": bell_draw(key_of[2], (D, H, 3 * HS), D ** -0.5, 0.1875, ((0, 4), (1, 4))),
        "state_qkv": bell_draw(key_of[3], (D, H, 3 * HS), D ** -0.5, 0.1875, ((0, 4), (1, 4))),
        "tok_out": bell_draw(key_of[4], (H, HS, D), (D // 16) ** -0.5, 0.75, ((0, 4), (2, 4))),
        "state_out": bell_draw(key_of[5], (H, HS, D), (D // 16) ** -0.5, 0.75, ((0, 4), (2, 4))),
        "mlp_in": bell_draw(key_of[6], (D, FF), D ** -0.5, 0.1875, ((0, 4), (1, 4))),
        "mlp_out": bell_draw(key_of[7], (FF, D), FF ** -0.5, 0.09375, ((0, 4), (1, 4))),
        "rel_bias": bell_draw(key_of[8], (NBUCKET, H), 1.0, 4.0, ((0, 4), (1, 4))),
        "init_state": bell_draw(key_of[9], (NSTATE, D), 1.0, 5.0, ((0, 4), (1, 4))),
        "norm_gains": jnp.clip(1.0 + 0.1 * jax.random.normal(key_of[10], (3, D), jnp.float32), 0.5, 1.5).astype(jnp.bfloat16),
        "decay_param": jnp.clip(1.0 + 3.0 * jax.random.uniform(key_of[11], (D,), jnp.float32) ** shard_levels(key_of[11], (D,), ((0, 16),), -0.2, 0.2), 1.0, 4.0).astype(jnp.bfloat16),
        "cotangent": bell_draw(key_of[12], (SEQS, LEN, D), 1.0, 6.0, ((0, 4), (1, 8))),
    }


HIGHEST = lax.Precision.HIGHEST
EDGES = (12, 16, 23, 32, 46, 64, 91)

@jax.custom_vjp
def low(v):
    return lax.optimization_barrier(v.astype(jnp.bfloat16)).astype(jnp.float32)

@jax.custom_vjp
def low_back(v):
    return v

def low_keep(v):
    return (low(v), None)

def low_pass(kept, grad):
    return (grad,)

def back_keep(v):
    return (v, None)

def back_low(kept, grad):
    return (low(grad),)
low.defvjp(low_keep, low_pass)
low_back.defvjp(back_keep, back_low)

def both_ways(value):
    return low_back(low(value))

def bucket_of(offsets):
    distance = np.abs(offsets)
    far_part = 8 + np.sum(distance[..., None] >= np.array(EDGES), axis=-1)
    near_part = np.where(distance < 8, distance, far_part)
    return np.where(offsets < 0, 16 + near_part, near_part)

def root_mean(features, gain_row):
    return features * lax.rsqrt(lax.optimization_barrier(jnp.mean(features * features, axis=-1, keepdims=True)) + 1e-06) * gain_row

def one_sequence(inputs, piece_row, params):
    tok_qkv, state_qkv, tok_out, state_out, mlp_in, mlp_out, rel_bias, init_state, norm_gains, decay_param = params
    scaling = HS ** (-0.5)
    decay_rate = jax.nn.sigmoid(decay_param)
    query_pos = np.arange(BLK)[:, None]
    key_pos = np.arange(2 * BLK)[None, :]
    window_bias = jnp.transpose(rel_bias[bucket_of(query_pos + BLK - key_pos)], (2, 0, 1))
    bias_all = jnp.concatenate([jnp.zeros((H, BLK, NSTATE), jnp.float32), window_bias], axis=-1)
    causal = np.arange(BLK)[None, :] <= np.arange(BLK)[:, None]
    normed = low(root_mean(inputs, norm_gains[0]))
    projected = jnp.einsum('ld,dhe->lhe', normed, tok_qkv, precision=HIGHEST)
    queries = both_ways(projected[..., :HS])
    keys_tok = both_ways(projected[..., HS:2 * HS])
    values_tok = both_ways(projected[..., 2 * HS:])
    state_now = init_state
    mixed_list = []
    for block_idx in range(LEN // BLK):
        lower = block_idx * BLK
        upper = lower + BLK
        keys_cur = keys_tok[lower:upper]
        values_cur = values_tok[lower:upper]
        queries_blk = queries[lower:upper]
        normed_state = low(root_mean(state_now, norm_gains[2]))
        state_proj = jnp.einsum('nd,dhe->nhe', normed_state, state_qkv, precision=HIGHEST)
        squery = both_ways(state_proj[..., :HS])
        state_keys = both_ways(state_proj[..., HS:2 * HS])
        state_values = both_ways(state_proj[..., 2 * HS:])
        if block_idx > 0:
            keys_prev = keys_tok[lower - BLK:lower]
            values_prev = values_tok[lower - BLK:lower]
        else:
            keys_prev = jnp.zeros_like(keys_cur)
            values_prev = jnp.zeros_like(values_cur)
        keys_all = jnp.concatenate([state_keys, keys_prev, keys_cur], axis=0)
        values_all = jnp.concatenate([state_values, values_prev, values_cur], axis=0)
        ids_blk = piece_row[lower:upper]
        same_piece = (ids_blk[:, None] == ids_blk[None, :]) & (ids_blk[:, None] > 0)
        current_ok = causal | same_piece
        prior_ok = jnp.full((BLK, BLK), block_idx > 0)
        allowed = jnp.concatenate([jnp.ones((BLK, NSTATE), jnp.bool_), prior_ok, current_ok], axis=-1)
        logits = low_back(jnp.einsum('ihe,jhe->hij', queries_blk, keys_all, precision=HIGHEST) * scaling + bias_all)
        logits = jnp.where(allowed[None], logits, -1e+30)
        attn_weights = low(jax.nn.softmax(logits, axis=-1))
        mixed_list.append(both_ways(jnp.einsum('hij,jhe->ihe', attn_weights, values_all, precision=HIGHEST)))
        slogits = low_back(jnp.einsum('nhe,jhe->hnj', squery, keys_cur, precision=HIGHEST) * scaling)
        sprobs = low(jax.nn.softmax(slogits, axis=-1))
        smixed = both_ways(jnp.einsum('hnj,jhe->nhe', sprobs, values_cur, precision=HIGHEST))
        update = low_back(jnp.einsum('nhe,hed->nd', smixed, state_out, precision=HIGHEST))
        state_now = decay_rate * state_now + (1.0 - decay_rate) * update
    mixed_all = jnp.concatenate(mixed_list, axis=0)
    branch_a = low_back(jnp.einsum('lhe,hed->ld', mixed_all, tok_out, precision=HIGHEST))
    residual = inputs + branch_a
    normed_m = low(root_mean(residual, norm_gains[1]))
    pre_act = low_back(jnp.dot(normed_m, mlp_in, precision=HIGHEST))
    hidden = low(jax.nn.gelu(pre_act, approximate=False))
    branch_m = low_back(jnp.dot(hidden, mlp_out, precision=HIGHEST))
    return (residual + branch_m, (branch_a, branch_m))

def reference(tokens, piece_ids, tok_qkv, state_qkv, tok_out, state_out, mlp_in, mlp_out, rel_bias, init_state, norm_gains, decay_param, cotangent):
    params = tuple((weight_arg.astype(jnp.float32) for weight_arg in (tok_qkv, state_qkv, tok_out, state_out, mlp_in, mlp_out, rel_bias, init_state, norm_gains, decay_param)))
    inputs = tokens.astype(jnp.float32)

    def forward(inputs, params):

        def per_sequence(seq_args):
            return one_sequence(seq_args[0], seq_args[1], params)
        outputs, extras = lax.map(jax.checkpoint(per_sequence), (inputs, piece_ids))
        return (outputs, extras)
    outputs, backward, extras = jax.vjp(forward, inputs, params, has_aux=True)
    grad_inputs, grad_params = backward(cotangent.astype(jnp.float32))
    rms_out = jnp.stack([jnp.sqrt(jnp.mean(inputs * inputs)), jnp.sqrt(jnp.mean(extras[0] * extras[0])), jnp.sqrt(jnp.mean(extras[1] * extras[1]))])
    return (outputs.astype(jnp.bfloat16), grad_inputs.astype(jnp.bfloat16), grad_params[0], grad_params[1], grad_params[2], grad_params[3], grad_params[4], grad_params[5], grad_params[6], grad_params[7], grad_params[8], grad_params[9], rms_out)
```

```python
import functools

import jax
import jax.numpy as jnp
from jax import lax
from jax.experimental import pallas as pl
from jax.experimental.pallas import tpu as pltpu
from jax.sharding import PartitionSpec as P

HS = 128
BLK = 512
NBUCKET = 32
EDGES = (12, 16, 23, 32, 46, 64, 91)
LOW = jnp.bfloat16
F32 = jnp.float32
SCALE = HS ** (-0.5)
EPS = 1e-06
DIAG = 3 * BLK
VMEM_LIMIT = 60 * 1024 * 1024


def mm(a, b, ca, cb):
    return lax.dot_general(a, b, (((ca,), (cb,)), ((), ())), preferred_element_type=F32)


def whole():
    return pl.BlockSpec(memory_space=pltpu.VMEM)


def scalars():
    return pl.BlockSpec(memory_space=pltpu.SMEM)


def params(grid_rank=0):
    if grid_rank:
        return pltpu.CompilerParams(
            dimension_semantics=("arbitrary",) * grid_rank, vmem_limit_bytes=VMEM_LIMIT
        )
    return pltpu.CompilerParams(vmem_limit_bytes=VMEM_LIMIT)


def cost(flops, nbytes, trans=0):
    return pl.CostEstimate(flops=int(flops), bytes_accessed=int(nbytes), transcendentals=int(trans))


def rms_scale(v):
    return lax.rsqrt(jnp.mean(v * v, axis=-1, keepdims=True) + EPS)


def token_proj_kernel(count, me_ref, gain_ref, w_ref, *refs):
    pieces = refs[:count]
    q_ref, kv_ref, normed_ref = refs[count:]
    heads = w_ref.shape[0]
    rows = pieces[0].shape[0]
    for m in range(count):
        start = pl.multiple_of((me_ref[0] ^ m) * rows, rows)
        v = pieces[m][...].astype(F32)
        normed = (v * rms_scale(v) * gain_ref[...]).astype(LOW)
        normed_ref[pl.ds(start, rows), :] = normed
        for h in range(heads):
            out = mm(normed, w_ref[h], 1, 0).astype(LOW)
            q_ref[pl.ds(start, rows), h * HS : (h + 1) * HS] = out[:, :HS]
            kv_ref[pl.ds(start, rows), h * HS : (h + 1) * HS] = out[:, HS : 2 * HS]
            kv_ref[pl.ds(start, rows), (heads + h) * HS : (heads + h + 1) * HS] = out[:, 2 * HS :]


def token_proj(me, gain, weight, pieces):
    heads, width, _ = weight.shape
    rows = pieces[0].shape[0] * len(pieces)
    return pl.pallas_call(
        functools.partial(token_proj_kernel, len(pieces)),
        out_shape=(
            jax.ShapeDtypeStruct((rows, heads * HS), LOW),
            jax.ShapeDtypeStruct((rows, 2 * heads * HS), LOW),
            jax.ShapeDtypeStruct((rows, width), LOW),
        ),
        in_specs=[scalars(), whole(), whole()] + [whole()] * len(pieces),
        out_specs=(whole(),) * 3,
        compiler_params=params(),
        cost_estimate=cost(2 * rows * width * heads * 384, rows * width * 6),
        name="token_proj",
    )(me, gain, weight, *pieces)


def state_proj_kernel(count, w_ref, *refs):
    pieces = refs[:count]
    out_ref = refs[count]
    rows = pieces[0].shape[0]
    for m in range(count):
        for h in range(w_ref.shape[0]):
            out_ref[m * rows : (m + 1) * rows, h * 384 : (h + 1) * 384] = mm(
                pieces[m][...], w_ref[h], 1, 0
            ).astype(LOW)


def state_proj(weight, pieces):
    heads, width, _ = weight.shape
    rows = pieces[0].shape[0] * len(pieces)
    return pl.pallas_call(
        functools.partial(state_proj_kernel, len(pieces)),
        out_shape=jax.ShapeDtypeStruct((rows, heads * 384), LOW),
        in_specs=[whole()] * (1 + len(pieces)),
        out_specs=whole(),
        compiler_params=params(),
        cost_estimate=cost(2 * rows * width * heads * 384, rows * width * 4),
        name="state_proj",
    )(weight, *pieces)


def proj_back_kernel(first, g_ref, w_ref, out_ref):
    span = w_ref.shape[2] - first
    total = None
    for h in range(w_ref.shape[0]):
        term = mm(g_ref[:, h * span : (h + 1) * span], w_ref[h, :, first:], 1, 1)
        total = term if total is None else total + term
    out_ref[...] = total.astype(LOW)


def proj_back(grads, weight, first):
    heads, width, _ = weight.shape
    rows = grads.shape[0]
    tile = min(256, rows)
    return pl.pallas_call(
        functools.partial(proj_back_kernel, first),
        grid=(rows // tile,),
        out_shape=jax.ShapeDtypeStruct((rows, width), LOW),
        in_specs=[
            pl.BlockSpec((tile, grads.shape[1]), lambda i: (i, 0)),
            pl.BlockSpec(weight.shape, lambda i: (0, 0, 0)),
        ],
        out_specs=pl.BlockSpec((tile, width), lambda i: (i, 0)),
        compiler_params=params(1),
        cost_estimate=cost(2 * rows * width * grads.shape[1], rows * width * 4),
        name="proj_back",
    )(grads, weight)


def column_softmax(scores):
    peak = jnp.max(scores, axis=0, keepdims=True)
    exponent = jnp.exp(scores - peak)
    return exponent * (1.0 / jnp.sum(exponent, axis=0, keepdims=True))


def chain_forward_kernel(count, heads, blocks, start_ref, gain_ref, dec_ref, *refs):
    kv = refs[:count]
    w = refs[count : 2 * count]
    keep_ref, normed_ref, update_ref, last_ref = refs[2 * count :]
    span = heads * HS
    dec = dec_ref[...]
    state = start_ref[...]
    for b in range(blocks):
        lo, hi = b * BLK, (b + 1) * BLK
        keep_ref[b] = state
        normed = (state * rms_scale(state) * gain_ref[...]).astype(LOW)
        normed_ref[b] = normed
        update = None
        for m in range(count):
            q = mm(w[m][:span, :], normed, 1, 1).astype(LOW)
            mixed = []
            for h in range(heads):
                k = kv[m][lo:hi, h * HS : (h + 1) * HS]
                v = kv[m][lo:hi, (heads + h) * HS : (heads + h + 1) * HS]
                weights = column_softmax(mm(k, q[h * HS : (h + 1) * HS], 1, 0) * SCALE)
                mixed.append(mm(v, weights.astype(LOW), 0, 0).astype(LOW))
            mixed = mixed[0] if heads == 1 else jnp.concatenate(mixed, axis=0)
            term = mm(mixed, w[m][span:, :], 0, 0)
            update = term if update is None else update + term
        update_ref[b] = update
        state = dec * state + (1.0 - dec) * update
    last_ref[...] = state


def chain_forward(start, gain, dec, kv, weights, blocks):
    count = len(kv)
    rows, width = start.shape
    heads = kv[0].shape[1] // (2 * HS)
    flops = blocks * (4 * rows * width * count * heads * HS + 4 * rows * BLK * count * heads * HS)
    return pl.pallas_call(
        functools.partial(chain_forward_kernel, count, heads, blocks),
        out_shape=(
            jax.ShapeDtypeStruct((blocks, rows, width), F32),
            jax.ShapeDtypeStruct((blocks, rows, width), LOW),
            jax.ShapeDtypeStruct((blocks, rows, width), F32),
            jax.ShapeDtypeStruct((rows, width), F32),
        ),
        in_specs=[whole()] * (3 + 2 * count),
        out_specs=(whole(),) * 4,
        compiler_params=params(),
        cost_estimate=cost(flops, 8 * 1024 * 1024),
        name="chain_forward",
    )(start, gain, dec, *kv, *weights)


def chain_backward_kernel(
    count, heads, blocks, carry_ref, gain_ref, dec_ref, keep_ref, normed_ref, update_ref, gkv_ref, *refs
):
    kv = refs[:count]
    w = refs[count : 2 * count]
    gup_ref, last_ref, small_ref = refs[2 * count :]
    span = heads * HS
    dec = dec_ref[...]
    gain = gain_ref[...]
    carry = carry_ref[...]
    grad_dec = None
    grad_gain = None
    for b in reversed(range(blocks)):
        lo, hi = b * BLK, (b + 1) * BLK
        state = keep_ref[b]
        term = jnp.sum(carry * (state - update_ref[b]), axis=0, keepdims=True)
        grad_dec = term if grad_dec is None else grad_dec + term
        gup = ((1.0 - dec) * carry).astype(LOW)
        gup_ref[b] = gup
        normed = normed_ref[b]
        grad_normed = gkv_ref[b]
        for m in range(count):
            q = mm(w[m][:span, :], normed, 1, 1).astype(LOW)
            gmix = mm(w[m][span:, :], gup, 1, 1).astype(LOW)
            grad_q = []
            for h in range(heads):
                k = kv[m][lo:hi, h * HS : (h + 1) * HS]
                v = kv[m][lo:hi, (heads + h) * HS : (heads + h + 1) * HS]
                weights = column_softmax(mm(k, q[h * HS : (h + 1) * HS], 1, 0) * SCALE)
                grad_w = mm(v, gmix[h * HS : (h + 1) * HS], 1, 0)
                inner = jnp.sum(grad_w * weights, axis=0, keepdims=True)
                grad_s = (weights * (grad_w - inner)).astype(LOW)
                grad_q.append((mm(k, grad_s, 0, 0) * SCALE).astype(LOW))
            grad_q = grad_q[0] if heads == 1 else jnp.concatenate(grad_q, axis=0)
            grad_normed = grad_normed + mm(grad_q, w[m][:span, :], 0, 0)
        r = rms_scale(state)
        unit = state * r
        scaled = grad_normed * gain
        term = jnp.sum(grad_normed * unit, axis=0, keepdims=True)
        grad_gain = term if grad_gain is None else grad_gain + term
        carry = dec * carry + r * (
            scaled - unit * jnp.mean(scaled * unit, axis=-1, keepdims=True)
        )
    last_ref[...] = carry
    small_ref[0:1, :] = grad_gain
    small_ref[1:2, :] = grad_dec


def chain_backward(carry, gain, dec, keep, normed, update, gkv, kv, weights):
    count = len(kv)
    blocks, rows, width = keep.shape
    heads = kv[0].shape[1] // (2 * HS)
    flops = blocks * (6 * rows * width * count * heads * HS + 6 * rows * BLK * count * heads * HS)
    return pl.pallas_call(
        functools.partial(chain_backward_kernel, count, heads, blocks),
        out_shape=(
            jax.ShapeDtypeStruct((blocks, rows, width), LOW),
            jax.ShapeDtypeStruct((rows, width), F32),
            jax.ShapeDtypeStruct((2, width), F32),
        ),
        in_specs=[whole()] * (7 + 2 * count),
        out_specs=(whole(),) * 3,
        compiler_params=params(),
        cost_estimate=cost(flops, 10 * 1024 * 1024),
        name="chain_backward",
    )(carry, gain, dec, keep, normed, update, gkv, *kv, *weights)


def bucket_tile():
    lane = lax.broadcasted_iota(jnp.int32, (8, DIAG), 1)
    row = lax.broadcasted_iota(jnp.int32, (8, DIAG), 0)
    diff = lane - row
    diff = jnp.where(diff < 0, diff + DIAG, diff)
    offset = jnp.where(diff < BLK, diff, diff - DIAG) + BLK
    distance = jnp.abs(offset)
    far = jnp.full((8, DIAG), 8, jnp.int32)
    for edge in EDGES:
        far = far + (distance >= edge).astype(jnp.int32)
    near = jnp.where(distance < 8, distance, far)
    return jnp.where(offset >= 0, near, near + NBUCKET // 2)


def fill_bias(table_ref, h, bias_ref):
    bucket = bucket_tile()
    base = jnp.zeros((8, DIAG), F32)
    for k in range(NBUCKET):
        base = jnp.where(bucket == k, table_ref[h, k], base)

    def body(g, carry):
        rolled = pltpu.roll(base, 8 * g, 1)
        bias_ref[pl.ds(pl.multiple_of(8 * g, 8), 8), :] = rolled[:, :BLK]
        return carry

    lax.fori_loop(0, 2 * BLK // 8, body, 0, unroll=4)


def collapse_bias(grad_ref, out_ref):
    def body(g, acc):
        tile = grad_ref[pl.ds(pl.multiple_of(8 * g, 8), 8), :]
        wide = jnp.concatenate([tile, jnp.zeros((8, DIAG - BLK), F32)], axis=1)
        return acc + pltpu.roll(wide, lax.rem(DIAG - 8 * g, DIAG), 1)

    acc = lax.fori_loop(0, 2 * BLK // 8, body, jnp.zeros((8, DIAG), F32), unroll=4)
    bucket = bucket_tile()
    lane = lax.broadcasted_iota(jnp.int32, (8, HS), 1)
    out = jnp.zeros((8, HS), F32)
    for k in range(NBUCKET):
        out = jnp.where(lane == k, jnp.sum(jnp.where(bucket == k, acc, 0.0)), out)
    out_ref[...] = out


def current_mask(ids_col_ref, ids_row_ref):
    key = lax.broadcasted_iota(jnp.int32, (BLK, BLK), 0)
    query = lax.broadcasted_iota(jnp.int32, (BLK, BLK), 1)
    ids_row = ids_row_ref[...]
    return (key <= query) | ((ids_col_ref[...] == ids_row) & (ids_row > 0))


def attend_kernel(
    run_ref, table_ref, q_ref, kc_ref, vc_ref, kp_ref, vp_ref, ko_ref, vo_ref, ks_ref, vs_ref,
    row_ref, col_ref, out_ref, lse_ref, bias_ref, score_ref,
):
    h = pl.program_id(0)
    b = pl.program_id(1)

    @pl.when(b == 0)
    def _():
        fill_bias(table_ref, h, bias_ref)

    q = q_ref[...]
    first = b == 0
    keys = (
        ks_ref[...].reshape(BLK, HS),
        jnp.where(first, ko_ref[...], kp_ref[...]),
        kc_ref[...],
    )
    values = (
        vs_ref[...].reshape(BLK, HS),
        jnp.where(first, vo_ref[...], vp_ref[...]),
        vc_ref[...],
    )
    prior_ok = (run_ref[0] > 0) | (b > 0)
    score = mm(keys[0], q, 1, 1) * SCALE
    score_ref[0] = score
    peak = jnp.max(score, axis=0, keepdims=True)
    score = mm(keys[1], q, 1, 1) * SCALE + bias_ref[:BLK]
    score = jnp.where(prior_ok, score, -1e30)
    score_ref[1] = score
    peak = jnp.maximum(peak, jnp.max(score, axis=0, keepdims=True))
    score = mm(keys[2], q, 1, 1) * SCALE + bias_ref[BLK:]
    score = jnp.where(current_mask(col_ref, row_ref), score, -1e30)
    score_ref[2] = score
    peak = jnp.maximum(peak, jnp.max(score, axis=0, keepdims=True))
    total = jnp.zeros((1, BLK), F32)
    for c in range(3):
        exponent = jnp.exp(score_ref[c] - peak)
        score_ref[c] = exponent
        total = total + jnp.sum(exponent, axis=0, keepdims=True)
    inverse = 1.0 / total
    mixed = jnp.zeros((HS, BLK), F32)
    for c in range(3):
        mixed = mixed + mm(values[c], (score_ref[c] * inverse).astype(LOW), 0, 0)
    out_ref[...] = mixed.T.astype(LOW)
    lse_ref[...] = peak + jnp.log(total)


def attend_specs(heads, pieces, part, blocks):
    def at(col):
        return pl.BlockSpec((BLK, HS), lambda h, b: (b, col(h)))

    def before(col):
        return pl.BlockSpec((BLK, HS), lambda h, b: (jnp.maximum(b - 1, 0), col(h)))

    def outer(col):
        return pl.BlockSpec((BLK, HS), lambda h, b: (0, col(h)))

    def state(col):
        return pl.BlockSpec((pieces, None, part, HS), lambda h, b: (0, b, 0, col(h)))

    key, value = (lambda h: h), (lambda h: heads + h)
    return [
        scalars(),
        scalars(),
        at(key),
        at(key),
        at(value),
        before(key),
        before(value),
        outer(key),
        outer(value),
        state(lambda h: 3 * h + 1),
        state(lambda h: 3 * h + 2),
        pl.BlockSpec((None, 1, BLK), lambda h, b: (b, 0, 0)),
        pl.BlockSpec((None, BLK, 1), lambda h, b: (b, 0, 0)),
    ]


def attend(run, table, q, kv, outer, sproj, ids_row, ids_col):
    rows = q.shape[0]
    heads = q.shape[1] // HS
    pieces, blocks, part, _ = sproj.shape
    return pl.pallas_call(
        attend_kernel,
        grid=(heads, blocks),
        out_shape=(
            jax.ShapeDtypeStruct((rows, heads * HS), LOW),
            jax.ShapeDtypeStruct((heads, blocks, 1, BLK), F32),
        ),
        in_specs=attend_specs(heads, pieces, part, blocks),
        out_specs=(
            pl.BlockSpec((BLK, HS), lambda h, b: (b, h)),
            pl.BlockSpec((None, None, 1, BLK), lambda h, b: (h, b, 0, 0)),
        ),
        scratch_shapes=[pltpu.VMEM((2 * BLK, BLK), F32), pltpu.VMEM((3, BLK, BLK), F32)],
        compiler_params=params(2),
        cost_estimate=cost(
            heads * blocks * 12 * BLK * BLK * HS, 6 * 1024 * 1024, heads * blocks * 3 * BLK * BLK
        ),
        name="attend",
    )(run, table, q, kv, kv, kv, kv, outer, outer, sproj, sproj, ids_row, ids_col)


def attend_back_kernel(
    run_ref, table_ref, q_ref, kc_ref, vc_ref, kp_ref, vp_ref, ko_ref, vo_ref, ks_ref, vs_ref,
    row_ref, col_ref, gmix_ref, lse_ref,
    gq_ref, gkc_ref, gvc_ref, gkp_ref, gvp_ref, gs_ref, gtab_ref,
    bias_ref, gbias_ref, prob_ref, gprob_ref,
):
    h = pl.program_id(0)
    b = pl.program_id(1)

    @pl.when(b == 0)
    def _():
        fill_bias(table_ref, h, bias_ref)
        gbias_ref[...] = jnp.zeros_like(gbias_ref)

    q = q_ref[...]
    gmix = gmix_ref[...]
    lse = lse_ref[...]
    first = b == 0
    keys = (
        ks_ref[...].reshape(BLK, HS),
        jnp.where(first, ko_ref[...], kp_ref[...]),
        kc_ref[...],
    )
    values = (
        vs_ref[...].reshape(BLK, HS),
        jnp.where(first, vo_ref[...], vp_ref[...]),
        vc_ref[...],
    )
    prior_ok = (run_ref[0] > 0) | (b > 0)
    inner = jnp.zeros((1, BLK), F32)
    grad_values = []
    for c in range(3):
        score = mm(keys[c], q, 1, 1) * SCALE
        if c == 1:
            score = jnp.where(prior_ok, score + bias_ref[:BLK], -1e30)
        if c == 2:
            score = jnp.where(current_mask(col_ref, row_ref), score + bias_ref[BLK:], -1e30)
        prob = jnp.exp(score - lse)
        prob_ref[c] = prob
        grad_values.append(mm(prob.astype(LOW), gmix, 1, 0))
        grad_prob = mm(values[c], gmix, 1, 1)
        gprob_ref[c] = grad_prob
        inner = inner + jnp.sum(prob * grad_prob, axis=0, keepdims=True)
    grad_q = jnp.zeros((HS, BLK), F32)
    grad_keys = []
    for c in range(3):
        grad_score = (prob_ref[c] * (gprob_ref[c] - inner)).astype(LOW)
        if c > 0:
            gbias_ref[(c - 1) * BLK : c * BLK, :] += grad_score.astype(F32)
        grad_keys.append(mm(grad_score, q, 1, 0) * SCALE)
        grad_q = grad_q + mm(keys[c], grad_score, 0, 0)
    gq_ref[...] = (grad_q * SCALE).T.astype(LOW)
    part = gs_ref.shape[0], gs_ref.shape[1], HS
    gs_ref[:, :, :HS] = grad_keys[0].astype(LOW).reshape(part)
    gs_ref[:, :, HS:] = grad_values[0].astype(LOW).reshape(part)
    gkp_ref[...] = grad_keys[1]
    gvp_ref[...] = grad_values[1]
    gkc_ref[...] = grad_keys[2]
    gvc_ref[...] = grad_values[2]

    @pl.when(b == pl.num_programs(1) - 1)
    def _():
        collapse_bias(gbias_ref, gtab_ref)


def attend_back(run, table, q, kv, outer, sproj, ids_row, ids_col, gmix, lse):
    rows = q.shape[0]
    heads = q.shape[1] // HS
    pieces, blocks, part, _ = sproj.shape

    def at():
        return pl.BlockSpec((BLK, HS), lambda h, b: (b, h))

    side = jax.ShapeDtypeStruct((rows, heads * HS), F32)
    return pl.pallas_call(
        attend_back_kernel,
        grid=(heads, blocks),
        out_shape=(
            jax.ShapeDtypeStruct((rows, heads * HS), LOW),
            side,
            side,
            side,
            side,
            jax.ShapeDtypeStruct((pieces, blocks, part, heads * 2 * HS), LOW),
            jax.ShapeDtypeStruct((heads, 8, HS), F32),
        ),
        in_specs=attend_specs(heads, pieces, part, blocks)
        + [at(), pl.BlockSpec((None, None, 1, BLK), lambda h, b: (h, b, 0, 0))],
        out_specs=(
            at(),
            at(),
            at(),
            at(),
            at(),
            pl.BlockSpec((pieces, None, part, 2 * HS), lambda h, b: (0, b, 0, h)),
            pl.BlockSpec((None, 8, HS), lambda h, b: (h, 0, 0)),
        ),
        scratch_shapes=[
            pltpu.VMEM((2 * BLK, BLK), F32),
            pltpu.VMEM((2 * BLK, BLK), F32),
            pltpu.VMEM((3, BLK, BLK), F32),
            pltpu.VMEM((3, BLK, BLK), F32),
        ],
        compiler_params=params(2),
        cost_estimate=cost(
            heads * blocks * 30 * BLK * BLK * HS, 10 * 1024 * 1024, heads * blocks * 3 * BLK * BLK
        ),
        name="attend_back",
    )(run, table, q, kv, kv, kv, kv, outer, outer, sproj, sproj, ids_row, ids_col, gmix, lse)


def state_back_kernel(
    sq_ref, k_ref, v_ref, gmix_ref, gs_ref, gq_ref, gkc_ref, gvc_ref, gkn_ref, gvn_ref, gko_ref, gvo_ref,
    tok_ref, sproj_ref, smix_ref,
):
    b = pl.program_id(1)
    last = b == pl.num_programs(1) - 1
    pieces, part = gs_ref.shape[0], gs_ref.shape[1]
    sq = sq_ref[...].reshape(BLK, HS)
    gmix = gmix_ref[...].reshape(BLK, HS)
    k, v = k_ref[...], v_ref[...]
    weights = column_softmax(mm(k, sq, 1, 1) * SCALE)
    low = weights.astype(LOW)
    grad_w = mm(v, gmix, 1, 1)
    inner = jnp.sum(grad_w * weights, axis=0, keepdims=True)
    grad_s = (weights * (grad_w - inner)).astype(LOW)
    grad_k = mm(grad_s, sq, 1, 0) * SCALE
    grad_v = mm(low, gmix, 1, 0)
    grad_q = mm(k, grad_s, 0, 0) * SCALE
    smix = mm(v, low, 0, 0)
    later_k = jnp.where(last, gko_ref[...].astype(F32), gkn_ref[...])
    later_v = jnp.where(last, gvo_ref[...].astype(F32), gvn_ref[...])
    tok_ref[:, :HS] = gq_ref[...]
    tok_ref[:, HS : 2 * HS] = (gkc_ref[...] + grad_k + later_k).astype(LOW)
    tok_ref[:, 2 * HS :] = (gvc_ref[...] + grad_v + later_v).astype(LOW)
    sproj_ref[:, :, :HS] = grad_q.T.astype(LOW).reshape(pieces, part, HS)
    sproj_ref[:, :, HS:] = gs_ref[...]
    smix_ref[...] = smix.T.astype(LOW).reshape(pieces, part, HS)


def state_back(sproj, kv, gmix, gs, gq, gkc, gvc, gkp, gvp, outer):
    rows = gq.shape[0]
    heads = gq.shape[1] // HS
    pieces, blocks, part, _ = sproj.shape

    def at(col=lambda h: h):
        return pl.BlockSpec((BLK, HS), lambda h, b: (b, col(h)))

    def after():
        return pl.BlockSpec((BLK, HS), lambda h, b: (jnp.minimum(b + 1, blocks - 1), h))

    def state(width, col):
        return pl.BlockSpec((pieces, None, part, width), lambda h, b: (0, b, 0, col(h)))

    return pl.pallas_call(
        state_back_kernel,
        grid=(heads, blocks),
        out_shape=(
            jax.ShapeDtypeStruct((heads, rows, 384), LOW),
            jax.ShapeDtypeStruct((heads, pieces, blocks, part, 384), LOW),
            jax.ShapeDtypeStruct((pieces, blocks, part, heads * HS), LOW),
        ),
        in_specs=[
            state(HS, lambda h: 3 * h),
            at(),
            at(lambda h: heads + h),
            state(HS, lambda h: h),
            state(2 * HS, lambda h: h),
            at(),
            at(),
            at(),
            after(),
            after(),
            pl.BlockSpec((BLK, HS), lambda h, b: (0, h)),
            pl.BlockSpec((BLK, HS), lambda h, b: (0, heads + h)),
        ],
        out_specs=(
            pl.BlockSpec((None, BLK, 384), lambda h, b: (h, b, 0)),
            pl.BlockSpec((None, pieces, None, part, 384), lambda h, b: (h, 0, b, 0, 0)),
            state(HS, lambda h: h),
        ),
        compiler_params=params(2),
        cost_estimate=cost(heads * blocks * 14 * BLK * BLK * HS, 8 * 1024 * 1024),
        name="state_back",
    )(sproj, kv, kv, gmix, gs, gq, gkc, gvc, gkp, gvp, outer, outer)


def head_back_kernel(g_ref, w_ref, out_ref):
    total = None
    for h in range(w_ref.shape[0]):
        term = mm(g_ref[h], w_ref[h], 1, 1)
        total = term if total is None else total + term
    out_ref[...] = total.astype(LOW)


def head_back(grads, weight):
    heads, width, span = weight.shape
    rows = grads.shape[1]
    tile = 256
    return pl.pallas_call(
        head_back_kernel,
        grid=(rows // tile,),
        out_shape=jax.ShapeDtypeStruct((rows, width), LOW),
        in_specs=[
            pl.BlockSpec((heads, tile, span), lambda i: (0, i, 0)),
            pl.BlockSpec(weight.shape, lambda i: (0, 0, 0)),
        ],
        out_specs=pl.BlockSpec((tile, width), lambda i: (i, 0)),
        compiler_params=params(1),
        cost_estimate=cost(2 * rows * width * heads * span, rows * width * 4),
        name="head_back",
    )(grads, weight)


def passed_along(array, axis, by):
    size = lax.axis_size(axis)
    pairs = [(i, i + by) for i in range(size) if 0 <= i + by < size]
    return lax.ppermute(array, axis, pairs)


def swap(array, axis, bits):
    return lax.ppermute(array, axis, [(i, i ^ bits) for i in range(lax.axis_size(axis))])


def gather_rel(array):
    size = lax.axis_size("tensor")
    pieces = []
    for m in range(0, size, 2):
        piece = array if m == 0 else swap(array, "tensor", m)
        pieces += [piece, swap(piece, "tensor", 1)]
    return pieces


def reduce_rel(array):
    size = lax.axis_size("tensor")
    pairs = array.reshape((size // 2, 2) + array.shape[1:])
    got = swap(pairs[:, 1], "tensor", 1)
    sums = pairs[:, 0].astype(F32) + got.astype(F32)
    total = sums[0]
    for j in range(1, size // 2):
        total = total + swap(sums[j].astype(LOW), "tensor", 2 * j).astype(F32)
    return total


def exchange_rel(parts):
    return [part if m == 0 else swap(part, "tensor", m) for m, part in enumerate(parts)]


def cut(array, me):
    size = lax.axis_size("tensor")
    rows = array.shape[0] // size
    return [lax.dynamic_slice_in_dim(array, (me ^ m) * rows, rows, 0) for m in range(size)]


def place(pieces, me):
    rows = pieces[0].shape[0]
    out = jnp.zeros((rows * len(pieces),) + pieces[0].shape[1:], pieces[0].dtype)
    for m, piece in enumerate(pieces):
        out = lax.dynamic_update_slice_in_dim(out, piece, (me ^ m) * rows, 0)
    return out


def sum_all(array):
    for axis in ("tensor", "context", "shard"):
        bits = 1
        while bits < lax.axis_size(axis):
            array = array + swap(array, axis, bits)
            bits *= 2
    return array


def rms_back(v, gain, grad):
    r = rms_scale(v)
    unit = v * r
    scaled = grad * gain
    grad_v = r * (scaled - unit * jnp.mean(scaled * unit, axis=-1, keepdims=True))
    return grad_v, jnp.sum(grad * unit, axis=0)


def gelu_exact(features):
    return jax.nn.gelu(features, approximate=False)


def dot(a, b, ca, cb):
    return lax.dot_general(a, b, (((ca,), (cb,)), ((), ())), preferred_element_type=F32)


def shards(
    tokens,
    piece_ids,
    tok_qkv,
    state_qkv,
    tok_out,
    state_out,
    mlp_in,
    mlp_out,
    rel_bias,
    init_state,
    norm_gains,
    decay_param,
    cotangent,
):
    size = lax.axis_size("tensor")
    shard_count = lax.axis_size("shard")
    me = lax.axis_index("tensor")
    shard_pos = lax.axis_index("shard")
    run_pos = lax.axis_index("context")
    run_count = lax.axis_size("context")
    me_arr = me.astype(jnp.int32)[None]
    run_arr = run_pos.astype(jnp.int32)[None]
    own = tokens[0]
    own_rows, width = own.shape
    rows = own_rows * size
    blocks = rows // BLK
    heads = tok_qkv.shape[1]
    part = init_state.shape[0]
    span = heads * HS

    cols = norm_gains.shape[1]
    bias_rows = rel_bias.shape[0]
    small = jnp.concatenate(
        [norm_gains.reshape(-1), decay_param.reshape(-1), rel_bias.reshape(-1)]
    )
    small = lax.all_gather(small, ("shard", "tensor"), axis=0, tiled=False).astype(F32)
    vectors = (
        small[:, : 4 * cols].reshape(-1, 4, cols).transpose(1, 0, 2).reshape(4, width)
    )
    gains = vectors[:3]
    decay = jax.nn.sigmoid(vectors[3:4])
    tables = small[:, 4 * cols :].reshape(shard_count, size, bias_rows, heads)
    table = lax.dynamic_index_in_dim(tables, me, 1, keepdims=False).reshape(NBUCKET, heads).T

    w_tok = lax.all_gather(tok_qkv.transpose(1, 0, 2), "shard", axis=1, tiled=True)
    w_state = lax.all_gather(state_qkv.transpose(1, 0, 2), "shard", axis=1, tiled=True)
    outs = jnp.concatenate(
        [tok_out.reshape(span, -1), state_out.reshape(span, -1), init_state], axis=0
    )
    outs = lax.all_gather(outs, "shard", axis=1, tiled=True)
    w_tout, w_sout, start = outs[:span], outs[span : 2 * span], outs[2 * span :].astype(F32)
    w_in = lax.all_gather(mlp_in, "shard", axis=0, tiled=True)
    w_out = lax.all_gather(mlp_out, "shard", axis=1, tiled=True)

    token_pieces = gather_rel(own)
    q, kv, normed_a = token_proj(me_arr, gains[0:1], w_tok, token_pieces)
    chain_q = w_state[:, :, :HS].transpose(0, 2, 1).reshape(span, width)
    chain_w = gather_rel(jnp.concatenate([chain_q, w_sout], axis=0))
    kv_pieces = gather_rel(kv)
    outer = passed_along(kv[rows - BLK :], "context", 1)
    full_tout = jnp.concatenate(gather_rel(w_tout), axis=0)

    incoming = start
    for round_index in range(run_count):
        current = jnp.where(run_pos == 0, start, incoming)
        keep, normed_s, update, last = chain_forward(
            current, gains[2:3], decay, kv_pieces, chain_w, blocks
        )
        if round_index + 1 < run_count:
            incoming = passed_along(last.astype(LOW), "context", 1).astype(F32)
    state_pieces = gather_rel(normed_s.reshape(blocks * part, width))
    sproj = state_proj(w_state, state_pieces).reshape(size, blocks, part, heads * 384)

    ids_row = piece_ids.reshape(blocks, 1, BLK)
    ids_col = piece_ids.reshape(blocks, BLK, 1)
    mixed, lse = attend(run_arr, table, q, kv, outer, sproj, ids_row, ids_col)
    mixed_parts = cut(mixed, me)
    mixed_rel = jnp.concatenate(mixed_parts, axis=0)
    mixed_rows = jnp.concatenate(exchange_rel(mixed_parts), axis=1)
    branch_a = dot(mixed_rows, full_tout, 1, 0)
    inputs = own.astype(F32)
    residual = inputs + branch_a
    normed_m = (residual * rms_scale(residual) * gains[1]).astype(LOW)

    mlp_rows = jnp.concatenate(gather_rel(normed_m), axis=0)
    grad_rows = jnp.concatenate(gather_rel(cotangent[0]), axis=0)
    pre = dot(mlp_rows, w_in, 1, 0)
    hidden = gelu_exact(pre).astype(LOW)
    branch_m = reduce_rel(dot(hidden, w_out, 1, 0).astype(LOW).reshape(size, own_rows, width))
    output = residual + branch_m
    grad_hidden = dot(grad_rows, w_out, 1, 1)
    grad_pre = jax.vjp(gelu_exact, pre)[1](grad_hidden)[0].astype(LOW)
    grad_normed_m = reduce_rel(dot(grad_pre, w_in, 1, 1).astype(LOW).reshape(size, own_rows, width))
    grad_w_out = dot(hidden, grad_rows, 0, 0)
    grad_w_in = dot(mlp_rows, grad_pre, 0, 0)
    grad_res_n, grad_gain_m = rms_back(residual, gains[1], grad_normed_m)
    grad_res = cotangent[0].astype(F32) + grad_res_n

    grad_branch = grad_res.astype(LOW)
    grad_branch_rel = jnp.concatenate(gather_rel(grad_branch), axis=0)
    grad_w_tout = dot(mixed_rel, grad_branch_rel, 0, 0)
    gmix_rows = dot(grad_branch, full_tout, 1, 1).astype(LOW)
    gmix = place(
        exchange_rel([gmix_rows[:, m * span : (m + 1) * span] for m in range(size)]), me
    )
    gq, gkc, gvc, gkp, gvp, gs, gtab = attend_back(
        run_arr, table, q, kv, outer, sproj, ids_row, ids_col, gmix, lse
    )
    outer_back = passed_along(
        jnp.concatenate([gkp[:BLK], gvp[:BLK]], axis=1).astype(LOW), "context", -1
    )

    grad_state_kv = reduce_rel(
        proj_back(gs.reshape(-1, heads * 2 * HS), w_state, HS).reshape(
            size, blocks * part, width
        )
    ).reshape(blocks, part, width)
    incoming = jnp.zeros_like(start)
    for round_index in range(run_count):
        carry = jnp.where(run_pos == run_count - 1, 0.0, incoming)
        gup, first_grad, chain_small = chain_backward(
            carry, gains[2:3], decay, keep, normed_s, update, grad_state_kv, kv_pieces, chain_w
        )
        if round_index + 1 < run_count:
            incoming = passed_along(first_grad.astype(LOW), "context", -1).astype(F32)
    grad_start = jnp.where(run_pos == 0, first_grad, 0.0).astype(LOW)
    gup_rel = jnp.concatenate(gather_rel(gup.reshape(blocks * part, width)), axis=0)
    gsmix = dot(gup_rel, w_sout, 1, 1).astype(LOW).reshape(size, blocks, part, span)
    gtproj, gsproj, smix = state_back(sproj, kv, gsmix, gs, gq, gkc, gvc, gkp, gvp, outer_back)
    normed_s_rel = jnp.concatenate(state_pieces, axis=0)
    grad_w_state = jnp.einsum(
        "rd,hre->hde", normed_s_rel, gsproj.reshape(heads, -1, 384), preferred_element_type=F32
    )
    grad_w_sout = dot(smix.reshape(-1, span), gup_rel, 0, 0)

    grad_w_tok = jnp.einsum("rd,hre->hde", normed_a, gtproj, preferred_element_type=F32)
    partial = head_back(gtproj, w_tok)
    grad_normed_a = reduce_rel(jnp.stack(cut(partial, me)))
    grad_in_n, grad_gain_a = rms_back(inputs, gains[0], grad_normed_a)
    grad_tokens = (grad_res + grad_in_n).astype(LOW)

    def scatter(array, dim):
        return lax.psum_scatter(array.astype(LOW), "shard", scatter_dimension=dim, tiled=True)

    def both_runs(array):
        return array.astype(F32) + swap(array, "context", 1).astype(F32)

    g_in = both_runs(scatter(grad_w_in, 0))
    g_out = both_runs(scatter(grad_w_out, 1))
    g_state = both_runs(scatter(grad_w_state, 1)).transpose(1, 0, 2)
    g_outs = both_runs(
        scatter(jnp.concatenate([grad_w_tout.astype(LOW), grad_w_sout.astype(LOW), grad_start], 0), 1)
    )
    g_tok = both_runs(scatter(grad_w_tok, 1)).transpose(1, 0, 2)

    squares = jnp.stack(
        [jnp.sum(inputs * inputs), jnp.sum(branch_a * branch_a), jnp.sum(branch_m * branch_m)]
    )
    slot = gtab[:, 0, :NBUCKET].reshape(-1)
    slots = lax.dynamic_update_slice_in_dim(
        jnp.zeros((size * slot.size,), F32), slot, me * slot.size, 0
    )
    tail = jnp.concatenate([slots, squares])
    tail = jnp.pad(tail, (0, width - tail.size))
    grad_decay = chain_small[1] * (decay * (1.0 - decay))[0]
    sums = sum_all(
        jnp.stack([grad_gain_a, grad_gain_m, chain_small[0], grad_decay, tail])
    )
    place_at = (shard_pos * size + me) * cols
    mine = lax.dynamic_slice_in_dim(sums[:4], place_at, cols, 1)
    table_sum = lax.dynamic_slice_in_dim(sums[4], me * slot.size, slot.size, 0)
    table_sum = table_sum.reshape(heads, NBUCKET).T
    g_table = lax.dynamic_slice_in_dim(table_sum, shard_pos * bias_rows, bias_rows, 0)
    entries = inputs.size * shard_count * run_count * size
    first = size * slot.size
    rms_out = jnp.sqrt(sums[4, first : first + 3] / entries)

    return (
        output.astype(LOW)[None],
        grad_tokens[None],
        g_tok,
        g_state,
        g_outs[:span].reshape(heads, HS, -1),
        g_outs[span : 2 * span].reshape(heads, HS, -1),
        g_in,
        g_out,
        g_table,
        g_outs[2 * span :],
        mine[:3],
        mine[3],
        rms_out,
    )


def solution(mesh):
    return jax.shard_map(
        shards,
        mesh=mesh,
        in_specs=(
            P("shard", ("context", "tensor"), None),
            P("shard", "context"),
            P("shard", "tensor", None),
            P("shard", "tensor", None),
            P("tensor", None, "shard"),
            P("tensor", None, "shard"),
            P("shard", "tensor"),
            P("tensor", "shard"),
            P("shard", "tensor"),
            P("tensor", "shard"),
            P(None, ("shard", "tensor")),
            P(("shard", "tensor")),
            P("shard", ("context", "tensor"), None),
        ),
        out_specs=(
            P("shard", ("context", "tensor"), None),
            P("shard", ("context", "tensor"), None),
            P("shard", "tensor", None),
            P("shard", "tensor", None),
            P("tensor", None, "shard"),
            P("tensor", None, "shard"),
            P("shard", "tensor"),
            P("tensor", "shard"),
            P("shard", "tensor"),
            P("tensor", "shard"),
            P(None, ("shard", "tensor")),
            P(("shard", "tensor")),
            P(),
        ),
        check_vma=False,
    )
```

```python
import functools

import jax
import jax.numpy as jnp
from jax import lax
from jax.experimental import pallas as pl
from jax.experimental.pallas import tpu as pltpu
from jax.sharding import PartitionSpec as P

HS = 128
BLK = 512
NBUCKET = 32
EDGES = (12, 16, 23, 32, 46, 64, 91)
LOW = jnp.bfloat16
F32 = jnp.float32
SCALE = HS ** (-0.5)
EPS = 1e-06
DIAG = 3 * BLK
SMALL = 16
PACE = 0.5


def mm(a, b, ca, cb):
    return lax.dot_general(a, b, (((ca,), (cb,)), ((), ())), preferred_element_type=F32)


def whole():
    return pl.BlockSpec(memory_space=pltpu.VMEM)


def scalars():
    return pl.BlockSpec(memory_space=pltpu.SMEM)


def params(grid_rank=0, mib=40):
    limit = mib * 1024 * 1024
    if grid_rank:
        return pltpu.CompilerParams(
            dimension_semantics=("arbitrary",) * grid_rank, vmem_limit_bytes=limit
        )
    return pltpu.CompilerParams(vmem_limit_bytes=limit)


def lasts(microseconds):
    return pl.CostEstimate(
        flops=int(microseconds * PACE * 1.1e9), bytes_accessed=int(microseconds * PACE * 3e6), transcendentals=0
    )


def rms_scale(v):
    return lax.rsqrt(jnp.mean(v * v, axis=-1, keepdims=True) + EPS)


def assemble_kernel(count, pos_ref, *refs):
    pieces, other_ref, outs = refs[:count], refs[count], refs[count + 1 :]
    part = pieces[0].shape[0]
    for s in range(count):
        base = (pos_ref[0] ^ s) * (2 * part)
        mine = pl.multiple_of(base + pos_ref[1] * part, part)
        theirs = pl.multiple_of(base + (1 - pos_ref[1]) * part, part)
        first = 0
        for out_ref in outs:
            last = first + out_ref.shape[1]
            out_ref[pl.ds(mine, part), :] = pieces[s][:, first:last]
            out_ref[pl.ds(theirs, part), :] = other_ref[s, :, first:last]
            first = last


def assemble(pos, pieces, other, widths):
    part, cols = pieces[0].shape
    rows = 2 * part * len(pieces)
    return pl.pallas_call(
        functools.partial(assemble_kernel, len(pieces)),
        out_shape=tuple(jax.ShapeDtypeStruct((rows, w), LOW) for w in widths),
        in_specs=[scalars()] + [whole()] * (len(pieces) + 1),
        out_specs=(whole(),) * len(widths),
        compiler_params=params(mib=16),
        cost_estimate=lasts(1.5),
        name="assemble",
    )(pos, *pieces, other)


def weight_grad_kernel(counts, *refs):
    out_ref = refs[-1]
    at = 0
    first = 0
    for count in counts:
        right = refs[at + count]
        total = None
        row = 0
        for left in refs[at : at + count]:
            term = mm(left[...], right[row : row + left.shape[0], :], 0, 0)
            row += left.shape[0]
            total = term if total is None else total + term
        out_ref[:, first : first + right.shape[1]] = total.astype(LOW)
        first += right.shape[1]
        at += count + 1


def weight_grad(pairs):
    width = pairs[0][0][0].shape[1]
    tile = 256
    specs, args, flops = [], [], 0
    for lefts, right in pairs:
        specs += [pl.BlockSpec((left.shape[0], tile), lambda i: (0, i)) for left in lefts]
        specs.append(pl.BlockSpec(right.shape, lambda i: (0, 0)))
        args += list(lefts) + [right]
        flops += 2 * right.size * width
    cols = sum(right.shape[1] for _, right in pairs)
    return pl.pallas_call(
        functools.partial(weight_grad_kernel, [len(lefts) for lefts, _ in pairs]),
        grid=(width // tile,),
        out_shape=jax.ShapeDtypeStruct((width, cols), LOW),
        in_specs=specs,
        out_specs=pl.BlockSpec((tile, cols), lambda i: (i, 0)),
        compiler_params=params(1, 32),
        cost_estimate=lasts(6),
        name="weight_grad",
    )(*args)


def token_proj_kernel(count, shards, blocks, me_ref, pos_ref, *refs):
    pieces, parts = refs[:count], refs[count : count + shards]
    q_ref, normed_ref, vec_ref, wq_ref, wkv_ref, scratch, *kv_refs, w_ref = refs[count + shards :]
    heads = w_ref.shape[1] // 384
    span = heads * HS
    rows = pieces[0].shape[0] - SMALL
    for s in range(shards):
        part = parts[s].shape[0]
        at = pl.ds(pl.multiple_of((pos_ref[0] ^ s) * part, part), part)
        w_ref[at, :] = parts[s][...]
    vectors = pieces[0][rows:, :].astype(F32)
    for m in range(1, count):
        vectors = vectors + pieces[m][rows:, :].astype(F32)
    vec_ref[...] = vectors
    gain = vectors[0:1]
    for m in range(count):
        start = pl.multiple_of((me_ref[0] ^ m) * rows, rows)
        v = pieces[m][:rows, :].astype(F32)
        normed = (v * rms_scale(v) * gain).astype(LOW)
        normed_ref[pl.ds(start, rows), :] = normed
        for h in range(heads):
            out = mm(normed, w_ref[:, h * 384 : (h + 1) * 384], 1, 0).astype(LOW)
            q_ref[pl.ds(start, rows), h * HS : (h + 1) * HS] = out[:, :HS]
            scratch[pl.ds(start, rows), h * HS : (h + 1) * HS] = out[:, HS : 2 * HS]
            scratch[pl.ds(start, rows), span + h * HS : span + (h + 1) * HS] = out[:, 2 * HS :]
    for b in range(blocks):
        kv_refs[b][...] = scratch[b * BLK : (b + 1) * BLK, :]
    for h in range(heads):
        wq_ref[:, h * HS : (h + 1) * HS] = w_ref[:, h * 384 : h * 384 + HS]
        wkv_ref[:, 2 * h * HS : 2 * (h + 1) * HS] = w_ref[:, h * 384 + HS : (h + 1) * 384]


def token_proj(me, pos, pieces, parts, blocks):
    width = pieces[0].shape[1]
    cols = parts[0].shape[1]
    span = cols // 3
    rows = (pieces[0].shape[0] - SMALL) * len(pieces)
    return pl.pallas_call(
        functools.partial(token_proj_kernel, len(pieces), len(parts), blocks),
        out_shape=(
            jax.ShapeDtypeStruct((rows, span), LOW),
            jax.ShapeDtypeStruct((rows, width), LOW),
            jax.ShapeDtypeStruct((SMALL, width), F32),
            jax.ShapeDtypeStruct((width, span), LOW),
            jax.ShapeDtypeStruct((width, 2 * span), LOW),
            jax.ShapeDtypeStruct((rows, 2 * span), LOW),
        )
        + (jax.ShapeDtypeStruct((BLK, 2 * span), LOW),) * blocks,
        in_specs=[scalars(), scalars()] + [whole()] * (len(pieces) + len(parts)),
        out_specs=(whole(),) * (6 + blocks),
        scratch_shapes=[pltpu.VMEM((width, cols), LOW)],
        compiler_params=params(mib=24),
        cost_estimate=lasts(5),
        name="token_proj",
    )(me, pos, *pieces, *parts)


def proj_kernel(count, weights, *refs):
    pieces, ws, outs = refs[:count], refs[count : count + weights], refs[count + weights :]
    rows = pieces[0].shape[0]
    for m in range(count):
        for w, out in zip(ws, outs, strict=True):
            out[m * rows : (m + 1) * rows, :] = mm(pieces[m][...], w[...], 1, 0).astype(LOW)


def proj(pieces, weights):
    rows, width = pieces[0].shape[0] * len(pieces), pieces[0].shape[1]
    cols = sum(w.shape[1] for w in weights)
    return pl.pallas_call(
        functools.partial(proj_kernel, len(pieces), len(weights)),
        out_shape=tuple(jax.ShapeDtypeStruct((rows, w.shape[1]), LOW) for w in weights),
        in_specs=[whole()] * (len(pieces) + len(weights)),
        out_specs=(whole(),) * len(weights),
        compiler_params=params(mib=24),
        cost_estimate=lasts(3),
        name="proj",
    )(*pieces, *weights)


def back_kernel(count, gained, me_ref, *refs):
    even_ref, odd_ref = refs[2 * count + gained : 2 * count + gained + 2]
    total = None
    for i in range(count):
        term = mm(refs[i][...], refs[count + i][...], 1, 1)
        total = term if total is None else total + term
    if gained:
        sums = jnp.sum(total * refs[2 * count][...].astype(F32), axis=0, keepdims=True)
        first = pl.program_id(0) == 0
        refs[-1][...] = sums + jnp.where(first, 0.0, refs[-1][...])
    total = total.astype(LOW)
    even = lax.rem(pl.program_id(0), 2) == 0

    @pl.when(even)
    def _():
        even_ref[...] = total

    @pl.when(jnp.logical_not(even))
    def _():
        odd_ref[...] = total


def back(me, grads, weights, normed=None):
    rows, width = grads[0].shape[0], weights[0].shape[0]
    size = lax.axis_size("tensor")
    tile = rows // size
    inner = sum(w.shape[1] for w in weights)
    half = jax.ShapeDtypeStruct((size // 2, tile, width), LOW)
    extra = [] if normed is None else [normed]
    grid_spec = pltpu.PrefetchScalarGridSpec(
        num_scalar_prefetch=1,
        grid=(size,),
        in_specs=[pl.BlockSpec((tile, g.shape[1]), lambda i, me_ref: (i ^ me_ref[0], 0)) for g in grads]
        + [pl.BlockSpec(w.shape, lambda i, me_ref: (0, 0)) for w in weights]
        + [pl.BlockSpec((tile, width), lambda i, me_ref: (i ^ me_ref[0], 0)) for _ in extra],
        out_specs=(
            pl.BlockSpec((None, tile, width), lambda i, me_ref: (i // 2, 0, 0)),
            pl.BlockSpec((None, tile, width), lambda i, me_ref: (i // 2, 0, 0)),
        )
        + (pl.BlockSpec((1, width), lambda i, me_ref: (0, 0)),) * len(extra),
    )
    return pl.pallas_call(
        functools.partial(back_kernel, len(grads), len(extra)),
        grid_spec=grid_spec,
        out_shape=(half, half) + (jax.ShapeDtypeStruct((1, width), F32),) * len(extra),
        compiler_params=params(1, 24),
        cost_estimate=lasts(3),
        name="back",
    )(me, *grads, *weights, *extra)


def branch_kernel(count, own_ref, gain_ref, *refs):
    parts, weights = refs[:count], refs[count : 2 * count]
    residual_ref, normed_ref, sums_ref = refs[2 * count :]
    branch = None
    for part, weight in zip(parts, weights, strict=True):
        term = mm(part[...], weight[...], 1, 1)
        branch = term if branch is None else branch + term
    own = own_ref[...].astype(F32)
    residual = own + branch
    residual_ref[...] = residual
    normed_ref[...] = (residual * rms_scale(residual) * gain_ref[...]).astype(LOW)
    sums_ref[0:1, :] = jnp.sum(own * own, axis=0, keepdims=True)
    sums_ref[1:2, :] = jnp.sum(branch * branch, axis=0, keepdims=True)


def branch_out(own, gain, parts, weights):
    rows, width = own.shape
    return pl.pallas_call(
        functools.partial(branch_kernel, len(parts)),
        out_shape=(
            jax.ShapeDtypeStruct((rows, width), F32),
            jax.ShapeDtypeStruct((rows, width), LOW),
            jax.ShapeDtypeStruct((2, width), F32),
        ),
        in_specs=[whole()] * (2 + 2 * len(parts)),
        out_specs=(whole(),) * 3,
        compiler_params=params(mib=12),
        cost_estimate=lasts(3),
        name="branch_out",
    )(own, gain, *parts, *weights)


def branch_back_kernel(count, sums, cot_ref, residual_ref, gain_ref, *refs):
    terms, weights, outs = refs[:sums], refs[sums : sums + count], refs[sums + count :]
    grad_ref, low_ref, gain_sum_ref, parts = outs[0], outs[1], outs[2], outs[3:]
    grad = terms[0][...].astype(F32)
    for term in terms[1:]:
        grad = grad + term[...].astype(F32)
    residual = residual_ref[...]
    r = rms_scale(residual)
    unit = residual * r
    gain_sum_ref[...] = jnp.sum(grad * unit, axis=0, keepdims=True)
    scaled = grad * gain_ref[...]
    grad = cot_ref[...].astype(F32) + r * (
        scaled - unit * jnp.mean(scaled * unit, axis=-1, keepdims=True)
    )
    grad_ref[...] = grad
    low = grad.astype(LOW)
    low_ref[...] = low
    for part, weight in zip(parts, weights, strict=True):
        part[...] = mm(low, weight[...], 1, 0).astype(LOW)


def branch_back(cot, residual, gain, terms, weights):
    rows, width = cot.shape
    span = weights[0].shape[1]
    return pl.pallas_call(
        functools.partial(branch_back_kernel, len(weights), len(terms)),
        out_shape=(
            jax.ShapeDtypeStruct((rows, width), F32),
            jax.ShapeDtypeStruct((rows, width), LOW),
            jax.ShapeDtypeStruct((1, width), F32),
        )
        + (jax.ShapeDtypeStruct((rows, span), LOW),) * len(weights),
        in_specs=[whole()] * (3 + len(terms) + len(weights)),
        out_specs=(whole(),) * (3 + len(weights)),
        compiler_params=params(mib=56),
        cost_estimate=lasts(2.5),
        name="branch_back",
    )(cot, residual, gain, *terms, *weights)


def gelu_parts(pre):
    half = 0.5 * (1.0 + lax.erf(pre * 0.7071067811865476))
    density = jnp.exp(pre * pre * -0.5) * 0.3989422804014327
    return half, density


def feed_kernel(count, w_ref, ghid_ref, *refs):
    pieces = refs[:count]
    hidden_ref, gpre_ref, even_ref, odd_ref = refs[count:]
    rows = pieces[0].shape[0]
    for m in range(count):
        at = slice(m * rows, (m + 1) * rows)
        pre = mm(pieces[m][...], w_ref[...], 1, 0)
        half, density = gelu_parts(pre)
        hidden_ref[at, :] = (pre * half).astype(LOW)
        gpre = ((half + pre * density) * ghid_ref[at, :].astype(F32)).astype(LOW)
        gpre_ref[at, :] = gpre
        (even_ref, odd_ref)[m % 2][m // 2] = mm(gpre, w_ref[...], 1, 1).astype(LOW)


def feed(w_in, ghid, pieces):
    width, units = w_in.shape
    own = pieces[0].shape[0]
    rows = own * len(pieces)
    half = jax.ShapeDtypeStruct((len(pieces) // 2, own, width), LOW)
    return pl.pallas_call(
        functools.partial(feed_kernel, len(pieces)),
        out_shape=(
            jax.ShapeDtypeStruct((rows, units), LOW),
            jax.ShapeDtypeStruct((rows, units), LOW),
            half,
            half,
        ),
        in_specs=[whole()] * (2 + len(pieces)),
        out_specs=(whole(),) * 4,
        compiler_params=params(mib=32),
        cost_estimate=lasts(7),
        name="feed",
    )(w_in, ghid, *pieces)


def column_softmax(scores):
    peak = jnp.max(scores, axis=0, keepdims=True)
    exponent = jnp.exp(scores - peak)
    return exponent * (1.0 / jnp.sum(exponent, axis=0, keepdims=True))


def chain_forward_kernel(count, heads, state_ref, gain_ref, dec_ref, *refs):
    kv = refs[:count]
    w = refs[count : 2 * count]
    normed_ref, update_ref, next_ref = refs[2 * count :]
    span = heads * HS
    dec = dec_ref[...]
    state = state_ref[...]
    normed = (state * rms_scale(state) * gain_ref[...]).astype(LOW)
    normed_ref[...] = normed
    update = None
    for m in range(count):
        q = mm(normed, w[m][:, :span], 1, 0).astype(LOW)
        mixed = []
        for h in range(heads):
            k = kv[m][:, h * HS : (h + 1) * HS]
            v = kv[m][:, (heads + h) * HS : (heads + h + 1) * HS]
            weights = column_softmax(mm(k, q[:, h * HS : (h + 1) * HS], 1, 1) * SCALE)
            mixed.append(mm(v, weights.astype(LOW), 0, 0))
        mixed = mixed[0] if heads == 1 else jnp.concatenate(mixed, axis=0)
        term = mm(mixed.T.astype(LOW), w[m][:, span:], 1, 1)
        update = term if update is None else update + term
    update_ref[...] = update
    next_ref[...] = dec * state + (1.0 - dec) * update


def chain_forward(state, gain, dec, kv, weights):
    count = len(kv)
    rows, width = state.shape
    heads = kv[0].shape[1] // (2 * HS)
    flops = 4 * rows * width * count * heads * HS + 4 * rows * BLK * count * heads * HS
    return pl.pallas_call(
        functools.partial(chain_forward_kernel, count, heads),
        out_shape=(
            jax.ShapeDtypeStruct((rows, width), LOW),
            jax.ShapeDtypeStruct((rows, width), F32),
            jax.ShapeDtypeStruct((rows, width), F32),
        ),
        in_specs=[whole()] * (3 + 2 * count),
        out_specs=(whole(),) * 3,
        compiler_params=params(mib=56),
        cost_estimate=lasts(6.5),
        name="chain_forward",
    )(state, gain, dec, *kv, *weights)


def chain_backward_kernel(
    count, heads, carry_ref, gain_ref, dec_ref, state_ref, normed_ref, update_ref, gkv_ref, *refs
):
    kv = refs[:count]
    w = refs[count : 2 * count]
    next_ref, gup_next_ref, small_ref = refs[2 * count :]
    span = heads * HS
    dec = dec_ref[...]
    gain = gain_ref[...]
    carry = carry_ref[...]
    state = state_ref[...]
    small_ref[1:2, :] = jnp.sum(carry * (state - update_ref[...]), axis=0, keepdims=True)
    gup = ((1.0 - dec) * carry).astype(LOW)
    normed = normed_ref[...]
    grad_normed = gkv_ref[...]
    for m in range(count):
        q = mm(normed, w[m][:, :span], 1, 0).astype(LOW)
        gmix = mm(gup, w[m][:, span:], 1, 0).astype(LOW)
        grad_q = []
        for h in range(heads):
            at = slice(h * HS, (h + 1) * HS)
            k = kv[m][:, at]
            v = kv[m][:, (heads + h) * HS : (heads + h + 1) * HS]
            weights = column_softmax(mm(k, q[:, at], 1, 1) * SCALE)
            grad_w = mm(v, gmix[:, at], 1, 1)
            inner = jnp.sum(grad_w * weights, axis=0, keepdims=True)
            grad_s = (weights * (grad_w - inner)).astype(LOW)
            grad_q.append(mm(k, grad_s, 0, 0) * SCALE)
        grad_q = grad_q[0] if heads == 1 else jnp.concatenate(grad_q, axis=0)
        grad_normed = grad_normed + mm(grad_q.T.astype(LOW), w[m][:, :span], 1, 1)
    r = rms_scale(state)
    unit = state * r
    scaled = grad_normed * gain
    small_ref[0:1, :] = jnp.sum(grad_normed * unit, axis=0, keepdims=True)
    carry = dec * carry + r * (scaled - unit * jnp.mean(scaled * unit, axis=-1, keepdims=True))
    next_ref[...] = carry
    gup_next_ref[...] = ((1.0 - dec) * carry).astype(LOW)


def chain_backward(carry, gain, dec, state, normed, update, gkv, kv, weights):
    count = len(kv)
    rows, width = state.shape
    heads = kv[0].shape[1] // (2 * HS)
    flops = 6 * rows * width * count * heads * HS + 6 * rows * BLK * count * heads * HS
    return pl.pallas_call(
        functools.partial(chain_backward_kernel, count, heads),
        out_shape=(
            jax.ShapeDtypeStruct((rows, width), F32),
            jax.ShapeDtypeStruct((rows, width), LOW),
            jax.ShapeDtypeStruct((2, width), F32),
        ),
        in_specs=[whole()] * (7 + 2 * count),
        out_specs=(whole(),) * 3,
        compiler_params=params(mib=56),
        cost_estimate=lasts(8.3),
        name="chain_backward",
    )(carry, gain, dec, state, normed, update, gkv, *kv, *weights)


def bucket_tile():
    lane = lax.broadcasted_iota(jnp.int32, (8, DIAG), 1)
    row = lax.broadcasted_iota(jnp.int32, (8, DIAG), 0)
    diff = lane - row
    diff = jnp.where(diff < 0, diff + DIAG, diff)
    offset = jnp.where(diff < BLK, diff, diff - DIAG) + BLK
    distance = jnp.abs(offset)
    far = jnp.full((8, DIAG), 8, jnp.int32)
    for edge in EDGES:
        far = far + (distance >= edge).astype(jnp.int32)
    near = jnp.where(distance < 8, distance, far)
    return jnp.where(offset >= 0, near, near + NBUCKET // 2)


def fill_bias(table_ref, h, bias_ref):
    bucket = bucket_tile()
    base = jnp.zeros((8, DIAG), F32)
    for k in range(NBUCKET):
        base = jnp.where(bucket == k, table_ref[h, k], base)
    for r in range(16):
        rolled = pltpu.roll(base, 8 * r, 1) if r else base
        wide = jnp.concatenate([rolled, rolled[:, :BLK]], axis=1)
        for k in range(2 * BLK // 128):
            start = (DIAG - 128 * k) % DIAG
            row = 8 * (16 * k + r)
            bias_ref[row : row + 8, :] = wide[:, start : start + BLK]


def collapse_bias(grad_ref, out_ref):
    total = jnp.zeros((8, DIAG), F32)
    for r in range(16):
        acc = [jnp.zeros((8, 128), F32)] * (DIAG // 128)
        for k in range(2 * BLK // 128):
            row = 8 * (16 * k + r)
            for c in range(BLK // 128):
                at = (c - k) % (DIAG // 128)
                acc[at] = acc[at] + grad_ref[row : row + 8, c * 128 : (c + 1) * 128]
        acc = jnp.concatenate(acc, axis=1)
        total = total + (pltpu.roll(acc, DIAG - 8 * r, 1) if r else acc)
    bucket = bucket_tile()
    lane = lax.broadcasted_iota(jnp.int32, (8, HS), 1)
    out = jnp.zeros((8, HS), F32)
    for k in range(NBUCKET):
        out = jnp.where(lane == k, jnp.sum(jnp.where(bucket == k, total, 0.0)), out)
    out_ref[...] = out


def current_mask(ids_col_ref, ids_row_ref):
    key = lax.broadcasted_iota(jnp.int32, (BLK, BLK), 0)
    query = lax.broadcasted_iota(jnp.int32, (BLK, BLK), 1)
    ids_row = ids_row_ref[...]
    return (key <= query) | ((ids_col_ref[...] == ids_row) & (ids_row > 0))


def attend_kernel(
    run_ref, table_ref, q_ref, kc_ref, vc_ref, kp_ref, vp_ref, ko_ref, vo_ref, ks_ref, vs_ref,
    row_ref, col_ref, out_ref, lse_ref, bias_ref, score_ref,
):
    h = pl.program_id(0)
    b = pl.program_id(1)

    @pl.when(b == 0)
    def _():
        fill_bias(table_ref, h, bias_ref)

    q = q_ref[...]
    first = b == 0
    keys = (
        ks_ref[...].reshape(BLK, HS),
        jnp.where(first, ko_ref[...], kp_ref[...]),
        kc_ref[...],
    )
    values = (
        vs_ref[...].reshape(BLK, HS),
        jnp.where(first, vo_ref[...], vp_ref[...]),
        vc_ref[...],
    )
    prior_ok = (run_ref[0] > 0) | (b > 0)
    score = mm(keys[0], q, 1, 1) * SCALE
    score_ref[0] = score
    peak = jnp.max(score, axis=0, keepdims=True)
    score = mm(keys[1], q, 1, 1) * SCALE + bias_ref[:BLK]
    score = jnp.where(prior_ok, score, -1e30)
    score_ref[1] = score
    peak = jnp.maximum(peak, jnp.max(score, axis=0, keepdims=True))
    score = mm(keys[2], q, 1, 1) * SCALE + bias_ref[BLK:]
    score = jnp.where(current_mask(col_ref, row_ref), score, -1e30)
    score_ref[2] = score
    peak = jnp.maximum(peak, jnp.max(score, axis=0, keepdims=True))
    total = jnp.zeros((1, BLK), F32)
    for c in range(3):
        exponent = jnp.exp(score_ref[c] - peak)
        score_ref[c] = exponent
        total = total + jnp.sum(exponent, axis=0, keepdims=True)
    inverse = 1.0 / total
    mixed = jnp.zeros((HS, BLK), F32)
    for c in range(3):
        mixed = mixed + mm(values[c], (score_ref[c] * inverse).astype(LOW), 0, 0)
    out_ref[...] = mixed.T.astype(LOW)
    lse_ref[...] = peak + jnp.log(total)


def attend_specs(heads, pieces, part, blocks):
    def at(col):
        return pl.BlockSpec((BLK, HS), lambda h, b: (b, col(h)))

    def before(col):
        return pl.BlockSpec((BLK, HS), lambda h, b: (jnp.maximum(b - 1, 0), col(h)))

    def outer(col):
        return pl.BlockSpec((BLK, HS), lambda h, b: (0, col(h)))

    def state(col):
        return pl.BlockSpec((pieces, None, part, HS), lambda h, b: (0, b, 0, col(h)))

    key, value = (lambda h: h), (lambda h: heads + h)
    return [
        scalars(),
        scalars(),
        at(key),
        at(key),
        at(value),
        before(key),
        before(value),
        outer(key),
        outer(value),
        state(lambda h: 2 * h),
        state(lambda h: 2 * h + 1),
        pl.BlockSpec((None, 1, BLK), lambda h, b: (b, 0, 0)),
        pl.BlockSpec((None, BLK, 1), lambda h, b: (b, 0, 0)),
    ]


def attend(run, table, q, kv, outer, sproj, ids_row, ids_col):
    rows = q.shape[0]
    heads = q.shape[1] // HS
    pieces, blocks, part, _ = sproj.shape
    return pl.pallas_call(
        attend_kernel,
        grid=(heads, blocks),
        out_shape=(
            jax.ShapeDtypeStruct((rows, heads * HS), LOW),
            jax.ShapeDtypeStruct((heads, blocks, 1, BLK), F32),
        ),
        in_specs=attend_specs(heads, pieces, part, blocks),
        out_specs=(
            pl.BlockSpec((BLK, HS), lambda h, b: (b, h)),
            pl.BlockSpec((None, None, 1, BLK), lambda h, b: (h, b, 0, 0)),
        ),
        scratch_shapes=[pltpu.VMEM((2 * BLK, BLK), F32), pltpu.VMEM((3, BLK, BLK), F32)],
        compiler_params=params(2, 20),
        cost_estimate=lasts(9.7),
        name="attend",
    )(run, table, q, kv, kv, kv, kv, outer, outer, sproj, sproj, ids_row, ids_col)


def attend_back_kernel(
    run_ref, table_ref, q_ref, kc_ref, vc_ref, kp_ref, vp_ref, ko_ref, vo_ref, ks_ref, vs_ref,
    row_ref, col_ref, gmix_ref, lse_ref,
    gq_ref, gcur_ref, gprev_ref, gs_ref, gtab_ref,
    bias_ref, gbias_ref, prob_ref, gprob_ref,
):
    h = pl.program_id(0)
    b = pl.program_id(1)

    @pl.when(b == 0)
    def _():
        fill_bias(table_ref, h, bias_ref)
        gbias_ref[...] = jnp.zeros_like(gbias_ref)

    q = q_ref[...]
    gmix = gmix_ref[...]
    lse = lse_ref[...]
    first = b == 0
    keys = (
        ks_ref[...].reshape(BLK, HS),
        jnp.where(first, ko_ref[...], kp_ref[...]),
        kc_ref[...],
    )
    values = (
        vs_ref[...].reshape(BLK, HS),
        jnp.where(first, vo_ref[...], vp_ref[...]),
        vc_ref[...],
    )
    prior_ok = (run_ref[0] > 0) | (b > 0)
    inner = jnp.zeros((1, BLK), F32)
    grad_values = []
    for c in range(3):
        score = mm(keys[c], q, 1, 1) * SCALE
        if c == 1:
            score = jnp.where(prior_ok, score + bias_ref[:BLK], -1e30)
        if c == 2:
            score = jnp.where(current_mask(col_ref, row_ref), score + bias_ref[BLK:], -1e30)
        prob = jnp.exp(score - lse)
        prob_ref[c] = prob
        grad_values.append(mm(prob.astype(LOW), gmix, 1, 0))
        grad_prob = mm(values[c], gmix, 1, 1)
        gprob_ref[c] = grad_prob
        inner = inner + jnp.sum(prob * grad_prob, axis=0, keepdims=True)
    grad_q = jnp.zeros((HS, BLK), F32)
    grad_keys = []
    for c in range(3):
        grad_score = (prob_ref[c] * (gprob_ref[c] - inner)).astype(LOW)
        if c > 0:
            gbias_ref[(c - 1) * BLK : c * BLK, :] += grad_score.astype(F32)
        grad_keys.append(mm(grad_score, q, 1, 0) * SCALE)
        grad_q = grad_q + mm(keys[c], grad_score, 0, 0)
    gq_ref[...] = (grad_q * SCALE).T.astype(LOW)
    part = gs_ref.shape[0], gs_ref.shape[1], HS
    gs_ref[:, :, :HS] = grad_keys[0].astype(LOW).reshape(part)
    gs_ref[:, :, HS:] = grad_values[0].astype(LOW).reshape(part)
    gprev_ref[:, :HS] = grad_keys[1].astype(LOW)
    gprev_ref[:, HS:] = grad_values[1].astype(LOW)
    gcur_ref[:, :HS] = grad_keys[2].astype(LOW)
    gcur_ref[:, HS:] = grad_values[2].astype(LOW)

    @pl.when(b == pl.num_programs(1) - 1)
    def _():
        collapse_bias(gbias_ref, gtab_ref)


def attend_back(run, table, q, kv, outer, sproj, ids_row, ids_col, gmix, lse):
    rows = q.shape[0]
    heads = q.shape[1] // HS
    pieces, blocks, part, _ = sproj.shape

    def at():
        return pl.BlockSpec((BLK, HS), lambda h, b: (b, h))

    side = jax.ShapeDtypeStruct((rows, heads * 2 * HS), LOW)
    pair = pl.BlockSpec((BLK, 2 * HS), lambda h, b: (b, h))
    return pl.pallas_call(
        attend_back_kernel,
        grid=(heads, blocks),
        out_shape=(
            jax.ShapeDtypeStruct((rows, heads * HS), LOW),
            side,
            side,
            jax.ShapeDtypeStruct((pieces, blocks, part, heads * 2 * HS), LOW),
            jax.ShapeDtypeStruct((heads, 8, HS), F32),
        ),
        in_specs=attend_specs(heads, pieces, part, blocks)
        + [at(), pl.BlockSpec((None, None, 1, BLK), lambda h, b: (h, b, 0, 0))],
        out_specs=(
            at(),
            pair,
            pair,
            pl.BlockSpec((pieces, None, part, 2 * HS), lambda h, b: (0, b, 0, h)),
            pl.BlockSpec((None, 8, HS), lambda h, b: (h, 0, 0)),
        ),
        scratch_shapes=[
            pltpu.VMEM((2 * BLK, BLK), F32),
            pltpu.VMEM((2 * BLK, BLK), F32),
            pltpu.VMEM((3, BLK, BLK), F32),
            pltpu.VMEM((3, BLK, BLK), F32),
        ],
        compiler_params=params(2, 28),
        cost_estimate=lasts(16),
        name="attend_back",
    )(run, table, q, kv, kv, kv, kv, outer, outer, sproj, sproj, ids_row, ids_col, gmix, lse)


def state_back_kernel(
    sq_ref, k_ref, v_ref, gmix_ref, gcur_ref, gnext_ref, gouter_ref,
    gkv_ref, gsq_ref, smix_ref,
):
    b = pl.program_id(1)
    last = b == pl.num_programs(1) - 1
    pieces, part = sq_ref.shape[0], sq_ref.shape[1]
    sq = sq_ref[...].reshape(BLK, HS)
    gmix = gmix_ref[...].reshape(BLK, HS)
    k, v = k_ref[...], v_ref[...]
    weights = column_softmax(mm(k, sq, 1, 1) * SCALE)
    low = weights.astype(LOW)
    grad_w = mm(v, gmix, 1, 1)
    inner = jnp.sum(grad_w * weights, axis=0, keepdims=True)
    grad_s = (weights * (grad_w - inner)).astype(LOW)
    grad_k = mm(grad_s, sq, 1, 0) * SCALE
    grad_v = mm(low, gmix, 1, 0)
    grad_q = mm(k, grad_s, 0, 0) * SCALE
    smix = mm(v, low, 0, 0)
    rest = gcur_ref[...].astype(F32) + jnp.where(last, gouter_ref[...], gnext_ref[...]).astype(F32)
    gkv_ref[:, :HS] = (rest[:, :HS] + grad_k).astype(LOW)
    gkv_ref[:, HS:] = (rest[:, HS:] + grad_v).astype(LOW)
    gsq_ref[...] = grad_q.T.astype(LOW).reshape(pieces, part, HS)
    smix_ref[...] = smix.T.astype(LOW).reshape(pieces, part, HS)


def state_back(sq, kv, gmix, gcur, gprev, outer):
    rows = gcur.shape[0]
    heads = gcur.shape[1] // (2 * HS)
    pieces, blocks, part, _ = sq.shape

    def at(col=lambda h: h):
        return pl.BlockSpec((BLK, HS), lambda h, b: (b, col(h)))

    def state():
        return pl.BlockSpec((pieces, None, part, HS), lambda h, b: (0, b, 0, h))

    side = jax.ShapeDtypeStruct((pieces, blocks, part, heads * HS), LOW)
    return pl.pallas_call(
        state_back_kernel,
        grid=(heads, blocks),
        out_shape=(jax.ShapeDtypeStruct((rows, heads * 2 * HS), LOW), side, side),
        in_specs=[
            state(),
            at(),
            at(lambda h: heads + h),
            state(),
            pl.BlockSpec((BLK, 2 * HS), lambda h, b: (b, h)),
            pl.BlockSpec((BLK, 2 * HS), lambda h, b: (jnp.minimum(b + 1, blocks - 1), h)),
            pl.BlockSpec((BLK, 2 * HS), lambda h, b: (0, h)),
        ],
        out_specs=(
            pl.BlockSpec((BLK, 2 * HS), lambda h, b: (b, h)),
            state(),
            state(),
        ),
        compiler_params=params(2, 16),
        cost_estimate=lasts(6.5),
        name="state_back",
    )(sq, kv, kv, gmix, gcur, gprev, outer)


def passed_along(array, axis, by):
    size = lax.axis_size(axis)
    pairs = [(i, i + by) for i in range(size) if 0 <= i + by < size]
    return lax.ppermute(array, axis, pairs)


def swap(array, axis, bits):
    return lax.ppermute(array, axis, [(i, i ^ bits) for i in range(lax.axis_size(axis))])


def gather_rel(array, filler=None):
    size = lax.axis_size("tensor")
    pieces = []
    for m in range(0, size, 2):
        piece = array if m == 0 else swap(array, "tensor", m)
        if m and filler is not None:
            piece = after(piece, filler)
        pieces += [piece, swap(piece, "tensor", 1)]
    return pieces


def reduce_first(even, odd):
    got = swap(odd, "tensor", 1)
    return [even[j].astype(F32) + got[j].astype(F32) for j in range(even.shape[0])]


def reduce_last(sums, filler=None):
    terms = [sums[0]]
    for j, send in enumerate(sums[1:], 1):
        term = swap(send, "tensor", 2 * j)
        terms.append(term if filler is None else after(term, filler))
    return terms


def lower(sums):
    return [sums[0]] + [term.astype(LOW) for term in sums[1:]]


def exchange_rel(parts):
    return [part if m == 0 else swap(part, "tensor", m) for m, part in enumerate(parts)]


def cut(array, me):
    size = lax.axis_size("tensor")
    rows = array.shape[0] // size
    return [lax.dynamic_slice_in_dim(array, (me ^ m) * rows, rows, 0) for m in range(size)]


def place(pieces, me):
    rows = pieces[0].shape[0]
    out = jnp.zeros((rows * len(pieces),) + pieces[0].shape[1:], pieces[0].dtype)
    for m, piece in enumerate(pieces):
        out = lax.dynamic_update_slice_in_dim(out, piece, (me ^ m) * rows, 0)
    return out


def sum_all(array):
    for axis in ("tensor", "context", "shard"):
        bits = 1
        while bits < lax.axis_size(axis):
            array = array + swap(array, axis, bits)
            bits *= 2
    return array


def rms_back(v, gain, grad):
    r = rms_scale(v)
    unit = v * r
    scaled = grad * gain
    return r * (scaled - unit * jnp.mean(scaled * unit, axis=-1, keepdims=True))


def dot(a, b, ca, cb):
    return lax.dot_general(a, b, (((ca,), (cb,)), ((), ())), preferred_element_type=F32)


def after(array, *others):
    return lax.optimization_barrier((array,) + others)[0]


def half_rows(local, run):
    part = local.shape[0] // 2
    return lax.dynamic_slice_in_dim(local, run * part, part, 0)


def shard_pieces(array):
    return [array if s == 0 else swap(array, "shard", s) for s in range(lax.axis_size("shard"))]


def scatter_rows(grad):
    return lax.psum_scatter(grad, "shard", scatter_dimension=0, tiled=True)


def shards(
    tokens,
    piece_ids,
    tok_qkv,
    state_qkv,
    tok_out,
    state_out,
    mlp_in,
    mlp_out,
    rel_bias,
    init_state,
    norm_gains,
    decay_param,
    cotangent,
):
    size = lax.axis_size("tensor")
    shard_count = lax.axis_size("shard")
    me = lax.axis_index("tensor")
    shard_pos = lax.axis_index("shard")
    run_pos = lax.axis_index("context")
    run_count = lax.axis_size("context")
    me_arr = me.astype(jnp.int32)[None]
    run_arr = run_pos.astype(jnp.int32)[None]
    pos = jnp.stack([shard_pos, run_pos]).astype(jnp.int32)
    own = tokens[0]
    own_rows, width = own.shape
    rows = own_rows * size
    blocks = rows // BLK
    heads = tok_qkv.shape[1]
    part = init_state.shape[0]
    span = heads * HS

    cols = norm_gains.shape[1]
    bias_rows = rel_bias.shape[0]
    slot_size = NBUCKET * heads
    small = jnp.zeros((SMALL, width), LOW)
    small = lax.dynamic_update_slice(
        small, jnp.concatenate([norm_gains, decay_param[None]], 0), (0, (shard_pos * size + me) * cols)
    )
    small = lax.dynamic_update_slice(
        small, rel_bias.reshape(1, -1), (4, me * slot_size + shard_pos * bias_rows * heads)
    )
    small = sum(piece.astype(F32) for piece in shard_pieces(small)).astype(LOW)
    token_pieces = gather_rel(jnp.concatenate([own, small], axis=0))

    local_chain = jnp.concatenate(
        [state_qkv[:, :, :HS].reshape(-1, span), state_out.reshape(span, -1).T, init_state.T], axis=1
    )
    chain_pieces = shard_pieces(half_rows(local_chain, run_pos))
    chain_other = swap(jnp.stack(chain_pieces), "context", 1)
    tok_parts = shard_pieces(after(tok_qkv.reshape(-1, heads * 384), small, *chain_pieces))
    chain_other = after(chain_other, *token_pieces)
    chain_own, start = assemble(pos, chain_pieces, chain_other, (2 * span, part))
    start = start.astype(F32).T
    chain_w = gather_rel(chain_own)
    w_sq, w_sout = chain_own[:, :span], chain_own[:, span:]

    local_side = jnp.concatenate(
        [state_qkv[:, :, HS:].reshape(-1, 2 * span), tok_out.reshape(span, -1).T], axis=1
    )
    local_mlp = jnp.concatenate([mlp_in, mlp_out.T], axis=1)

    q, normed_a, vectors, wq_tok, wkv_tok, kv, *kv_blocks = token_proj(
        me_arr, pos, token_pieces, [after(piece, chain_own) for piece in tok_parts], blocks
    )
    w_side = lax.all_gather(after(local_side, q), "shard", axis=0, tiled=True)
    w_skv, w_tout = w_side[:, : 2 * span], w_side[:, 2 * span :]
    gains = vectors[:3]
    decay = jax.nn.sigmoid(vectors[3:4])
    table = lax.dynamic_slice_in_dim(vectors[4], me * slot_size, slot_size, 0)
    table = table.reshape(NBUCKET, heads).T
    kv_pieces = [gather_rel(after(kv_blocks[0], *chain_w))]
    outer = passed_along(kv_blocks[-1], "context", 1)

    gain_s = gains[2:3]
    incoming = start = after(start, outer)
    for round_index in range(run_count):
        state = jnp.where(run_pos == 0, start, incoming)
        states, normeds, updates = [], [], []
        for b in range(blocks):
            states.append(state)
            if b == len(kv_pieces):
                kv_pieces.append(gather_rel(after(kv_blocks[b], *kv_pieces[-1]), state))
            normed, update, state = chain_forward(state, gain_s, decay, kv_pieces[b], chain_w)
            if round_index + b == 0:
                w_mlp = lax.all_gather(after(local_mlp, state), "shard", axis=0, tiled=True)
            normeds.append(normed)
            updates.append(update)
        if round_index + 1 < run_count:
            incoming = passed_along(state.astype(LOW), "context", 1)
            if round_index == 0:
                grad_pieces = gather_rel(after(cotangent[0], *kv_pieces[-1]))
                tout_pieces = gather_rel(after(w_tout, *grad_pieces))
            incoming = incoming.astype(F32)
    units = mlp_in.shape[1]
    w_in, w_out = w_mlp[:, :units], w_mlp[:, units:]
    normeds[-1] = (states[-1] * rms_scale(states[-1]) * gain_s).astype(LOW)
    state_pieces = gather_rel(jnp.concatenate(normeds, axis=0), updates[-1])
    sq, skv = proj(state_pieces, [w_sq, w_skv])
    sq = sq.reshape(size, blocks, part, span)
    skv = skv.reshape(size, blocks, part, 2 * span)

    ids_row = piece_ids.reshape(blocks, 1, BLK)
    ids_col = piece_ids.reshape(blocks, BLK, 1)
    mixed, lse = attend(run_arr, table, q, kv, outer, skv, ids_row, ids_col)
    mixed_parts = cut(mixed, me)
    residual, normed_m, squares = branch_out(own, gains[1:2], exchange_rel(mixed_parts), tout_pieces)

    (grad_hidden,) = proj([after(piece, normed_m) for piece in grad_pieces], [w_out])
    mlp_pieces = gather_rel(normed_m, grad_hidden)
    hidden, grad_pre, even, odd = feed(w_in, grad_hidden, mlp_pieces)
    sums = lower(reduce_first(even, odd))
    grad_w_mlp = weight_grad([(mlp_pieces, after(grad_pre, *sums)), (grad_pieces, hidden)])
    terms = reduce_last(sums, grad_w_mlp)
    mlp_mine = scatter_rows(grad_w_mlp)

    grad_res, grad_branch, grad_gain_m, *gmix_parts = branch_back(
        cotangent[0], residual, gains[1:2], terms, tout_pieces
    )
    gmix = place(exchange_rel(gmix_parts), me)
    gq, gcur, gprev, gs, gtab = attend_back(
        run_arr, table, q, kv, outer, skv, ids_row, ids_col, gmix, lse
    )
    branch_pieces = gather_rel(after(grad_branch, gmix), gq)
    gs = after(gs, branch_pieces[-2])
    outer_back = passed_along(gprev[:BLK], "context", -1)

    gs = gs.reshape(-1, 2 * span)
    zero_arr = jnp.zeros((1,), jnp.int32)
    even, odd = back(zero_arr, [gs], [w_skv])
    sums = lower(reduce_first(even, odd))
    even, odd = back(zero_arr, [after(hidden, *sums)], [w_out])
    grad_state_kv = sum(term.astype(F32) for term in reduce_last(sums, even))
    grad_state_kv = after(grad_state_kv, outer_back).reshape(blocks, part, width)
    sums = lower(reduce_first(even, odd))
    branch_m = reduce_last([after(term, grad_state_kv) for term in sums])

    incoming = jnp.zeros_like(start)
    for round_index in range(run_count):
        carry = jnp.where(run_pos == run_count - 1, 0.0, incoming)
        gups = [None] * blocks
        gup = ((1.0 - decay) * carry).astype(LOW)
        chain_small = jnp.zeros((2, width), F32)
        for b in reversed(range(blocks)):
            gups[b] = gup
            carry, gup, row_sums = chain_backward(
                carry, gain_s, decay, states[b], normeds[b], updates[b], grad_state_kv[b],
                kv_pieces[b], chain_w,
            )
            chain_small = chain_small + row_sums
        if round_index + 1 < run_count:
            incoming = passed_along(carry.astype(LOW), "context", -1)
            if round_index == 0:
                grad_w_early = weight_grad(
                    [
                        ([normed_a], after(gq, carry)),
                        (state_pieces, gs),
                        (branch_pieces, jnp.concatenate(mixed_parts, axis=0)),
                    ]
                )
                incoming = after(incoming, grad_w_early, mlp_mine, *branch_m)
            incoming = incoming.astype(F32)
    grad_start = jnp.where(run_pos == 0, carry, 0.0).astype(LOW)
    branch_m = sum(term.astype(F32) for term in branch_m)
    output = (residual + branch_m).astype(LOW)
    gup_pieces = gather_rel(jnp.concatenate(gups, axis=0), carry)
    mlp_got = swap(after(mlp_mine, incoming), "context", 1)
    early_mine = scatter_rows(after(grad_w_early, mlp_mine))
    (gsmix,) = proj(gup_pieces, [w_sout])
    gsmix = gsmix.reshape(size, blocks, part, span)
    gkv, gsq, smix = state_back(sq, kv, gsmix, gcur, gprev, outer_back)
    grad_w_late = weight_grad(
        [([normed_a], gkv), (state_pieces, gsq.reshape(-1, span)), (gup_pieces, smix.reshape(-1, span))]
    )
    late_mine = scatter_rows(jnp.concatenate([after(grad_w_late, early_mine), grad_start.T], axis=1))
    early_got = swap(after(early_mine, mlp_got), "context", 1)
    g_mlp = mlp_mine.astype(F32) + mlp_got.astype(F32)
    g_early = early_mine.astype(F32) + early_got.astype(F32)
    g_late = late_mine.astype(F32) + swap(late_mine, "context", 1).astype(F32)

    even, odd, gain_sums = back(me_arr, [gq, after(gkv, grad_w_late)], [wq_tok, wkv_tok], normed_a)
    grad_gain_a = (gain_sums / gains[0:1])[0]
    inputs = own.astype(F32)
    grad_normed_a = sum(
        term.astype(F32) for term in reduce_last(lower(reduce_first(even, odd)))
    )
    grad_tokens = (grad_res + rms_back(inputs, gains[0], grad_normed_a)).astype(LOW)

    def by_head(array):
        return array.reshape(array.shape[0], heads, -1)

    g_tok = jnp.concatenate([by_head(g_early[:, :span]), by_head(g_late[:, : 2 * span])], axis=2)
    g_state = jnp.concatenate(
        [by_head(g_late[:, 2 * span : 3 * span]), by_head(g_early[:, span : 3 * span])], axis=2
    )
    g_tout = g_early[:, 3 * span :].T.reshape(heads, HS, -1)
    g_sout = g_late[:, 3 * span : 4 * span].T.reshape(heads, HS, -1)

    squares = jnp.concatenate([jnp.sum(squares, axis=1), jnp.sum(branch_m * branch_m)[None]])
    slot = gtab[:, 0, :NBUCKET].reshape(-1)
    slots = lax.dynamic_update_slice_in_dim(
        jnp.zeros((size * slot.size,), F32), slot, me * slot.size, 0
    )
    tail = jnp.concatenate([slots, squares])
    tail = jnp.pad(tail, (0, width - tail.size))
    grad_decay = chain_small[1] * (decay * (1.0 - decay))[0]
    sums = sum_all(
        jnp.stack([grad_gain_a, grad_gain_m[0], chain_small[0], grad_decay, tail])
    )
    place_at = (shard_pos * size + me) * cols
    mine = lax.dynamic_slice_in_dim(sums[:4], place_at, cols, 1)
    table_sum = lax.dynamic_slice_in_dim(sums[4], me * slot.size, slot.size, 0)
    table_sum = table_sum.reshape(heads, NBUCKET).T
    g_table = lax.dynamic_slice_in_dim(table_sum, shard_pos * bias_rows, bias_rows, 0)
    entries = own.size * shard_count * run_count * size
    first = size * slot.size
    rms_out = jnp.sqrt(sums[4, first : first + 3] / entries)

    return (
        output[None],
        grad_tokens[None],
        g_tok,
        g_state,
        g_tout,
        g_sout,
        g_mlp[:, :units],
        g_mlp[:, units:].T,
        g_table,
        g_late[:, 4 * span :].T,
        mine[:3],
        mine[3],
        rms_out,
    )


def solution(mesh):
    return jax.shard_map(
        shards,
        mesh=mesh,
        in_specs=(
            P("shard", ("context", "tensor"), None),
            P("shard", "context"),
            P("shard", "tensor", None),
            P("shard", "tensor", None),
            P("tensor", None, "shard"),
            P("tensor", None, "shard"),
            P("shard", "tensor"),
            P("tensor", "shard"),
            P("shard", "tensor"),
            P("tensor", "shard"),
            P(None, ("shard", "tensor")),
            P(("shard", "tensor")),
            P("shard", ("context", "tensor"), None),
        ),
        out_specs=(
            P("shard", ("context", "tensor"), None),
            P("shard", ("context", "tensor"), None),
            P("shard", "tensor", None),
            P("shard", "tensor", None),
            P("tensor", None, "shard"),
            P("tensor", None, "shard"),
            P("shard", "tensor"),
            P("tensor", "shard"),
            P("shard", "tensor"),
            P("tensor", "shard"),
            P(None, ("shard", "tensor")),
            P(("shard", "tensor")),
            P(),
        ),
        check_vma=False,
    )
```

```python
import functools

import jax
import jax.numpy as jnp
from jax import lax
from jax.experimental import pallas as pl
from jax.experimental.pallas import tpu as pltpu
from jax.sharding import PartitionSpec as P

HS = 128
BLK = 512
NBUCKET = 32
EDGES = (12, 16, 23, 32, 46, 64, 91)
LOW = jnp.bfloat16
F32 = jnp.float32
SCALE = HS ** (-0.5)
EPS = 1e-06
DIAG = 3 * BLK
SMALL = 16
PACE = 0.5


def mm(a, b, ca, cb):
    return lax.dot_general(a, b, (((ca,), (cb,)), ((), ())), preferred_element_type=F32)


def whole():
    return pl.BlockSpec(memory_space=pltpu.VMEM)


def columns(weight):
    _, width, index = weight
    return pl.BlockSpec((weight[0].shape[0], width), lambda *_: (0, index))


def scalars():
    return pl.BlockSpec(memory_space=pltpu.SMEM)


def params(grid_rank=0, mib=40):
    limit = mib * 1024 * 1024
    if grid_rank:
        return pltpu.CompilerParams(
            dimension_semantics=("arbitrary",) * grid_rank, vmem_limit_bytes=limit
        )
    return pltpu.CompilerParams(vmem_limit_bytes=limit)


def lasts(microseconds):
    return pl.CostEstimate(
        flops=int(microseconds * PACE * 1.1e9), bytes_accessed=int(microseconds * PACE * 3e6), transcendentals=0
    )


def rms_scale(v):
    return lax.rsqrt(jnp.mean(v * v, axis=-1, keepdims=True) + EPS)


def assemble_kernel(count, pos_ref, *refs):
    pieces, other_ref, outs = refs[:count], refs[count], refs[count + 1 :]
    part = pieces[0].shape[0]
    for s in range(count):
        base = (pos_ref[0] ^ s) * (2 * part)
        mine = pl.multiple_of(base + pos_ref[1] * part, part)
        theirs = pl.multiple_of(base + (1 - pos_ref[1]) * part, part)
        first = 0
        for out_ref in outs:
            last = first + out_ref.shape[1]
            out_ref[pl.ds(mine, part), :] = pieces[s][:, first:last]
            out_ref[pl.ds(theirs, part), :] = other_ref[s, :, first:last]
            first = last


def assemble(pos, pieces, other, widths):
    part, cols = pieces[0].shape
    rows = 2 * part * len(pieces)
    return pl.pallas_call(
        functools.partial(assemble_kernel, len(pieces)),
        out_shape=tuple(jax.ShapeDtypeStruct((rows, w), LOW) for w in widths),
        in_specs=[scalars()] + [whole()] * (len(pieces) + 1),
        out_specs=(whole(),) * len(widths),
        compiler_params=params(mib=16),
        cost_estimate=lasts(1.5),
        name="assemble",
    )(pos, *pieces, other)


def weight_grad_kernel(counts, *refs):
    out_ref = refs[-1]
    at = 0
    first = 0
    for count in counts:
        right = refs[at + count]
        total = None
        row = 0
        for left in refs[at : at + count]:
            term = mm(left[...], right[row : row + left.shape[0], :], 0, 0)
            row += left.shape[0]
            total = term if total is None else total + term
        out_ref[:, first : first + right.shape[1]] = total.astype(LOW)
        first += right.shape[1]
        at += count + 1


def weight_grad(pairs):
    width = pairs[0][0][0].shape[1]
    tile = 256
    specs, args, flops = [], [], 0
    for lefts, right in pairs:
        specs += [pl.BlockSpec((left.shape[0], tile), lambda i: (0, i)) for left in lefts]
        specs.append(pl.BlockSpec(right.shape, lambda i: (0, 0)))
        args += list(lefts) + [right]
        flops += 2 * right.size * width
    cols = sum(right.shape[1] for _, right in pairs)
    return pl.pallas_call(
        functools.partial(weight_grad_kernel, [len(lefts) for lefts, _ in pairs]),
        grid=(width // tile,),
        out_shape=jax.ShapeDtypeStruct((width, cols), LOW),
        in_specs=specs,
        out_specs=pl.BlockSpec((tile, cols), lambda i: (i, 0)),
        compiler_params=params(1, 32),
        cost_estimate=lasts(6),
        name="weight_grad",
    )(*args)


def token_proj_kernel(count, shards, blocks, me_ref, w_ref, *refs):
    pieces, small = refs[:count], refs[count : count + shards]
    q_ref, normed_ref, vec_ref, wq_ref, wkv_ref, scratch, *kv_refs = refs[count + shards :]
    heads = w_ref.shape[1] // 384
    span = heads * HS
    rows = pieces[0].shape[0] - SMALL
    vectors = small[0][...].astype(F32)
    for piece in small[1:]:
        vectors = vectors + piece[...].astype(F32)
    vec_ref[...] = vectors
    gain = vectors[0:1]
    for m in range(count):
        start = pl.multiple_of((me_ref[0] ^ m) * rows, rows)
        v = pieces[m][:rows, :].astype(F32)
        normed = (v * rms_scale(v) * gain).astype(LOW)
        normed_ref[pl.ds(start, rows), :] = normed
        for h in range(heads):
            out = mm(normed, w_ref[:, h * 384 : (h + 1) * 384], 1, 0).astype(LOW)
            q_ref[pl.ds(start, rows), h * HS : (h + 1) * HS] = out[:, :HS]
            scratch[pl.ds(start, rows), h * HS : (h + 1) * HS] = out[:, HS : 2 * HS]
            scratch[pl.ds(start, rows), span + h * HS : span + (h + 1) * HS] = out[:, 2 * HS :]
    for b in range(blocks):
        kv_refs[b][...] = scratch[b * BLK : (b + 1) * BLK, :]
    for h in range(heads):
        wq_ref[:, h * HS : (h + 1) * HS] = w_ref[:, h * 384 : h * 384 + HS]
        wkv_ref[:, 2 * h * HS : 2 * (h + 1) * HS] = w_ref[:, h * 384 + HS : (h + 1) * 384]


def token_proj(me, pieces, small, weight, blocks):
    width, cols = weight.shape
    span = cols // 3
    rows = (pieces[0].shape[0] - SMALL) * len(pieces)
    return pl.pallas_call(
        functools.partial(token_proj_kernel, len(pieces), len(small), blocks),
        out_shape=(
            jax.ShapeDtypeStruct((rows, span), LOW),
            jax.ShapeDtypeStruct((rows, width), LOW),
            jax.ShapeDtypeStruct((SMALL, width), F32),
            jax.ShapeDtypeStruct((width, span), LOW),
            jax.ShapeDtypeStruct((width, 2 * span), LOW),
            jax.ShapeDtypeStruct((rows, 2 * span), LOW),
        )
        + (jax.ShapeDtypeStruct((BLK, 2 * span), LOW),) * blocks,
        in_specs=[scalars(), whole()] + [whole()] * (len(pieces) + len(small)),
        out_specs=(whole(),) * (6 + blocks),
        compiler_params=params(mib=56),
        cost_estimate=lasts(5),
        name="token_proj",
    )(me, weight, *pieces, *small)


def proj_kernel(count, weights, *refs):
    pieces, ws, outs = refs[:count], refs[count : count + weights], refs[count + weights :]
    rows = pieces[0].shape[0]
    for m in range(count):
        for w, out in zip(ws, outs, strict=True):
            out[m * rows : (m + 1) * rows, :] = mm(pieces[m][...], w[...], 1, 0).astype(LOW)


def proj(pieces, weights):
    rows = pieces[0].shape[0] * len(pieces)
    return pl.pallas_call(
        functools.partial(proj_kernel, len(pieces), len(weights)),
        grid=(1,),
        out_shape=tuple(jax.ShapeDtypeStruct((rows, w[1]), LOW) for w in weights),
        in_specs=[whole()] * len(pieces) + [columns(w) for w in weights],
        out_specs=(whole(),) * len(weights),
        compiler_params=params(1, 24),
        cost_estimate=lasts(3),
        name="proj",
    )(*pieces, *[w[0] for w in weights])


def back_kernel(count, gained, me_ref, *refs):
    even_ref, odd_ref = refs[2 * count + gained : 2 * count + gained + 2]
    total = None
    for i in range(count):
        term = mm(refs[i][...], refs[count + i][...], 1, 1)
        total = term if total is None else total + term
    if gained:
        sums = jnp.sum(total * refs[2 * count][...].astype(F32), axis=0, keepdims=True)
        first = pl.program_id(0) == 0
        refs[-1][...] = sums + jnp.where(first, 0.0, refs[-1][...])
    total = total.astype(LOW)
    even = lax.rem(pl.program_id(0), 2) == 0

    @pl.when(even)
    def _():
        even_ref[...] = total

    @pl.when(jnp.logical_not(even))
    def _():
        odd_ref[...] = total


def back(me, grads, weights, normed=None):
    rows, width = grads[0].shape[0], weights[0][0].shape[0]
    size = lax.axis_size("tensor")
    tile = rows // size
    half = jax.ShapeDtypeStruct((size // 2, tile, width), LOW)
    extra = [] if normed is None else [normed]
    grid_spec = pltpu.PrefetchScalarGridSpec(
        num_scalar_prefetch=1,
        grid=(size,),
        in_specs=[pl.BlockSpec((tile, g.shape[1]), lambda i, me_ref: (i ^ me_ref[0], 0)) for g in grads]
        + [columns(w) for w in weights]
        + [pl.BlockSpec((tile, width), lambda i, me_ref: (i ^ me_ref[0], 0)) for _ in extra],
        out_specs=(
            pl.BlockSpec((None, tile, width), lambda i, me_ref: (i // 2, 0, 0)),
            pl.BlockSpec((None, tile, width), lambda i, me_ref: (i // 2, 0, 0)),
        )
        + (pl.BlockSpec((1, width), lambda i, me_ref: (0, 0)),) * len(extra),
    )
    return pl.pallas_call(
        functools.partial(back_kernel, len(grads), len(extra)),
        grid_spec=grid_spec,
        out_shape=(half, half) + (jax.ShapeDtypeStruct((1, width), F32),) * len(extra),
        compiler_params=params(1, 24),
        cost_estimate=lasts(3),
        name="back",
    )(me, *grads, *[w[0] for w in weights], *extra)


def branch_kernel(count, own_ref, gain_ref, *refs):
    parts, weights = refs[:count], refs[count : 2 * count]
    residual_ref, normed_ref, sums_ref = refs[2 * count :]
    branch = None
    for part, weight in zip(parts, weights, strict=True):
        term = mm(part[...], weight[...], 1, 1)
        branch = term if branch is None else branch + term
    own = own_ref[...].astype(F32)
    residual = own + branch
    residual_ref[...] = residual
    normed_ref[...] = (residual * rms_scale(residual) * gain_ref[...]).astype(LOW)
    sums_ref[0:1, :] = jnp.sum(own * own, axis=0, keepdims=True)
    sums_ref[1:2, :] = jnp.sum(branch * branch, axis=0, keepdims=True)


def branch_out(own, gain, parts, weights):
    rows, width = own.shape
    return pl.pallas_call(
        functools.partial(branch_kernel, len(parts)),
        out_shape=(
            jax.ShapeDtypeStruct((rows, width), F32),
            jax.ShapeDtypeStruct((rows, width), LOW),
            jax.ShapeDtypeStruct((2, width), F32),
        ),
        in_specs=[whole()] * (2 + 2 * len(parts)),
        out_specs=(whole(),) * 3,
        compiler_params=params(mib=12),
        cost_estimate=lasts(3),
        name="branch_out",
    )(own, gain, *parts, *weights)


def branch_back_kernel(count, sums, cot_ref, residual_ref, gain_ref, *refs):
    terms, weights, outs = refs[:sums], refs[sums : sums + count], refs[sums + count :]
    grad_ref, low_ref, gain_sum_ref, parts = outs[0], outs[1], outs[2], outs[3:]
    grad = terms[0][...].astype(F32)
    for term in terms[1:]:
        grad = grad + term[...].astype(F32)
    residual = residual_ref[...]
    r = rms_scale(residual)
    unit = residual * r
    gain_sum_ref[...] = jnp.sum(grad * unit, axis=0, keepdims=True)
    scaled = grad * gain_ref[...]
    grad = cot_ref[...].astype(F32) + r * (
        scaled - unit * jnp.mean(scaled * unit, axis=-1, keepdims=True)
    )
    grad_ref[...] = grad
    low = grad.astype(LOW)
    low_ref[...] = low
    for part, weight in zip(parts, weights, strict=True):
        part[...] = mm(low, weight[...], 1, 0).astype(LOW)


def branch_back(cot, residual, gain, terms, weights):
    rows, width = cot.shape
    span = weights[0].shape[1]
    return pl.pallas_call(
        functools.partial(branch_back_kernel, len(weights), len(terms)),
        out_shape=(
            jax.ShapeDtypeStruct((rows, width), F32),
            jax.ShapeDtypeStruct((rows, width), LOW),
            jax.ShapeDtypeStruct((1, width), F32),
        )
        + (jax.ShapeDtypeStruct((rows, span), LOW),) * len(weights),
        in_specs=[whole()] * (3 + len(terms) + len(weights)),
        out_specs=(whole(),) * (3 + len(weights)),
        compiler_params=params(mib=56),
        cost_estimate=lasts(2.5),
        name="branch_back",
    )(cot, residual, gain, *terms, *weights)


def gelu_parts(pre):
    half = 0.5 * (1.0 + lax.erf(pre * 0.7071067811865476))
    density = jnp.exp(pre * pre * -0.5) * 0.3989422804014327
    return half, density


def feed_kernel(count, w_ref, ghid_ref, *refs):
    pieces = refs[:count]
    hidden_ref, gpre_ref, even_ref, odd_ref = refs[count:]
    rows = pieces[0].shape[0]
    for m in range(count):
        at = slice(m * rows, (m + 1) * rows)
        pre = mm(pieces[m][...], w_ref[...], 1, 0)
        half, density = gelu_parts(pre)
        hidden_ref[at, :] = (pre * half).astype(LOW)
        gpre = ((half + pre * density) * ghid_ref[at, :].astype(F32)).astype(LOW)
        gpre_ref[at, :] = gpre
        (even_ref, odd_ref)[m % 2][m // 2] = mm(gpre, w_ref[...], 1, 1).astype(LOW)


def feed(w_in, ghid, pieces):
    width, units = w_in[0].shape[0], w_in[1]
    own = pieces[0].shape[0]
    rows = own * len(pieces)
    half = jax.ShapeDtypeStruct((len(pieces) // 2, own, width), LOW)
    return pl.pallas_call(
        functools.partial(feed_kernel, len(pieces)),
        grid=(1,),
        out_shape=(
            jax.ShapeDtypeStruct((rows, units), LOW),
            jax.ShapeDtypeStruct((rows, units), LOW),
            half,
            half,
        ),
        in_specs=[columns(w_in)] + [whole()] * (1 + len(pieces)),
        out_specs=(whole(),) * 4,
        compiler_params=params(1, 32),
        cost_estimate=lasts(7),
        name="feed",
    )(w_in[0], ghid, *pieces)


def column_softmax(scores):
    peak = jnp.max(scores, axis=0, keepdims=True)
    exponent = jnp.exp(scores - peak)
    return exponent * (1.0 / jnp.sum(exponent, axis=0, keepdims=True))


def chain_loads(count, refs, sems):
    kv_far, w_far, kv, w = (refs[i * count : (i + 1) * count] for i in range(4))
    copies = []
    for m in range(count):
        copies.append(
            (
                pltpu.make_async_copy(w_far[m], w[m], sems.at[m]),
                pltpu.make_async_copy(kv_far[m], kv[m], sems.at[count + m]),
            )
        )
    for pair in copies:
        for copy in pair:
            copy.start()
    return kv, w, copies


def chosen(flag_ref, mine_ref, got_refs):
    value = mine_ref[...]
    if got_refs:
        value = jnp.where(flag_ref[0] != 0, got_refs[0][...].astype(F32), value)
    return value


def head_keys(kv, h):
    return kv[:, h * HS : (h + 1) * HS]


def head_values(kv, heads, h):
    return kv[:, (heads + h) * HS : (heads + h + 1) * HS]


def stacked(parts):
    return parts[0] if len(parts) == 1 else jnp.concatenate(parts, axis=0)


def chain_forward_kernel(count, heads, got, flag_ref, gain_ref, dec_ref, *refs):
    mine_ref, got_refs = refs[0], refs[1 : 1 + got]
    far, refs = refs[1 + got : 1 + got + 2 * count], refs[1 + got + 2 * count :]
    state_ref, pair_ref, update_ref, next_ref, low_ref = refs[:5]
    kv, w, copies = chain_loads(count, far + refs[5 : 5 + 2 * count], refs[5 + 2 * count])
    span = heads * HS
    dec = dec_ref[...]
    gain = gain_ref[...]
    state = chosen(flag_ref, mine_ref, got_refs)
    rows = state.shape[0]
    state_ref[...] = state
    normed = (state * rms_scale(state) * gain).astype(LOW)
    pair_ref[:rows, :] = normed
    queries = []
    for m in range(count):
        copies[m][0].wait()
        queries.append(mm(normed, w[m][:, :span], 1, 0).astype(LOW))
    scores = []
    for m in range(count):
        copies[m][1].wait()
        for h in range(heads):
            scores.append(mm(head_keys(kv[m], h), queries[m][:, h * HS : (h + 1) * HS], 1, 1) * SCALE)
    weights = [column_softmax(score).astype(LOW) for score in scores]
    mixed = [
        stacked([mm(head_values(kv[m], heads, h), weights[m * heads + h], 0, 0) for h in range(heads)])
        for m in range(count)
    ]
    update = None
    for m in range(count):
        term = mm(mixed[m].T.astype(LOW), w[m][:, span:], 1, 1)
        update = term if update is None else update + term
    update_ref[...] = update
    state = dec * state + (1.0 - dec) * update
    next_ref[...] = state
    low_ref[...] = state.astype(LOW)
    pair_ref[rows:, :] = (state * rms_scale(state) * gain).astype(LOW)


def chain_scratch(kv, weights):
    return (
        [pltpu.VMEM(block.shape, LOW) for block in kv]
        + [pltpu.VMEM(weight.shape, LOW) for weight in weights]
        + [pltpu.SemaphoreType.DMA((2 * len(kv),))]
    )


def chain_forward(flag, mine, got, gain, dec, kv, weights):
    count = len(kv)
    rows, width = mine.shape
    heads = kv[0].shape[1] // (2 * HS)
    full = jax.ShapeDtypeStruct((rows, width), F32)
    far = pl.BlockSpec(memory_space=pl.ANY)
    return pl.pallas_call(
        functools.partial(chain_forward_kernel, count, heads, len(got)),
        out_shape=(
            full,
            jax.ShapeDtypeStruct((2 * rows, width), LOW),
            full,
            full,
            jax.ShapeDtypeStruct((rows, width), LOW),
        ),
        in_specs=[scalars()] + [whole()] * (3 + len(got)) + [far] * (2 * count),
        out_specs=(whole(),) * 5,
        scratch_shapes=chain_scratch(kv, weights),
        compiler_params=params(mib=56),
        cost_estimate=lasts(6.5),
        name="chain_forward",
    )(flag, gain, dec, mine, *got, *kv, *weights)


def chain_backward_kernel(
    count, heads, got, flag_ref, gain_ref, dec_ref, state_ref, normed_ref, update_ref, gkv_ref, *refs
):
    mine_ref, got_refs = refs[0], refs[1 : 1 + got]
    far, refs = refs[1 + got : 1 + got + 2 * count], refs[1 + got + 2 * count :]
    next_ref, low_ref, pair_ref, small_ref = refs[:4]
    kv, w, copies = chain_loads(count, far + refs[4 : 4 + 2 * count], refs[4 + 2 * count])
    span = heads * HS
    dec = dec_ref[...]
    gain = gain_ref[...]
    carry = chosen(flag_ref, mine_ref, got_refs)
    rows = carry.shape[0]
    state = state_ref[...]
    small_ref[1:2, :] = jnp.sum(carry * (state - update_ref[...]), axis=0, keepdims=True)
    gup = ((1.0 - dec) * carry).astype(LOW)
    pair_ref[rows:, :] = gup
    normed = normed_ref[...]
    queries, gmixes = [], []
    for m in range(count):
        copies[m][0].wait()
        queries.append(mm(normed, w[m][:, :span], 1, 0).astype(LOW))
        gmixes.append(mm(gup, w[m][:, span:], 1, 0).astype(LOW))
    scores, grads = [], []
    for m in range(count):
        copies[m][1].wait()
        for h in range(heads):
            at = slice(h * HS, (h + 1) * HS)
            scores.append(mm(head_keys(kv[m], h), queries[m][:, at], 1, 1) * SCALE)
            grads.append(mm(head_values(kv[m], heads, h), gmixes[m][:, at], 1, 1))
    lows = []
    for score, grad in zip(scores, grads, strict=True):
        weights = column_softmax(score)
        inner = jnp.sum(grad * weights, axis=0, keepdims=True)
        lows.append((weights * (grad - inner)).astype(LOW))
    grad_normed = gkv_ref[...]
    grad_queries = [
        stacked([mm(head_keys(kv[m], h), lows[m * heads + h], 0, 0) * SCALE for h in range(heads)])
        for m in range(count)
    ]
    for m in range(count):
        grad_normed = grad_normed + mm(grad_queries[m].T.astype(LOW), w[m][:, :span], 1, 1)
    r = rms_scale(state)
    unit = state * r
    scaled = grad_normed * gain
    small_ref[0:1, :] = jnp.sum(grad_normed * unit, axis=0, keepdims=True)
    carry = dec * carry + r * (scaled - unit * jnp.mean(scaled * unit, axis=-1, keepdims=True))
    next_ref[...] = carry
    low_ref[...] = carry.astype(LOW)
    pair_ref[:rows, :] = ((1.0 - dec) * carry).astype(LOW)


def chain_backward(flag, mine, got, gain, dec, state, normed, update, gkv, kv, weights):
    count = len(kv)
    rows, width = state.shape
    heads = kv[0].shape[1] // (2 * HS)
    far = pl.BlockSpec(memory_space=pl.ANY)
    return pl.pallas_call(
        functools.partial(chain_backward_kernel, count, heads, len(got)),
        out_shape=(
            jax.ShapeDtypeStruct((rows, width), F32),
            jax.ShapeDtypeStruct((rows, width), LOW),
            jax.ShapeDtypeStruct((2 * rows, width), LOW),
            jax.ShapeDtypeStruct((2, width), F32),
        ),
        in_specs=[scalars()] + [whole()] * (7 + len(got)) + [far] * (2 * count),
        out_specs=(whole(),) * 4,
        scratch_shapes=chain_scratch(kv, weights),
        compiler_params=params(mib=56),
        cost_estimate=lasts(8.3),
        name="chain_backward",
    )(flag, gain, dec, state, normed, update, gkv, mine, *got, *kv, *weights)


def bucket_tile():
    lane = lax.broadcasted_iota(jnp.int32, (8, DIAG), 1)
    row = lax.broadcasted_iota(jnp.int32, (8, DIAG), 0)
    diff = lane - row
    diff = jnp.where(diff < 0, diff + DIAG, diff)
    offset = jnp.where(diff < BLK, diff, diff - DIAG) + BLK
    distance = jnp.abs(offset)
    far = jnp.full((8, DIAG), 8, jnp.int32)
    for edge in EDGES:
        far = far + (distance >= edge).astype(jnp.int32)
    near = jnp.where(distance < 8, distance, far)
    return jnp.where(offset >= 0, near, near + NBUCKET // 2)


def fill_bias(table_ref, h, bias_ref):
    bucket = bucket_tile()
    base = jnp.zeros((8, DIAG), F32)
    for k in range(NBUCKET):
        base = jnp.where(bucket == k, table_ref[h, k], base)
    for r in range(16):
        rolled = pltpu.roll(base, 8 * r, 1) if r else base
        wide = jnp.concatenate([rolled, rolled[:, :BLK]], axis=1)
        for k in range(2 * BLK // 128):
            start = (DIAG - 128 * k) % DIAG
            row = 8 * (16 * k + r)
            bias_ref[row : row + 8, :] = wide[:, start : start + BLK]


def collapse_bias(grad_ref, out_ref):
    total = jnp.zeros((8, DIAG), F32)
    for r in range(16):
        acc = [jnp.zeros((8, 128), F32)] * (DIAG // 128)
        for k in range(2 * BLK // 128):
            row = 8 * (16 * k + r)
            for c in range(BLK // 128):
                at = (c - k) % (DIAG // 128)
                acc[at] = acc[at] + grad_ref[row : row + 8, c * 128 : (c + 1) * 128]
        acc = jnp.concatenate(acc, axis=1)
        total = total + (pltpu.roll(acc, DIAG - 8 * r, 1) if r else acc)
    bucket = bucket_tile()
    lane = lax.broadcasted_iota(jnp.int32, (8, HS), 1)
    out = jnp.zeros((8, HS), F32)
    for k in range(NBUCKET):
        out = jnp.where(lane == k, jnp.sum(jnp.where(bucket == k, total, 0.0)), out)
    out_ref[...] = out


def current_mask(ids_col_ref, ids_row_ref):
    key = lax.broadcasted_iota(jnp.int32, (BLK, BLK), 0)
    query = lax.broadcasted_iota(jnp.int32, (BLK, BLK), 1)
    ids_row = ids_row_ref[...]
    return (key <= query) | ((ids_col_ref[...] == ids_row) & (ids_row > 0))


def attend_kernel(
    run_ref, table_ref, q_ref, kc_ref, vc_ref, kp_ref, vp_ref, ko_ref, vo_ref, ks_ref, vs_ref,
    row_ref, col_ref, out_ref, lse_ref, bias_ref, score_ref,
):
    h = pl.program_id(0)
    b = pl.program_id(1)

    @pl.when(b == 0)
    def _():
        fill_bias(table_ref, h, bias_ref)

    q = q_ref[...]
    first = b == 0
    keys = (
        ks_ref[...].reshape(BLK, HS),
        jnp.where(first, ko_ref[...], kp_ref[...]),
        kc_ref[...],
    )
    values = (
        vs_ref[...].reshape(BLK, HS),
        jnp.where(first, vo_ref[...], vp_ref[...]),
        vc_ref[...],
    )
    prior_ok = (run_ref[0] > 0) | (b > 0)
    score = mm(keys[0], q, 1, 1) * SCALE
    score_ref[0] = score
    peak = jnp.max(score, axis=0, keepdims=True)
    score = mm(keys[1], q, 1, 1) * SCALE + bias_ref[:BLK]
    score = jnp.where(prior_ok, score, -1e30)
    score_ref[1] = score
    peak = jnp.maximum(peak, jnp.max(score, axis=0, keepdims=True))
    score = mm(keys[2], q, 1, 1) * SCALE + bias_ref[BLK:]
    score = jnp.where(current_mask(col_ref, row_ref), score, -1e30)
    score_ref[2] = score
    peak = jnp.maximum(peak, jnp.max(score, axis=0, keepdims=True))
    total = jnp.zeros((1, BLK), F32)
    for c in range(3):
        exponent = jnp.exp(score_ref[c] - peak)
        score_ref[c] = exponent
        total = total + jnp.sum(exponent, axis=0, keepdims=True)
    inverse = 1.0 / total
    mixed = jnp.zeros((HS, BLK), F32)
    for c in range(3):
        mixed = mixed + mm(values[c], (score_ref[c] * inverse).astype(LOW), 0, 0)
    out_ref[...] = mixed.T.astype(LOW)
    lse_ref[...] = peak + jnp.log(total)


def attend_specs(heads, pieces, part, blocks):
    def at(col):
        return pl.BlockSpec((BLK, HS), lambda h, b: (b, col(h)))

    def before(col):
        return pl.BlockSpec((BLK, HS), lambda h, b: (jnp.maximum(b - 1, 0), col(h)))

    def outer(col):
        return pl.BlockSpec((BLK, HS), lambda h, b: (0, col(h)))

    def state(col):
        return pl.BlockSpec((pieces, None, part, HS), lambda h, b: (0, b, 0, col(h)))

    key, value = (lambda h: h), (lambda h: heads + h)
    return [
        scalars(),
        scalars(),
        at(key),
        at(key),
        at(value),
        before(key),
        before(value),
        outer(key),
        outer(value),
        state(lambda h: 2 * h),
        state(lambda h: 2 * h + 1),
        pl.BlockSpec((None, 1, BLK), lambda h, b: (b, 0, 0)),
        pl.BlockSpec((None, BLK, 1), lambda h, b: (b, 0, 0)),
    ]


def attend(run, table, q, kv, outer, sproj, ids_row, ids_col):
    rows = q.shape[0]
    heads = q.shape[1] // HS
    pieces, blocks, part, _ = sproj.shape
    return pl.pallas_call(
        attend_kernel,
        grid=(heads, blocks),
        out_shape=(
            jax.ShapeDtypeStruct((rows, heads * HS), LOW),
            jax.ShapeDtypeStruct((heads, blocks, 1, BLK), F32),
        ),
        in_specs=attend_specs(heads, pieces, part, blocks),
        out_specs=(
            pl.BlockSpec((BLK, HS), lambda h, b: (b, h)),
            pl.BlockSpec((None, None, 1, BLK), lambda h, b: (h, b, 0, 0)),
        ),
        scratch_shapes=[pltpu.VMEM((2 * BLK, BLK), F32), pltpu.VMEM((3, BLK, BLK), F32)],
        compiler_params=params(2, 20),
        cost_estimate=lasts(9.7),
        name="attend",
    )(run, table, q, kv, kv, kv, kv, outer, outer, sproj, sproj, ids_row, ids_col)


def attend_back_kernel(
    run_ref, table_ref, q_ref, kc_ref, vc_ref, kp_ref, vp_ref, ko_ref, vo_ref, ks_ref, vs_ref,
    row_ref, col_ref, gmix_ref, lse_ref,
    gq_ref, gcur_ref, gprev_ref, gs_ref, gtab_ref,
    bias_ref, gbias_ref, prob_ref, gprob_ref,
):
    h = pl.program_id(0)
    b = pl.program_id(1)

    @pl.when(b == 0)
    def _():
        fill_bias(table_ref, h, bias_ref)
        gbias_ref[...] = jnp.zeros_like(gbias_ref)

    q = q_ref[...]
    gmix = gmix_ref[...]
    lse = lse_ref[...]
    first = b == 0
    keys = (
        ks_ref[...].reshape(BLK, HS),
        jnp.where(first, ko_ref[...], kp_ref[...]),
        kc_ref[...],
    )
    values = (
        vs_ref[...].reshape(BLK, HS),
        jnp.where(first, vo_ref[...], vp_ref[...]),
        vc_ref[...],
    )
    prior_ok = (run_ref[0] > 0) | (b > 0)
    inner = jnp.zeros((1, BLK), F32)
    grad_values = []
    for c in range(3):
        score = mm(keys[c], q, 1, 1) * SCALE
        if c == 1:
            score = jnp.where(prior_ok, score + bias_ref[:BLK], -1e30)
        if c == 2:
            score = jnp.where(current_mask(col_ref, row_ref), score + bias_ref[BLK:], -1e30)
        prob = jnp.exp(score - lse)
        prob_ref[c] = prob
        grad_values.append(mm(prob.astype(LOW), gmix, 1, 0))
        grad_prob = mm(values[c], gmix, 1, 1)
        gprob_ref[c] = grad_prob
        inner = inner + jnp.sum(prob * grad_prob, axis=0, keepdims=True)
    grad_q = jnp.zeros((HS, BLK), F32)
    grad_keys = []
    for c in range(3):
        grad_score = (prob_ref[c] * (gprob_ref[c] - inner)).astype(LOW)
        if c > 0:
            gbias_ref[(c - 1) * BLK : c * BLK, :] += grad_score.astype(F32)
        grad_keys.append(mm(grad_score, q, 1, 0) * SCALE)
        grad_q = grad_q + mm(keys[c], grad_score, 0, 0)
    gq_ref[...] = (grad_q * SCALE).T.astype(LOW)
    part = gs_ref.shape[0], gs_ref.shape[1], HS
    gs_ref[:, :, :HS] = grad_keys[0].astype(LOW).reshape(part)
    gs_ref[:, :, HS:] = grad_values[0].astype(LOW).reshape(part)
    gprev_ref[:, :HS] = grad_keys[1].astype(LOW)
    gprev_ref[:, HS:] = grad_values[1].astype(LOW)
    gcur_ref[:, :HS] = grad_keys[2].astype(LOW)
    gcur_ref[:, HS:] = grad_values[2].astype(LOW)

    @pl.when(b == pl.num_programs(1) - 1)
    def _():
        collapse_bias(gbias_ref, gtab_ref)


def attend_back(run, table, q, kv, outer, sproj, ids_row, ids_col, gmix, lse):
    rows = q.shape[0]
    heads = q.shape[1] // HS
    pieces, blocks, part, _ = sproj.shape

    def at():
        return pl.BlockSpec((BLK, HS), lambda h, b: (b, h))

    side = jax.ShapeDtypeStruct((rows, heads * 2 * HS), LOW)
    pair = pl.BlockSpec((BLK, 2 * HS), lambda h, b: (b, h))
    return pl.pallas_call(
        attend_back_kernel,
        grid=(heads, blocks),
        out_shape=(
            jax.ShapeDtypeStruct((rows, heads * HS), LOW),
            side,
            side,
            jax.ShapeDtypeStruct((pieces, blocks, part, heads * 2 * HS), LOW),
            jax.ShapeDtypeStruct((heads, 8, HS), F32),
        ),
        in_specs=attend_specs(heads, pieces, part, blocks)
        + [at(), pl.BlockSpec((None, None, 1, BLK), lambda h, b: (h, b, 0, 0))],
        out_specs=(
            at(),
            pair,
            pair,
            pl.BlockSpec((pieces, None, part, 2 * HS), lambda h, b: (0, b, 0, h)),
            pl.BlockSpec((None, 8, HS), lambda h, b: (h, 0, 0)),
        ),
        scratch_shapes=[
            pltpu.VMEM((2 * BLK, BLK), F32),
            pltpu.VMEM((2 * BLK, BLK), F32),
            pltpu.VMEM((3, BLK, BLK), F32),
            pltpu.VMEM((3, BLK, BLK), F32),
        ],
        compiler_params=params(2, 56),
        cost_estimate=lasts(16),
        name="attend_back",
    )(run, table, q, kv, kv, kv, kv, outer, outer, sproj, sproj, ids_row, ids_col, gmix, lse)


def state_back_kernel(
    sq_ref, k_ref, v_ref, gmix_ref, gcur_ref, gnext_ref, gouter_ref,
    gkv_ref, gsq_ref, smix_ref,
):
    b = pl.program_id(1)
    last = b == pl.num_programs(1) - 1
    pieces, part = sq_ref.shape[0], sq_ref.shape[1]
    sq = sq_ref[...].reshape(BLK, HS)
    gmix = gmix_ref[...].reshape(BLK, HS)
    k, v = k_ref[...], v_ref[...]
    weights = column_softmax(mm(k, sq, 1, 1) * SCALE)
    low = weights.astype(LOW)
    grad_w = mm(v, gmix, 1, 1)
    inner = jnp.sum(grad_w * weights, axis=0, keepdims=True)
    grad_s = (weights * (grad_w - inner)).astype(LOW)
    grad_k = mm(grad_s, sq, 1, 0) * SCALE
    grad_v = mm(low, gmix, 1, 0)
    grad_q = mm(k, grad_s, 0, 0) * SCALE
    smix = mm(v, low, 0, 0)
    rest = gcur_ref[...].astype(F32) + jnp.where(last, gouter_ref[...], gnext_ref[...]).astype(F32)
    gkv_ref[:, :HS] = (rest[:, :HS] + grad_k).astype(LOW)
    gkv_ref[:, HS:] = (rest[:, HS:] + grad_v).astype(LOW)
    gsq_ref[...] = grad_q.T.astype(LOW).reshape(pieces, part, HS)
    smix_ref[...] = smix.T.astype(LOW).reshape(pieces, part, HS)


def state_back(sq, kv, gmix, gcur, gprev, outer):
    rows = gcur.shape[0]
    heads = gcur.shape[1] // (2 * HS)
    pieces, blocks, part, _ = sq.shape

    def at(col=lambda h: h):
        return pl.BlockSpec((BLK, HS), lambda h, b: (b, col(h)))

    def state():
        return pl.BlockSpec((pieces, None, part, HS), lambda h, b: (0, b, 0, h))

    side = jax.ShapeDtypeStruct((pieces, blocks, part, heads * HS), LOW)
    return pl.pallas_call(
        state_back_kernel,
        grid=(heads, blocks),
        out_shape=(jax.ShapeDtypeStruct((rows, heads * 2 * HS), LOW), side, side),
        in_specs=[
            state(),
            at(),
            at(lambda h: heads + h),
            state(),
            pl.BlockSpec((BLK, 2 * HS), lambda h, b: (b, h)),
            pl.BlockSpec((BLK, 2 * HS), lambda h, b: (jnp.minimum(b + 1, blocks - 1), h)),
            pl.BlockSpec((BLK, 2 * HS), lambda h, b: (0, h)),
        ],
        out_specs=(
            pl.BlockSpec((BLK, 2 * HS), lambda h, b: (b, h)),
            state(),
            state(),
        ),
        compiler_params=params(2, 16),
        cost_estimate=lasts(6.5),
        name="state_back",
    )(sq, kv, kv, gmix, gcur, gprev, outer)


def passed_along(array, axis, by):
    size = lax.axis_size(axis)
    pairs = [(i, i + by) for i in range(size) if 0 <= i + by < size]
    return lax.ppermute(array, axis, pairs)


def swap(array, axis, bits):
    return lax.ppermute(array, axis, [(i, i ^ bits) for i in range(lax.axis_size(axis))])


def gather_rel(array, filler=None):
    size = lax.axis_size("tensor")
    pieces = []
    for m in range(0, size, 2):
        piece = array if m == 0 else swap(array, "tensor", m)
        if m and filler is not None:
            piece = after(piece, filler)
        pieces += [piece, swap(piece, "tensor", 1)]
    return pieces


def reduce_first(even, odd):
    got = swap(odd, "tensor", 1)
    return [even[j].astype(F32) + got[j].astype(F32) for j in range(even.shape[0])]


def reduce_last(sums, filler=None):
    terms = [sums[0]]
    for j, send in enumerate(sums[1:], 1):
        term = swap(send, "tensor", 2 * j)
        terms.append(term if filler is None else after(term, filler))
    return terms


def lower(sums):
    return [sums[0]] + [term.astype(LOW) for term in sums[1:]]


def exchange_rel(parts):
    return [part if m == 0 else swap(part, "tensor", m) for m, part in enumerate(parts)]


def cut(array, me):
    size = lax.axis_size("tensor")
    rows = array.shape[0] // size
    return [lax.dynamic_slice_in_dim(array, (me ^ m) * rows, rows, 0) for m in range(size)]


def place(pieces, me):
    rows = pieces[0].shape[0]
    out = jnp.zeros((rows * len(pieces),) + pieces[0].shape[1:], pieces[0].dtype)
    for m, piece in enumerate(pieces):
        out = lax.dynamic_update_slice_in_dim(out, piece, (me ^ m) * rows, 0)
    return out


def sum_all(array):
    for axis in ("tensor", "context", "shard"):
        bits = 1
        while bits < lax.axis_size(axis):
            array = array + swap(array, axis, bits)
            bits *= 2
    return array


def rms_back(v, gain, grad):
    r = rms_scale(v)
    unit = v * r
    scaled = grad * gain
    return r * (scaled - unit * jnp.mean(scaled * unit, axis=-1, keepdims=True))


def dot(a, b, ca, cb):
    return lax.dot_general(a, b, (((ca,), (cb,)), ((), ())), preferred_element_type=F32)


def after(array, *others):
    return lax.optimization_barrier((array,) + others)[0]


def half_rows(local, run):
    part = local.shape[0] // 2
    return lax.dynamic_slice_in_dim(local, run * part, part, 0)


def shard_pieces(array):
    return [array if s == 0 else swap(array, "shard", s) for s in range(lax.axis_size("shard"))]


def scatter_rows(grad):
    return lax.psum_scatter(grad, "shard", scatter_dimension=0, tiled=True)


def shards(
    tokens,
    piece_ids,
    tok_qkv,
    state_qkv,
    tok_out,
    state_out,
    mlp_in,
    mlp_out,
    rel_bias,
    init_state,
    norm_gains,
    decay_param,
    cotangent,
):
    size = lax.axis_size("tensor")
    shard_count = lax.axis_size("shard")
    me = lax.axis_index("tensor")
    shard_pos = lax.axis_index("shard")
    run_pos = lax.axis_index("context")
    run_count = lax.axis_size("context")
    me_arr = me.astype(jnp.int32)[None]
    run_arr = run_pos.astype(jnp.int32)[None]
    pos = jnp.stack([shard_pos, run_pos]).astype(jnp.int32)
    own = tokens[0]
    own_rows, width = own.shape
    rows = own_rows * size
    blocks = rows // BLK
    heads = tok_qkv.shape[1]
    part = init_state.shape[0]
    span = heads * HS

    cols = norm_gains.shape[1]
    bias_rows = rel_bias.shape[0]
    slot_size = NBUCKET * heads
    small = jnp.zeros((SMALL, width), LOW)
    small = lax.dynamic_update_slice(
        small, jnp.concatenate([norm_gains, decay_param[None]], 0), (0, (shard_pos * size + me) * cols)
    )
    small = lax.dynamic_update_slice(
        small, rel_bias.reshape(1, -1), (4, me * slot_size + shard_pos * bias_rows * heads)
    )

    local_chain = jnp.concatenate(
        [state_qkv[:, :, :HS].reshape(-1, span), state_out.reshape(span, -1).T, init_state.T], axis=1
    )
    chain_pieces = shard_pieces(half_rows(local_chain, run_pos))
    local_tok = after(tok_qkv.reshape(-1, heads * 384), *chain_pieces)
    w_tok = lax.all_gather(local_tok, "shard", axis=0, tiled=True)
    token_pieces = gather_rel(jnp.concatenate([own, small], axis=0), chain_pieces[-1])
    chain_other = swap(after(jnp.stack(chain_pieces), token_pieces[-2]), "context", 1)
    chain_own, start = assemble(pos, chain_pieces, chain_other, (2 * span, part))
    chip_own = swap(chain_own, "tensor", 1)
    small = sum(piece[own_rows:].astype(F32) for piece in token_pieces).astype(LOW)
    small_pieces = shard_pieces(after(small, chip_own))
    start = start.astype(F32).T
    small_pieces = [after(piece, start) for piece in small_pieces]
    w_sq, w_sout = (chain_own, span, 0), (chain_own, span, 1)

    chain_w = [chain_own, chip_own] + gather_rel(chain_own)[2:]

    local_side = jnp.concatenate(
        [state_qkv[:, :, HS:].reshape(-1, 2 * span), tok_out.reshape(span, -1).T], axis=1
    )
    local_mlp = jnp.concatenate([mlp_in, mlp_out.T], axis=1)

    q, normed_a, vectors, wq_tok, wkv_tok, kv, *kv_blocks = token_proj(
        me_arr, token_pieces, small_pieces, after(w_tok, *chain_w[2::2]), blocks
    )
    w_side = lax.all_gather(after(local_side, q), "shard", axis=0, tiled=True)
    w_skv, w_tout = (w_side, 2 * span, 0), w_side[:, 2 * span :]
    gains = vectors[:3]
    decay = jax.nn.sigmoid(vectors[3:4])
    table = lax.dynamic_slice_in_dim(vectors[4], me * slot_size, slot_size, 0)
    table = table.reshape(NBUCKET, heads).T
    kv_pieces = [gather_rel(kv_blocks[0])]
    outer = passed_along(kv_blocks[-1], "context", 1)

    w_mlp = lax.all_gather(after(local_mlp, kv_pieces[0][-2]), "shard", axis=0, tiled=True)

    gain_s = gains[2:3]
    got = []
    for round_index in range(run_count):
        state = start
        states, normeds, updates = [], [], []
        for b in range(blocks):
            if b == len(kv_pieces):
                kv_pieces.append(gather_rel(after(kv_blocks[b], *kv_pieces[-1]), state))
                state = after(state, outer)
            state, pair, update, following, low = chain_forward(
                run_arr, state, got if b == 0 else [], gain_s, decay, kv_pieces[b], chain_w
            )
            states.append(state)
            normeds.append(pair)
            updates.append(update)
            state = following
        if round_index + 1 < run_count:
            got = [passed_along(low, "context", 1)]
            if round_index == 0:
                grad_pieces = gather_rel(after(cotangent[0], *kv_pieces[-1]))
                tout_pieces = gather_rel(after(w_tout, *grad_pieces))
    units = mlp_in.shape[1]
    w_in, w_out = (w_mlp, units, 0), (w_mlp, units, 1)
    normed_s = stacked([pair for pair in normeds[::2]])[: blocks * part]
    state_pieces = gather_rel(normed_s, updates[-1])
    sq, skv = proj(state_pieces, [w_sq, w_skv])
    sq = sq.reshape(size, blocks, part, span)
    skv = skv.reshape(size, blocks, part, 2 * span)

    ids_row = piece_ids.reshape(blocks, 1, BLK)
    ids_col = piece_ids.reshape(blocks, BLK, 1)
    mixed, lse = attend(run_arr, table, q, kv, outer, skv, ids_row, ids_col)
    mixed_parts = cut(mixed, me)
    residual, normed_m, squares = branch_out(own, gains[1:2], exchange_rel(mixed_parts), tout_pieces)

    (grad_hidden,) = proj([after(piece, normed_m) for piece in grad_pieces], [w_out])
    mlp_pieces = gather_rel(normed_m, grad_hidden)
    hidden, grad_pre, even, odd = feed(w_in, grad_hidden, mlp_pieces)
    sums = lower(reduce_first(even, odd))
    grad_w_mlp = weight_grad([(mlp_pieces, after(grad_pre, *sums)), (grad_pieces, hidden)])
    terms = reduce_last(sums, grad_w_mlp)

    grad_res, grad_branch, grad_gain_m, *gmix_parts = branch_back(
        cotangent[0], residual, gains[1:2], terms, tout_pieces
    )
    mlp_mine = scatter_rows(after(grad_w_mlp, grad_branch))
    gmix = place(exchange_rel(gmix_parts), me)
    gq, gcur, gprev, gs, gtab = attend_back(
        run_arr, table, q, kv, outer, skv, ids_row, ids_col, gmix, lse
    )
    branch_pieces = gather_rel(after(grad_branch, gmix), gq)
    gs = after(gs, branch_pieces[-2])
    outer_back = passed_along(gprev[:BLK], "context", -1)

    gs = gs.reshape(-1, 2 * span)
    zero_arr = jnp.zeros((1,), jnp.int32)
    even, odd = back(zero_arr, [gs], [w_skv])
    sums = lower(reduce_first(even, odd))
    even, odd = back(zero_arr, [after(hidden, *sums)], [w_out])
    grad_state_kv = sum(term.astype(F32) for term in reduce_last(sums, even))
    grad_state_kv = after(grad_state_kv, outer_back).reshape(blocks, part, width)
    sums = lower(reduce_first(even, odd))
    branch_m = reduce_last([after(term, grad_state_kv) for term in sums])

    got = []
    not_last = (run_pos != run_count - 1).astype(jnp.int32)[None]
    for round_index in range(run_count):
        carry = jnp.zeros_like(start)
        gups = [None] * blocks
        chain_small = jnp.zeros((2, width), F32)
        for b in reversed(range(blocks)):
            carry, low, pair, row_sums = chain_backward(
                not_last, carry, got if b == blocks - 1 else [], gain_s, decay, states[b],
                normed_s[b * part : (b + 1) * part], updates[b], grad_state_kv[b], kv_pieces[b], chain_w,
            )
            chain_small = chain_small + row_sums
            gups[b] = pair
            if b and round_index:
                carry = after(carry, mlp_got[0])
        if round_index + 1 < run_count:
            got = [passed_along(low, "context", -1)]
            if round_index == 0:
                grad_w_early = weight_grad(
                    [
                        ([normed_a], after(gq, carry)),
                        (state_pieces, gs),
                        (branch_pieces, jnp.concatenate(mixed_parts, axis=0)),
                    ]
                )
                got = came = [after(got[0], grad_w_early, mlp_mine, *branch_m)]
                mlp_halves = [
                    after(mlp_mine[:, i * units : (i + 1) * units], *came) for i in range(2)
                ]
                mlp_got = [swap(mlp_halves[0], "context", 1)]
                mlp_got.append(swap(after(mlp_halves[1], mlp_got[0]), "context", 1))
    gup_all = stacked([gups[b] for b in range(blocks - 1, 0, -2)][::-1])
    grad_start = jnp.where(run_pos == 0, carry, 0.0).astype(LOW)
    branch_m = sum(term.astype(F32) for term in branch_m)
    output = (residual + branch_m).astype(LOW)
    gup_pieces = gather_rel(gup_all, carry)
    early_mine = scatter_rows(after(grad_w_early, mlp_mine, *came))
    early_got = swap(after(early_mine, *mlp_got), "context", 1)
    (gsmix,) = proj([after(gup_pieces[0], *mlp_got)] + gup_pieces[1:], [w_sout])
    gsmix = gsmix.reshape(size, blocks, part, span)
    gkv, gsq, smix = state_back(sq, kv, gsmix, gcur, gprev, outer_back)
    grad_w_late = weight_grad(
        [([normed_a], gkv), (state_pieces, gsq.reshape(-1, span)), (gup_pieces, smix.reshape(-1, span))]
    )
    late_mine = scatter_rows(jnp.concatenate([after(grad_w_late, early_mine), grad_start.T], axis=1))
    g_in, g_out = (
        half.astype(F32) + other.astype(F32) for half, other in zip(mlp_halves, mlp_got, strict=True)
    )
    g_early = early_mine.astype(F32) + early_got.astype(F32)
    g_late = late_mine.astype(F32) + swap(late_mine, "context", 1).astype(F32)

    even, odd, gain_sums = back(
        me_arr, [gq, after(gkv, grad_w_late)], [(wq_tok, span, 0), (wkv_tok, 2 * span, 0)], normed_a
    )
    grad_gain_a = (gain_sums / gains[0:1])[0]
    inputs = own.astype(F32)
    terms = reduce_last(lower(reduce_first(even, odd)))
    grad_normed_a = sum(term.astype(F32) for term in terms)
    grad_tokens = (grad_res + rms_back(inputs, gains[0], grad_normed_a)).astype(LOW)

    def by_head(array):
        return array.reshape(array.shape[0], heads, -1)

    g_tok = jnp.concatenate([by_head(g_early[:, :span]), by_head(g_late[:, : 2 * span])], axis=2)
    g_state = jnp.concatenate(
        [by_head(g_late[:, 2 * span : 3 * span]), by_head(g_early[:, span : 3 * span])], axis=2
    )
    g_tout = g_early[:, 3 * span :].T.reshape(heads, HS, -1)
    g_sout = g_late[:, 3 * span : 4 * span].T.reshape(heads, HS, -1)

    squares = jnp.concatenate([jnp.sum(squares, axis=1), jnp.sum(branch_m * branch_m)[None]])
    slot = gtab[:, 0, :NBUCKET].reshape(-1)
    slots = lax.dynamic_update_slice_in_dim(
        jnp.zeros((size * slot.size,), F32), slot, me * slot.size, 0
    )
    tail = jnp.concatenate([slots, squares])
    tail = jnp.pad(tail, (0, width - tail.size))
    grad_decay = chain_small[1] * (decay * (1.0 - decay))[0]
    sums = sum_all(
        after(jnp.stack([grad_gain_a, grad_gain_m[0], chain_small[0], grad_decay, tail]), early_got, *terms)
    )
    place_at = (shard_pos * size + me) * cols
    mine = lax.dynamic_slice_in_dim(sums[:4], place_at, cols, 1)
    table_sum = lax.dynamic_slice_in_dim(sums[4], me * slot.size, slot.size, 0)
    table_sum = table_sum.reshape(heads, NBUCKET).T
    g_table = lax.dynamic_slice_in_dim(table_sum, shard_pos * bias_rows, bias_rows, 0)
    entries = own.size * shard_count * run_count * size
    first = size * slot.size
    rms_out = jnp.sqrt(sums[4, first : first + 3] / entries)

    return (
        output[None],
        grad_tokens[None],
        g_tok,
        g_state,
        g_tout,
        g_sout,
        g_in,
        g_out.T,
        g_table,
        g_late[:, 4 * span :].T,
        mine[:3],
        mine[3],
        rms_out,
    )


def solution(mesh):
    return jax.shard_map(
        shards,
        mesh=mesh,
        in_specs=(
            P("shard", ("context", "tensor"), None),
            P("shard", "context"),
            P("shard", "tensor", None),
            P("shard", "tensor", None),
            P("tensor", None, "shard"),
            P("tensor", None, "shard"),
            P("shard", "tensor"),
            P("tensor", "shard"),
            P("shard", "tensor"),
            P("tensor", "shard"),
            P(None, ("shard", "tensor")),
            P(("shard", "tensor")),
            P("shard", ("context", "tensor"), None),
        ),
        out_specs=(
            P("shard", ("context", "tensor"), None),
            P("shard", ("context", "tensor"), None),
            P("shard", "tensor", None),
            P("shard", "tensor", None),
            P("tensor", None, "shard"),
            P("tensor", None, "shard"),
            P("shard", "tensor"),
            P("tensor", "shard"),
            P("shard", "tensor"),
            P("tensor", "shard"),
            P(None, ("shard", "tensor")),
            P(("shard", "tensor")),
            P(),
        ),
        check_vma=False,
    )
```

```python
import functools

import jax
import jax.numpy as jnp
from jax import lax
from jax.experimental import pallas as pl
from jax.experimental.pallas import tpu as pltpu
from jax.sharding import PartitionSpec as P

HS = 128
BLK = 512
NBUCKET = 32
EDGES = (12, 16, 23, 32, 46, 64, 91)
LOW = jnp.bfloat16
F32 = jnp.float32
SCALE = HS ** (-0.5)
EPS = 1e-06
DIAG = 3 * BLK
SMALL = 16
PACE = 0.5


def mm(a, b, ca, cb):
    return lax.dot_general(a, b, (((ca,), (cb,)), ((), ())), preferred_element_type=F32)


def whole():
    return pl.BlockSpec(memory_space=pltpu.VMEM)


def columns(weight):
    _, width, index = weight
    return pl.BlockSpec((weight[0].shape[0], width), lambda *_: (0, index))


def scalars():
    return pl.BlockSpec(memory_space=pltpu.SMEM)


def params(grid_rank=0, mib=40):
    limit = mib * 1024 * 1024
    if grid_rank:
        return pltpu.CompilerParams(
            dimension_semantics=("arbitrary",) * grid_rank, vmem_limit_bytes=limit
        )
    return pltpu.CompilerParams(vmem_limit_bytes=limit)


def lasts(microseconds):
    return pl.CostEstimate(
        flops=int(microseconds * PACE * 1.1e9), bytes_accessed=int(microseconds * PACE * 3e6), transcendentals=0
    )


def rms_scale(v):
    return lax.rsqrt(jnp.mean(v * v, axis=-1, keepdims=True) + EPS)


def assemble_kernel(count, pos_ref, *refs):
    pieces, other_ref, outs = refs[:count], refs[count], refs[count + 1 :]
    part = pieces[0].shape[0]
    for s in range(count):
        base = (pos_ref[0] ^ s) * (2 * part)
        mine = pl.multiple_of(base + pos_ref[1] * part, part)
        theirs = pl.multiple_of(base + (1 - pos_ref[1]) * part, part)
        first = 0
        for out_ref in outs:
            last = first + out_ref.shape[1]
            out_ref[pl.ds(mine, part), :] = pieces[s][:, first:last]
            out_ref[pl.ds(theirs, part), :] = other_ref[s, :, first:last]
            first = last


def assemble(pos, pieces, other, widths):
    part, cols = pieces[0].shape
    rows = 2 * part * len(pieces)
    return pl.pallas_call(
        functools.partial(assemble_kernel, len(pieces)),
        out_shape=tuple(jax.ShapeDtypeStruct((rows, w), LOW) for w in widths),
        in_specs=[scalars()] + [whole()] * (len(pieces) + 1),
        out_specs=(whole(),) * len(widths),
        compiler_params=params(mib=16),
        cost_estimate=lasts(1.5),
        name="assemble",
    )(pos, *pieces, other)


def weight_grad_kernel(counts, extras, *refs):
    out_ref = refs[-1]
    at = 0
    first = 0
    for count in counts:
        right = refs[at + count]
        total = None
        row = 0
        for left in refs[at : at + count]:
            term = mm(left[...], right[row : row + left.shape[0], :], 0, 0)
            row += left.shape[0]
            total = term if total is None else total + term
        out_ref[:, first : first + right.shape[1]] = total.astype(LOW)
        first += right.shape[1]
        at += count + 1
    for extra in refs[at : at + extras]:
        out_ref[:, first : first + extra.shape[1]] = extra[...]
        first += extra.shape[1]


def weight_grad(pairs, extras=()):
    width = pairs[0][0][0].shape[1]
    tile = 256
    specs, args = [], []
    for lefts, right in pairs:
        specs += [pl.BlockSpec((left.shape[0], tile), lambda i: (0, i)) for left in lefts]
        specs.append(pl.BlockSpec(right.shape, lambda i: (0, 0)))
        args += list(lefts) + [right]
    specs += [pl.BlockSpec((tile, extra.shape[1]), lambda i: (i, 0)) for extra in extras]
    cols = sum(right.shape[1] for _, right in pairs) + sum(extra.shape[1] for extra in extras)
    return pl.pallas_call(
        functools.partial(weight_grad_kernel, [len(lefts) for lefts, _ in pairs], len(extras)),
        grid=(width // tile,),
        out_shape=jax.ShapeDtypeStruct((width, cols), LOW),
        in_specs=specs,
        out_specs=pl.BlockSpec((tile, cols), lambda i: (i, 0)),
        compiler_params=params(1, 20),
        cost_estimate=lasts(6),
        name="weight_grad",
    )(*args, *extras)


def token_proj_kernel(count, shards, blocks, me_ref, w_ref, *refs):
    pieces, small = refs[:count], refs[count : count + shards]
    q_ref, normed_ref, vec_ref, kv_ref, *kv_refs = refs[count + shards :]
    span = q_ref.shape[1]
    vectors = small[0][...].astype(F32)
    for piece in small[1:]:
        vectors = vectors + piece[...].astype(F32)
    vec_ref[...] = vectors
    gain = vectors[0:1]
    rows = pieces[0].shape[0] - SMALL
    for m in range(count):
        start = pl.multiple_of((me_ref[0] ^ m) * rows, rows)
        v = pieces[m][:rows, :].astype(F32)
        normed = (v * rms_scale(v) * gain).astype(LOW)
        normed_ref[pl.ds(start, rows), :] = normed
        kv_ref[pl.ds(start, rows), :] = mm(normed, w_ref[:, : 2 * span], 1, 0).astype(LOW)
        q_ref[pl.ds(start, rows), :] = mm(normed, w_ref[:, 2 * span :], 1, 0).astype(LOW)
    for b in range(blocks):
        kv_refs[b][...] = kv_ref[b * BLK : (b + 1) * BLK, :]


def token_proj(me, pieces, small, weight, blocks):
    width, cols = weight.shape
    span = cols // 3
    step = pieces[0].shape[0]
    rows = (step - SMALL) * len(pieces)
    return pl.pallas_call(
        functools.partial(token_proj_kernel, len(pieces), len(small), blocks),
        out_shape=(
            jax.ShapeDtypeStruct((rows, span), LOW),
            jax.ShapeDtypeStruct((rows, width), LOW),
            jax.ShapeDtypeStruct((SMALL, width), F32),
            jax.ShapeDtypeStruct((rows, 2 * span), LOW),
        )
        + (jax.ShapeDtypeStruct((BLK, 2 * span), LOW),) * blocks,
        in_specs=[scalars(), whole()] + [whole()] * (len(pieces) + len(small)),
        out_specs=(whole(),) * (4 + blocks),
        compiler_params=params(mib=56),
        cost_estimate=lasts(5),
        name="token_proj",
    )(me, weight, *pieces, *small)


def proj_kernel(count, weights, *refs):
    pieces, ws, outs = refs[:count], refs[count : count + weights], refs[count + weights :]
    rows = pieces[0].shape[0]
    for m in range(count):
        for w, out in zip(ws, outs, strict=True):
            out[m * rows : (m + 1) * rows, :] = mm(pieces[m][...], w[...], 1, 0).astype(LOW)


def proj(pieces, weights, mib=24):
    rows = pieces[0].shape[0] * len(pieces)
    return pl.pallas_call(
        functools.partial(proj_kernel, len(pieces), len(weights)),
        grid=(1,),
        out_shape=tuple(jax.ShapeDtypeStruct((rows, w[1]), LOW) for w in weights),
        in_specs=[whole()] * len(pieces) + [columns(w) for w in weights],
        out_specs=(whole(),) * len(weights),
        compiler_params=params(1, mib),
        cost_estimate=lasts(3),
        name="proj",
    )(*pieces, *[w[0] for w in weights])


def back_kernel(count, gained, size, me_ref, *refs):
    outs = refs[2 * count + gained : 2 * count + gained + size]
    total = None
    for i in range(count):
        term = mm(refs[i][...], refs[count + i][...], 1, 1)
        total = term if total is None else total + term
    step = pl.program_id(0)
    if gained:
        sums = jnp.sum(total * refs[2 * count][...].astype(F32), axis=0, keepdims=True)
        refs[-1][...] = sums + jnp.where(step == 0, 0.0, refs[-1][...])
    total = total.astype(LOW)
    for m in range(size):

        @pl.when(step == m)
        def _(m=m):
            outs[m][...] = total


def back(me, grads, weights, normed=None):
    rows, width = grads[0].shape[0], weights[0][0].shape[0]
    size = lax.axis_size("tensor")
    tile = rows // size
    extra = [] if normed is None else [normed]
    grid_spec = pltpu.PrefetchScalarGridSpec(
        num_scalar_prefetch=1,
        grid=(size,),
        in_specs=[pl.BlockSpec((tile, g.shape[1]), lambda i, me_ref: (i ^ me_ref[0], 0)) for g in grads]
        + [columns(w) for w in weights]
        + [pl.BlockSpec((tile, width), lambda i, me_ref: (i ^ me_ref[0], 0)) for _ in extra],
        out_specs=(pl.BlockSpec((tile, width), lambda i, me_ref: (0, 0)),) * size
        + (pl.BlockSpec((1, width), lambda i, me_ref: (0, 0)),) * len(extra),
    )
    return pl.pallas_call(
        functools.partial(back_kernel, len(grads), len(extra), size),
        grid_spec=grid_spec,
        out_shape=(jax.ShapeDtypeStruct((tile, width), LOW),) * size
        + (jax.ShapeDtypeStruct((1, width), F32),) * len(extra),
        compiler_params=params(1, 24),
        cost_estimate=lasts(3),
        name="back",
    )(me, *grads, *[w[0] for w in weights], *extra)


def branch_kernel(count, own_ref, gain_ref, *refs):
    parts, weights = refs[:count], refs[count : 2 * count]
    residual_ref, normed_ref, sums_ref = refs[2 * count :]
    branch = None
    for part, weight in zip(parts, weights, strict=True):
        term = mm(part[...], weight[...], 1, 1)
        branch = term if branch is None else branch + term
    own = own_ref[...].astype(F32)
    residual = own + branch
    residual_ref[...] = residual
    normed_ref[...] = (residual * rms_scale(residual) * gain_ref[...]).astype(LOW)
    sums_ref[0:1, :] = jnp.sum(own * own, axis=0, keepdims=True)
    sums_ref[1:2, :] = jnp.sum(branch * branch, axis=0, keepdims=True)


def branch_out(own, gain, parts, weights):
    rows, width = own.shape
    return pl.pallas_call(
        functools.partial(branch_kernel, len(parts)),
        out_shape=(
            jax.ShapeDtypeStruct((rows, width), F32),
            jax.ShapeDtypeStruct((rows, width), LOW),
            jax.ShapeDtypeStruct((2, width), F32),
        ),
        in_specs=[whole()] * (2 + 2 * len(parts)),
        out_specs=(whole(),) * 3,
        compiler_params=params(mib=12),
        cost_estimate=lasts(3),
        name="branch_out",
    )(own, gain, *parts, *weights)


def branch_back_kernel(count, sums, cot_ref, residual_ref, gain_ref, *refs):
    terms, weights, outs = refs[:sums], refs[sums : sums + count], refs[sums + count :]
    grad_ref, low_ref, gain_sum_ref, parts = outs[0], outs[1], outs[2], outs[3:]
    grad = terms[0][...].astype(F32)
    for term in terms[1:]:
        grad = grad + term[...].astype(F32)
    residual = residual_ref[...]
    r = rms_scale(residual)
    unit = residual * r
    gain_sum_ref[...] = jnp.sum(grad * unit, axis=0, keepdims=True)
    scaled = grad * gain_ref[...]
    grad = cot_ref[...].astype(F32) + r * (
        scaled - unit * jnp.mean(scaled * unit, axis=-1, keepdims=True)
    )
    grad_ref[...] = grad
    low = grad.astype(LOW)
    low_ref[...] = low
    for part, weight in zip(parts, weights, strict=True):
        part[...] = mm(low, weight[...], 1, 0).astype(LOW)


def branch_back(cot, residual, gain, terms, weights):
    rows, width = cot.shape
    span = weights[0].shape[1]
    return pl.pallas_call(
        functools.partial(branch_back_kernel, len(weights), len(terms)),
        out_shape=(
            jax.ShapeDtypeStruct((rows, width), F32),
            jax.ShapeDtypeStruct((rows, width), LOW),
            jax.ShapeDtypeStruct((1, width), F32),
        )
        + (jax.ShapeDtypeStruct((rows, span), LOW),) * len(weights),
        in_specs=[whole()] * (3 + len(terms) + len(weights)),
        out_specs=(whole(),) * (3 + len(weights)),
        compiler_params=params(mib=56),
        cost_estimate=lasts(2.5),
        name="branch_back",
    )(cot, residual, gain, *terms, *weights)


def gelu_parts(pre):
    half = 0.5 * (1.0 + lax.erf(pre * 0.7071067811865476))
    density = jnp.exp(pre * pre * -0.5) * 0.3989422804014327
    return half, density


def feed_kernel(count, w_ref, ghid_ref, *refs):
    pieces, (hidden_ref, gpre_ref), outs = refs[:count], refs[count : count + 2], refs[count + 2 :]
    rows = pieces[0].shape[0]
    for m in range(count):
        at = slice(m * rows, (m + 1) * rows)
        pre = mm(pieces[m][...], w_ref[...], 1, 0)
        half, density = gelu_parts(pre)
        hidden_ref[at, :] = (pre * half).astype(LOW)
        gpre = ((half + pre * density) * ghid_ref[at, :].astype(F32)).astype(LOW)
        gpre_ref[at, :] = gpre
        outs[m][...] = mm(gpre, w_ref[...], 1, 1).astype(LOW)


def feed(w_in, ghid, pieces):
    width, units = w_in[0].shape[0], w_in[1]
    own, count = pieces[0].shape[0], len(pieces)
    rows = own * count
    return pl.pallas_call(
        functools.partial(feed_kernel, count),
        grid=(1,),
        out_shape=(
            jax.ShapeDtypeStruct((rows, units), LOW),
            jax.ShapeDtypeStruct((rows, units), LOW),
        )
        + (jax.ShapeDtypeStruct((own, width), LOW),) * count,
        in_specs=[columns(w_in)] + [whole()] * (1 + count),
        out_specs=(whole(),) * (2 + count),
        compiler_params=params(1, 32),
        cost_estimate=lasts(7),
        name="feed",
    )(w_in[0], ghid, *pieces)


def column_softmax(scores):
    peak = jnp.max(scores, axis=0, keepdims=True)
    exponent = jnp.exp(scores - peak)
    return exponent * (1.0 / jnp.sum(exponent, axis=0, keepdims=True))


def chain_operands(count, brought, refs):
    kv, w = refs[:count], refs[count : 2 * count]
    if not brought:
        return kv, w, [(), ()] * count
    here, sems = refs[2 * count : 4 * count], refs[4 * count]
    copies = []
    for m in range(count):
        copies.append((pltpu.make_async_copy(w[m], here[count + m], sems.at[m]),))
        copies.append((pltpu.make_async_copy(kv[m], here[m], sems.at[count + m]),))
    for (copy,) in copies:
        copy.start()
    return here[:count], here[count:], copies


def chain_specs(kv, weights, brought):
    if not brought:
        return [whole()] * (2 * len(kv)), [], 24
    scratch = [pltpu.VMEM(array.shape, LOW) for array in list(kv) + list(weights)]
    scratch.append(pltpu.SemaphoreType.DMA((2 * len(kv),)))
    return [pl.BlockSpec(memory_space=pl.ANY)] * (2 * len(kv)), scratch, 56


def ready(copies):
    for copy in copies:
        copy.wait()


def chosen(flag_ref, mine_ref, got_ref):
    return jnp.where(flag_ref[0] != 0, got_ref[...].astype(F32), mine_ref[...])


def head_keys(kv, h):
    return kv[:, 2 * h * HS : (2 * h + 1) * HS]


def head_values(kv, h):
    return kv[:, (2 * h + 1) * HS : 2 * (h + 1) * HS]


def stacked(parts):
    return parts[0] if len(parts) == 1 else jnp.concatenate(parts, axis=0)


def chain_forward_kernel(
    count, heads, brought, flag_ref, gain_ref, dec_ref, mine_ref, got_ref, *refs
):
    outs = refs[2 * count : 2 * count + 5]
    state_ref, pair_ref, update_ref, next_ref, low_ref = outs
    kv, w, copies = chain_operands(count, brought, refs[: 2 * count] + refs[2 * count + 5 :])
    span = heads * HS
    dec = dec_ref[...]
    gain = gain_ref[...]
    state = chosen(flag_ref, mine_ref, got_ref)
    rows = state.shape[0]
    state_ref[...] = state
    normed = (state * rms_scale(state) * gain).astype(LOW)
    pair_ref[:rows, :] = normed
    queries = []
    for m in range(count):
        ready(copies[2 * m])
        queries.append(mm(normed, w[m][:, :span], 1, 0).astype(LOW))
    scores = []
    for m in range(count):
        ready(copies[2 * m + 1])
        for h in range(heads):
            scores.append(mm(head_keys(kv[m], h), queries[m][:, h * HS : (h + 1) * HS], 1, 1) * SCALE)
    weights = [column_softmax(score).astype(LOW) for score in scores]
    mixed = [
        stacked([mm(head_values(kv[m], h), weights[m * heads + h], 0, 0) for h in range(heads)])
        for m in range(count)
    ]
    update = None
    for m in range(count):
        term = mm(mixed[m].T.astype(LOW), w[m][:, span:], 1, 1)
        update = term if update is None else update + term
    update_ref[...] = update
    state = dec * state + (1.0 - dec) * update
    next_ref[...] = state
    low_ref[...] = state.astype(LOW)
    pair_ref[rows:, :] = (state * rms_scale(state) * gain).astype(LOW)


def chain_forward(flag, mine, got, gain, dec, kv, weights, brought):
    count = len(kv)
    rows, width = mine.shape
    heads = kv[0].shape[1] // (2 * HS)
    full = jax.ShapeDtypeStruct((rows, width), F32)
    specs, scratch, mib = chain_specs(kv, weights, brought)
    return pl.pallas_call(
        functools.partial(chain_forward_kernel, count, heads, brought),
        out_shape=(
            full,
            jax.ShapeDtypeStruct((2 * rows, width), LOW),
            full,
            full,
            jax.ShapeDtypeStruct((rows, width), LOW),
        ),
        in_specs=[scalars()] + [whole()] * 4 + specs,
        out_specs=(whole(),) * 5,
        scratch_shapes=scratch,
        compiler_params=params(mib=mib),
        cost_estimate=lasts(6.5),
        name="chain_forward",
    )(flag, gain, dec, mine, got, *kv, *weights)


def chain_backward_kernel(
    count, heads, terms, brought, flag_ref, gain_ref, dec_ref, state_ref, normed_ref, update_ref, mine_ref,
    got_ref, *refs
):
    gkv, refs = refs[:terms], refs[terms:]
    next_ref, low_ref, pair_ref, small_ref = refs[2 * count : 2 * count + 4]
    kv, w, copies = chain_operands(count, brought, refs[: 2 * count] + refs[2 * count + 4 :])
    span = heads * HS
    dec = dec_ref[...]
    gain = gain_ref[...]
    carry = chosen(flag_ref, mine_ref, got_ref)
    rows = carry.shape[0]
    state = state_ref[...]
    small_ref[1:2, :] = jnp.sum(carry * (state - update_ref[...]), axis=0, keepdims=True)
    gup = ((1.0 - dec) * carry).astype(LOW)
    pair_ref[rows:, :] = gup
    normed = normed_ref[...]
    queries, gmixes = [], []
    for m in range(count):
        ready(copies[2 * m])
        queries.append(mm(normed, w[m][:, :span], 1, 0).astype(LOW))
        gmixes.append(mm(gup, w[m][:, span:], 1, 0).astype(LOW))
    scores, grads = [], []
    for m in range(count):
        ready(copies[2 * m + 1])
        for h in range(heads):
            at = slice(h * HS, (h + 1) * HS)
            scores.append(mm(head_keys(kv[m], h), queries[m][:, at], 1, 1) * SCALE)
            grads.append(mm(head_values(kv[m], h), gmixes[m][:, at], 1, 1))
    lows = []
    for score, grad in zip(scores, grads, strict=True):
        weights = column_softmax(score)
        inner = jnp.sum(grad * weights, axis=0, keepdims=True)
        lows.append((weights * (grad - inner)).astype(LOW))
    grad_normed = gkv[0][...].astype(F32)
    for term in gkv[1:]:
        grad_normed = grad_normed + term[...].astype(F32)
    grad_queries = [
        stacked([mm(head_keys(kv[m], h), lows[m * heads + h], 0, 0) * SCALE for h in range(heads)])
        for m in range(count)
    ]
    for m in range(count):
        grad_normed = grad_normed + mm(grad_queries[m].T.astype(LOW), w[m][:, :span], 1, 1)
    r = rms_scale(state)
    unit = state * r
    scaled = grad_normed * gain
    small_ref[0:1, :] = jnp.sum(grad_normed * unit, axis=0, keepdims=True)
    carry = dec * carry + r * (scaled - unit * jnp.mean(scaled * unit, axis=-1, keepdims=True))
    next_ref[...] = carry
    low_ref[...] = carry.astype(LOW)
    pair_ref[:rows, :] = ((1.0 - dec) * carry).astype(LOW)


def chain_backward(flag, mine, got, gain, dec, state, normed, update, b, gkv, kv, weights, brought):
    count = len(kv)
    rows, width = state.shape
    heads = kv[0].shape[1] // (2 * HS)
    specs, scratch, mib = chain_specs(kv, weights, brought)
    return pl.pallas_call(
        functools.partial(chain_backward_kernel, count, heads, len(gkv), brought),
        grid=(1,),
        out_shape=(
            jax.ShapeDtypeStruct((rows, width), F32),
            jax.ShapeDtypeStruct((rows, width), LOW),
            jax.ShapeDtypeStruct((2 * rows, width), LOW),
            jax.ShapeDtypeStruct((2, width), F32),
        ),
        in_specs=[scalars()]
        + [whole()] * 3
        + [pl.BlockSpec((rows, width), lambda i: (b, 0))]
        + [whole()] * 3
        + [pl.BlockSpec((rows, width), lambda i: (b, 0)) for _ in gkv]
        + specs,
        out_specs=(whole(),) * 4,
        scratch_shapes=scratch,
        compiler_params=params(1, mib),
        cost_estimate=lasts(8.3),
        name="chain_backward",
    )(flag, gain, dec, state, normed, update, mine, got, *gkv, *kv, *weights)


def bucket_tile():
    lane = lax.broadcasted_iota(jnp.int32, (8, DIAG), 1)
    row = lax.broadcasted_iota(jnp.int32, (8, DIAG), 0)
    diff = lane - row
    diff = jnp.where(diff < 0, diff + DIAG, diff)
    offset = jnp.where(diff < BLK, diff, diff - DIAG) + BLK
    distance = jnp.abs(offset)
    far = jnp.full((8, DIAG), 8, jnp.int32)
    for edge in EDGES:
        far = far + (distance >= edge).astype(jnp.int32)
    near = jnp.where(distance < 8, distance, far)
    return jnp.where(offset >= 0, near, near + NBUCKET // 2)


def fill_bias(table_ref, h, bias_ref):
    bucket = bucket_tile()
    base = jnp.zeros((8, DIAG), F32)
    for k in range(NBUCKET):
        base = jnp.where(bucket == k, table_ref[h, k], base)
    for r in range(16):
        rolled = pltpu.roll(base, 8 * r, 1) if r else base
        wide = jnp.concatenate([rolled, rolled[:, :BLK]], axis=1)
        for k in range(2 * BLK // 128):
            start = (DIAG - 128 * k) % DIAG
            row = 8 * (16 * k + r)
            bias_ref[row : row + 8, :] = wide[:, start : start + BLK]


def collapse_bias(grad_ref, out_ref):
    total = jnp.zeros((8, DIAG), F32)
    for r in range(16):
        acc = [jnp.zeros((8, 128), F32)] * (DIAG // 128)
        for k in range(2 * BLK // 128):
            row = 8 * (16 * k + r)
            for c in range(BLK // 128):
                at = (c - k) % (DIAG // 128)
                acc[at] = acc[at] + grad_ref[row : row + 8, c * 128 : (c + 1) * 128]
        acc = jnp.concatenate(acc, axis=1)
        total = total + (pltpu.roll(acc, DIAG - 8 * r, 1) if r else acc)
    bucket = bucket_tile()
    lane = lax.broadcasted_iota(jnp.int32, (8, HS), 1)
    out = jnp.zeros((8, HS), F32)
    for k in range(NBUCKET):
        out = jnp.where(lane == k, jnp.sum(jnp.where(bucket == k, total, 0.0)), out)
    out_ref[...] = out


def current_mask(ids_ref):
    key = lax.broadcasted_iota(jnp.int32, (BLK, BLK), 0)
    query = lax.broadcasted_iota(jnp.int32, (BLK, BLK), 1)
    ids = ids_ref[...].astype(F32)
    column = jnp.broadcast_to(ids, (HS, BLK)).T[:, :1]
    return (key <= query) | ((column == ids) & (ids > 0.0))


def attend_kernel(
    run_ref, table_ref, q_ref, kc_ref, vc_ref, kp_ref, vp_ref, ko_ref, vo_ref, ks_ref, vs_ref,
    row_ref, out_ref, lse_ref, bias_ref, score_ref,
):
    h = pl.program_id(0)
    b = pl.program_id(1)

    @pl.when(b == 0)
    def _():
        fill_bias(table_ref, h, bias_ref)

    q = q_ref[...]
    first = b == 0
    keys = (
        ks_ref[...].reshape(BLK, HS),
        jnp.where(first, ko_ref[...], kp_ref[...]),
        kc_ref[...],
    )
    values = (
        vs_ref[...].reshape(BLK, HS),
        jnp.where(first, vo_ref[...], vp_ref[...]),
        vc_ref[...],
    )
    prior_ok = (run_ref[0] > 0) | (b > 0)
    score = mm(keys[0], q, 1, 1) * SCALE
    score_ref[0] = score
    peak = jnp.max(score, axis=0, keepdims=True)
    score = mm(keys[1], q, 1, 1) * SCALE + bias_ref[:BLK]
    score = jnp.where(prior_ok, score, -1e30)
    score_ref[1] = score
    peak = jnp.maximum(peak, jnp.max(score, axis=0, keepdims=True))
    score = mm(keys[2], q, 1, 1) * SCALE + bias_ref[BLK:]
    score = jnp.where(current_mask(row_ref), score, -1e30)
    score_ref[2] = score
    peak = jnp.maximum(peak, jnp.max(score, axis=0, keepdims=True))
    total = jnp.zeros((1, BLK), F32)
    for c in range(3):
        exponent = jnp.exp(score_ref[c] - peak)
        score_ref[c] = exponent
        total = total + jnp.sum(exponent, axis=0, keepdims=True)
    inverse = 1.0 / total
    mixed = jnp.zeros((HS, BLK), F32)
    for c in range(3):
        mixed = mixed + mm(values[c], (score_ref[c] * inverse).astype(LOW), 0, 0)
    out_ref[...] = mixed.T.astype(LOW)
    lse_ref[...] = peak + jnp.log(total)


def attend_specs(heads, pieces, part, blocks):
    def at(col):
        return pl.BlockSpec((BLK, HS), lambda h, b: (b, col(h)))

    def before(col):
        return pl.BlockSpec((BLK, HS), lambda h, b: (jnp.maximum(b - 1, 0), col(h)))

    def outer(col):
        return pl.BlockSpec((BLK, HS), lambda h, b: (0, col(h)))

    def state(col):
        return pl.BlockSpec((pieces, None, part, HS), lambda h, b: (0, b, 0, col(h)))

    key, value = (lambda h: 2 * h), (lambda h: 2 * h + 1)
    return [
        scalars(),
        scalars(),
        at(lambda h: h),
        at(key),
        at(value),
        before(key),
        before(value),
        outer(key),
        outer(value),
        state(lambda h: 2 * h),
        state(lambda h: 2 * h + 1),
        pl.BlockSpec((None, 1, BLK), lambda h, b: (b, 0, 0)),
    ]


def attend(run, table, q, kv, outer, sproj, ids_row):
    rows = q.shape[0]
    heads = q.shape[1] // HS
    pieces, blocks, part, _ = sproj.shape
    return pl.pallas_call(
        attend_kernel,
        grid=(heads, blocks),
        out_shape=(
            jax.ShapeDtypeStruct((rows, heads * HS), LOW),
            jax.ShapeDtypeStruct((heads, blocks, 1, BLK), F32),
        ),
        in_specs=attend_specs(heads, pieces, part, blocks),
        out_specs=(
            pl.BlockSpec((BLK, HS), lambda h, b: (b, h)),
            pl.BlockSpec((None, None, 1, BLK), lambda h, b: (h, b, 0, 0)),
        ),
        scratch_shapes=[pltpu.VMEM((2 * BLK, BLK), F32), pltpu.VMEM((3, BLK, BLK), F32)],
        compiler_params=params(2, 20),
        cost_estimate=lasts(9.7),
        name="attend",
    )(run, table, q, kv, kv, kv, kv, outer, outer, sproj, sproj, ids_row)


def attend_back_kernel(
    run_ref, table_ref, q_ref, kc_ref, vc_ref, kp_ref, vp_ref, ko_ref, vo_ref, ks_ref, vs_ref,
    row_ref, gmix_ref, lse_ref,
    gq_ref, gcur_ref, gprev_ref, gs_ref, gtab_ref,
    bias_ref, gbias_ref, prob_ref, gprob_ref,
):
    h = pl.program_id(0)
    b = pl.program_id(1)

    @pl.when(b == 0)
    def _():
        fill_bias(table_ref, h, bias_ref)
        gbias_ref[...] = jnp.zeros_like(gbias_ref)

    q = q_ref[...]
    gmix = gmix_ref[...]
    lse = lse_ref[...]
    first = b == 0
    keys = (
        ks_ref[...].reshape(BLK, HS),
        jnp.where(first, ko_ref[...], kp_ref[...]),
        kc_ref[...],
    )
    values = (
        vs_ref[...].reshape(BLK, HS),
        jnp.where(first, vo_ref[...], vp_ref[...]),
        vc_ref[...],
    )
    prior_ok = (run_ref[0] > 0) | (b > 0)
    inner = jnp.zeros((1, BLK), F32)
    grad_values = []
    for c in range(3):
        score = mm(keys[c], q, 1, 1) * SCALE
        if c == 1:
            score = jnp.where(prior_ok, score + bias_ref[:BLK], -1e30)
        if c == 2:
            score = jnp.where(current_mask(row_ref), score + bias_ref[BLK:], -1e30)
        prob = jnp.exp(score - lse)
        prob_ref[c] = prob
        grad_values.append(mm(prob.astype(LOW), gmix, 1, 0))
        grad_prob = mm(values[c], gmix, 1, 1)
        gprob_ref[c] = grad_prob
        inner = inner + jnp.sum(prob * grad_prob, axis=0, keepdims=True)
    grad_q = jnp.zeros((HS, BLK), F32)
    grad_keys = []
    for c in range(3):
        grad_score = (prob_ref[c] * (gprob_ref[c] - inner)).astype(LOW)
        if c > 0:
            gbias_ref[(c - 1) * BLK : c * BLK, :] += grad_score.astype(F32)
        grad_keys.append(mm(grad_score, q, 1, 0) * SCALE)
        grad_q = grad_q + mm(keys[c], grad_score, 0, 0)
    gq_ref[...] = (grad_q * SCALE).T.astype(LOW)
    part = gs_ref.shape[0], gs_ref.shape[1], HS
    gs_ref[:, :, :HS] = grad_keys[0].astype(LOW).reshape(part)
    gs_ref[:, :, HS:] = grad_values[0].astype(LOW).reshape(part)
    gprev_ref[:, :HS] = grad_keys[1].astype(LOW)
    gprev_ref[:, HS:] = grad_values[1].astype(LOW)
    gcur_ref[:, :HS] = grad_keys[2].astype(LOW)
    gcur_ref[:, HS:] = grad_values[2].astype(LOW)

    @pl.when(b == pl.num_programs(1) - 1)
    def _():
        collapse_bias(gbias_ref, gtab_ref)


def attend_back(run, table, q, kv, outer, sproj, ids_row, gmix, lse):
    rows = q.shape[0]
    heads = q.shape[1] // HS
    pieces, blocks, part, _ = sproj.shape

    def at():
        return pl.BlockSpec((BLK, HS), lambda h, b: (b, h))

    side = jax.ShapeDtypeStruct((rows, heads * 2 * HS), LOW)
    pair = pl.BlockSpec((BLK, 2 * HS), lambda h, b: (b, h))
    return pl.pallas_call(
        attend_back_kernel,
        grid=(heads, blocks),
        out_shape=(
            jax.ShapeDtypeStruct((rows, heads * HS), LOW),
            side,
            side,
            jax.ShapeDtypeStruct((pieces, blocks, part, heads * 2 * HS), LOW),
            jax.ShapeDtypeStruct((heads, 8, HS), F32),
        ),
        in_specs=attend_specs(heads, pieces, part, blocks)
        + [at(), pl.BlockSpec((None, None, 1, BLK), lambda h, b: (h, b, 0, 0))],
        out_specs=(
            at(),
            pair,
            pair,
            pl.BlockSpec((pieces, None, part, 2 * HS), lambda h, b: (0, b, 0, h)),
            pl.BlockSpec((None, 8, HS), lambda h, b: (h, 0, 0)),
        ),
        scratch_shapes=[
            pltpu.VMEM((2 * BLK, BLK), F32),
            pltpu.VMEM((2 * BLK, BLK), F32),
            pltpu.VMEM((3, BLK, BLK), F32),
            pltpu.VMEM((3, BLK, BLK), F32),
        ],
        compiler_params=params(2, 56),
        cost_estimate=lasts(16),
        name="attend_back",
    )(run, table, q, kv, kv, kv, kv, outer, outer, sproj, sproj, ids_row, gmix, lse)


def state_back_kernel(
    sq_ref, k_ref, v_ref, gmix_ref, gcur_ref, gnext_ref, gouter_ref,
    gkv_ref, gsq_ref, smix_ref,
):
    b = pl.program_id(1)
    last = b == pl.num_programs(1) - 1
    pieces, part = sq_ref.shape[0], sq_ref.shape[1]
    sq = sq_ref[...].reshape(BLK, HS)
    gmix = gmix_ref[...].reshape(BLK, HS)
    k, v = k_ref[...], v_ref[...]
    weights = column_softmax(mm(k, sq, 1, 1) * SCALE)
    low = weights.astype(LOW)
    grad_w = mm(v, gmix, 1, 1)
    inner = jnp.sum(grad_w * weights, axis=0, keepdims=True)
    grad_s = (weights * (grad_w - inner)).astype(LOW)
    grad_k = mm(grad_s, sq, 1, 0) * SCALE
    grad_v = mm(low, gmix, 1, 0)
    grad_q = mm(k, grad_s, 0, 0) * SCALE
    smix = mm(v, low, 0, 0)
    rest = gcur_ref[...].astype(F32) + jnp.where(last, gouter_ref[...], gnext_ref[...]).astype(F32)
    gkv_ref[:, :HS] = (rest[:, :HS] + grad_k).astype(LOW)
    gkv_ref[:, HS:] = (rest[:, HS:] + grad_v).astype(LOW)
    gsq_ref[...] = grad_q.T.astype(LOW).reshape(pieces, part, HS)
    smix_ref[...] = smix.T.astype(LOW).reshape(pieces, part, HS)


def state_back(sq, kv, gmix, gcur, gprev, outer):
    rows = gcur.shape[0]
    heads = gcur.shape[1] // (2 * HS)
    pieces, blocks, part, _ = sq.shape

    def at(col=lambda h: h):
        return pl.BlockSpec((BLK, HS), lambda h, b: (b, col(h)))

    def state():
        return pl.BlockSpec((pieces, None, part, HS), lambda h, b: (0, b, 0, h))

    side = jax.ShapeDtypeStruct((pieces, blocks, part, heads * HS), LOW)
    return pl.pallas_call(
        state_back_kernel,
        grid=(heads, blocks),
        out_shape=(jax.ShapeDtypeStruct((rows, heads * 2 * HS), LOW), side, side),
        in_specs=[
            state(),
            at(lambda h: 2 * h),
            at(lambda h: 2 * h + 1),
            state(),
            pl.BlockSpec((BLK, 2 * HS), lambda h, b: (b, h)),
            pl.BlockSpec((BLK, 2 * HS), lambda h, b: (jnp.minimum(b + 1, blocks - 1), h)),
            pl.BlockSpec((BLK, 2 * HS), lambda h, b: (0, h)),
        ],
        out_specs=(
            pl.BlockSpec((BLK, 2 * HS), lambda h, b: (b, h)),
            state(),
            state(),
        ),
        compiler_params=params(2, 16),
        cost_estimate=lasts(6.5),
        name="state_back",
    )(sq, kv, kv, gmix, gcur, gprev, outer)


def passed_along(array, axis, by):
    size = lax.axis_size(axis)
    pairs = [(i, i + by) for i in range(size) if 0 <= i + by < size]
    return lax.ppermute(array, axis, pairs)


def swap(array, axis, bits):
    return lax.ppermute(array, axis, [(i, i ^ bits) for i in range(lax.axis_size(axis))])


def far_pieces(array):
    return [array] + [swap(array, "tensor", m) for m in range(2, lax.axis_size("tensor"), 2)]


def chip_pieces(pieces, *fillers):
    out = []
    for j, piece in enumerate(pieces):
        if j and fillers:
            piece = after(piece, *fillers)
        out += [piece, swap(piece, "tensor", 1)]
    return out


def gather_rel(array, *fillers):
    return chip_pieces(far_pieces(array), *fillers)


def reduce_first(parts):
    size = len(parts)
    got = [swap(parts[m + 1], "tensor", 1) for m in range(0, size, 2)]
    sends = [
        (parts[m].astype(F32) + got[m // 2].astype(F32)).astype(LOW) for m in range(2, size, 2)
    ]
    return [parts[0], got[0]], sends


def reduce_last(own, sends, filler=None):
    terms = list(own)
    for j, send in enumerate(sends, 1):
        term = swap(send, "tensor", 2 * j)
        terms.append(term if filler is None else after(term, filler))
    return terms


def added(terms):
    return sum(term.astype(F32) for term in terms)


def exchange_rel(parts):
    return [part if m == 0 else swap(part, "tensor", m) for m, part in enumerate(parts)]


def cut(array, me):
    size = lax.axis_size("tensor")
    rows = array.shape[0] // size
    return [lax.dynamic_slice_in_dim(array, (me ^ m) * rows, rows, 0) for m in range(size)]


def place(pieces, me):
    rows = pieces[0].shape[0]
    out = jnp.zeros((rows * len(pieces),) + pieces[0].shape[1:], pieces[0].dtype)
    for m, piece in enumerate(pieces):
        out = lax.dynamic_update_slice_in_dim(out, piece, (me ^ m) * rows, 0)
    return out


def sum_all(array):
    for axis in ("tensor", "context", "shard"):
        bits = 1
        while bits < lax.axis_size(axis):
            array = array + swap(array, axis, bits)
            bits *= 2
    return array


def rms_back(v, gain, grad):
    r = rms_scale(v)
    unit = v * r
    scaled = grad * gain
    return r * (scaled - unit * jnp.mean(scaled * unit, axis=-1, keepdims=True))


def dot(a, b, ca, cb):
    return lax.dot_general(a, b, (((ca,), (cb,)), ((), ())), preferred_element_type=F32)


def after(array, *others):
    return lax.optimization_barrier((array,) + others)[0]


def half_rows(local, run):
    part = local.shape[0] // 2
    return lax.dynamic_slice_in_dim(local, run * part, part, 0)


def shard_pieces(array):
    return [array if s == 0 else swap(array, "shard", s) for s in range(lax.axis_size("shard"))]


def scatter_rows(grad):
    return lax.psum_scatter(grad, "shard", scatter_dimension=0, tiled=True)


def shards(
    tokens,
    piece_ids,
    tok_qkv,
    state_qkv,
    tok_out,
    state_out,
    mlp_in,
    mlp_out,
    rel_bias,
    init_state,
    norm_gains,
    decay_param,
    cotangent,
):
    size = lax.axis_size("tensor")
    shard_count = lax.axis_size("shard")
    me = lax.axis_index("tensor")
    shard_pos = lax.axis_index("shard")
    run_pos = lax.axis_index("context")
    run_count = lax.axis_size("context")
    me_arr = me.astype(jnp.int32)[None]
    run_arr = run_pos.astype(jnp.int32)[None]
    pos = jnp.stack([shard_pos, run_pos]).astype(jnp.int32)
    own = tokens[0]
    own_rows, width = own.shape
    rows = own_rows * size
    blocks = rows // BLK
    heads = tok_qkv.shape[1]
    part = init_state.shape[0]
    span = heads * HS

    cols = norm_gains.shape[1]
    bias_rows = rel_bias.shape[0]
    slot_size = NBUCKET * heads
    small = jnp.zeros((SMALL, width), LOW)
    small = lax.dynamic_update_slice(
        small, jnp.concatenate([norm_gains, decay_param[None]], 0), (0, (shard_pos * size + me) * cols)
    )
    small = lax.dynamic_update_slice(
        small, rel_bias.reshape(1, -1), (4, me * slot_size + shard_pos * bias_rows * heads)
    )

    local_chain = jnp.concatenate(
        [state_qkv[:, :, :HS].reshape(-1, span), state_out.reshape(span, -1).T, init_state.T], axis=1
    )
    chain_pieces = shard_pieces(half_rows(local_chain, run_pos))
    local_tok = jnp.concatenate(
        [tok_qkv[:, :, HS:].reshape(-1, 2 * span), tok_qkv[:, :, :HS].reshape(-1, span)], axis=1
    )
    token_far = far_pieces(jnp.concatenate([own, small], axis=0))
    local_tok = after(local_tok, *token_far[1:], *chain_pieces)
    w_tok = lax.all_gather(local_tok, "shard", axis=0, tiled=True)
    token_pieces = chip_pieces(token_far, *chain_pieces)
    chain_other = swap(jnp.stack(chain_pieces), "context", 1)
    chain_own, start = assemble(pos, chain_pieces, chain_other, (2 * span, part))
    chip_own = swap(chain_own, "tensor", 1)
    small = sum(piece[own_rows:].astype(F32) for piece in token_pieces).astype(LOW)
    small_pieces = shard_pieces(after(small, chip_own))
    start = start.astype(F32).T
    small_pieces = [after(piece, start) for piece in small_pieces]
    w_sq, w_sout = (chain_own, span, 0), (chain_own, span, 1)

    chain_w = [chain_own, chip_own] + gather_rel(chain_own)[2:]

    local_side = jnp.concatenate(
        [state_qkv[:, :, HS:].reshape(-1, 2 * span), tok_out.reshape(span, -1).T], axis=1
    )
    local_mlp = jnp.concatenate([mlp_in, mlp_out.T], axis=1)

    w_side = lax.all_gather(after(local_side, chain_own), "shard", axis=0, tiled=True)
    w_skv, w_tout = (w_side, 2 * span, 0), w_side[:, 2 * span :]

    q, normed_a, vectors, kv, *kv_blocks = token_proj(
        me_arr, token_pieces, small_pieces, after(w_tok, *chain_w[2::2]), blocks
    )
    gains = vectors[:3]
    decay = jax.nn.sigmoid(vectors[3:4])
    table = lax.dynamic_slice_in_dim(vectors[4], me * slot_size, slot_size, 0)
    table = table.reshape(NBUCKET, heads).T
    kv_pieces = [gather_rel(kv_blocks[0])]

    w_mlp = lax.all_gather(after(local_mlp, q), "shard", axis=0, tiled=True)

    ids_row = piece_ids.reshape(blocks, 1, BLK)
    zero_arr = jnp.zeros((1,), jnp.int32)
    gain_s = gains[2:3]
    got, flag = jnp.zeros((part, width), LOW), zero_arr
    for round_index in range(run_count):
        state = start
        states, normeds, updates = [], [], []
        for b in range(blocks):
            if b == len(kv_pieces):
                kv_pieces.append(gather_rel(after(kv_blocks[b], *kv_pieces[-1][2::2]), state))
            if round_index + b == run_count:
                state = after(state, outer, *tout_far)
            state, pair, update, following, low = chain_forward(
                zero_arr if b else flag, state, got, gain_s, decay, kv_pieces[b], chain_w,
                round_index > 0,
            )
            if round_index + b == 0:
                outer = passed_along(after(kv_blocks[-1], low), "context", 1)
            states.append(state)
            normeds.append(pair)
            updates.append(update)
            state = following
        if round_index + 1 < run_count:
            got, flag = passed_along(low, "context", 1), run_arr
            if round_index == 0:
                grad_far = far_pieces(after(cotangent[0], *kv_pieces[-1][2::2]))
                tout_far = far_pieces(after(w_tout, *grad_far))
                got = after(got, *grad_far)
    units = mlp_in.shape[1]
    w_in, w_out = (w_mlp, units, 0), (w_mlp, units, 1)
    normed_s = stacked([pair for pair in normeds[::2]])[: blocks * part]
    state_pieces = gather_rel(normed_s, updates[-1])
    sq, skv = proj(state_pieces, [w_sq, w_skv])
    sq = sq.reshape(size, blocks, part, span)
    skv = skv.reshape(size, blocks, part, 2 * span)

    mixed, lse = attend(run_arr, table, q, kv, outer, skv, ids_row)
    grad_pieces = chip_pieces(grad_far, mixed)
    tout_pieces = chip_pieces(tout_far, mixed)
    mixed_parts = cut(mixed, me)
    residual, normed_m, squares = branch_out(own, gains[1:2], exchange_rel(mixed_parts), tout_pieces)

    (grad_hidden,) = proj([after(piece, normed_m) for piece in grad_pieces], [w_out])
    mlp_pieces = gather_rel(normed_m, grad_hidden)
    hidden, grad_pre, *parts = feed(w_in, grad_hidden, mlp_pieces)
    sums, sends = reduce_first(parts)
    grad_w_mlp = weight_grad([(mlp_pieces, after(grad_pre, *sends)), (grad_pieces, hidden)])
    terms = reduce_last(sums, sends, grad_w_mlp)

    grad_res, grad_branch, grad_gain_m, *gmix_parts = branch_back(
        cotangent[0], residual, gains[1:2], terms, tout_pieces
    )
    mlp_mine = scatter_rows(after(grad_w_mlp, grad_branch))
    gmix = place(exchange_rel(gmix_parts), me)
    gq, gcur, gprev, gs, gtab = attend_back(
        run_arr, table, q, kv, outer, skv, ids_row, gmix, lse
    )
    branch_pieces = gather_rel(after(grad_branch, gmix), gq)
    gs = after(gs, branch_pieces[-2])
    outer_back = passed_along(gprev[:BLK], "context", -1)

    gs = gs.reshape(-1, 2 * span)
    sums, sends = reduce_first(back(zero_arr, [gs], [w_skv]))
    parts = back(zero_arr, [after(hidden, *sends)], [w_out])
    state_terms = reduce_last(sums, sends, parts[0])
    state_terms[0] = after(state_terms[0], outer_back)
    sums, sends = reduce_first(parts)
    branch_m = reduce_last(sums, [after(send, *state_terms) for send in sends])

    got, flag = jnp.zeros((part, width), LOW), zero_arr
    not_last = (run_pos != run_count - 1).astype(jnp.int32)[None]
    for round_index in range(run_count):
        carry = jnp.zeros_like(start)
        gups = [None] * blocks
        chain_small = jnp.zeros((2, width), F32)
        for b in reversed(range(blocks)):
            carry, low, pair, row_sums = chain_backward(
                flag if b == blocks - 1 else zero_arr, carry, got, gain_s, decay, states[b], normed_s,
                updates[b], b, state_terms, kv_pieces[b], chain_w, round_index > 0,
            )
            chain_small = chain_small + row_sums
            gups[b] = pair
        if round_index + 1 < run_count:
            got, flag = passed_along(low, "context", -1), not_last
            if round_index == 0:
                grad_w_early = weight_grad(
                    [
                        ([normed_a], after(gq, carry)),
                        (state_pieces, gs),
                        (branch_pieces, jnp.concatenate(mixed_parts, axis=0)),
                    ]
                )
                got = came = after(got, grad_w_early, *branch_m)
    gup_all = stacked([gups[b] for b in range(blocks - 1, 0, -2)][::-1])
    grad_start = jnp.where(run_pos == 0, carry, 0.0).astype(LOW)
    branch_m = added(branch_m)
    output = (residual + branch_m).astype(LOW)
    mlp_halves = [after(mlp_mine[:, i * units : (i + 1) * units], gup_all) for i in range(2)]
    mlp_got = [swap(mlp_halves[0], "context", 1)]
    mlp_got.append(swap(after(mlp_halves[1], mlp_got[0]), "context", 1))
    gup_pieces = gather_rel(gup_all, carry, mlp_got[0])
    early_mine = scatter_rows(after(grad_w_early, mlp_mine, came))
    early_got = swap(after(early_mine, *mlp_got), "context", 1)
    (gsmix,) = proj(gup_pieces, [w_sout])
    gsmix = gsmix.reshape(size, blocks, part, span)
    gkv, gsq, smix = state_back(after(sq, mlp_got[1]), kv, gsmix, gcur, gprev, outer_back)
    grad_w_late = weight_grad(
        [([normed_a], gkv), (state_pieces, gsq.reshape(-1, span)), (gup_pieces, smix.reshape(-1, span))],
        [grad_start.T],
    )
    late_mine = scatter_rows(after(grad_w_late, early_mine))
    g_in, g_out = (
        half.astype(F32) + other.astype(F32) for half, other in zip(mlp_halves, mlp_got, strict=True)
    )
    g_early = early_mine.astype(F32) + early_got.astype(F32)
    g_late = late_mine.astype(F32) + swap(late_mine, "context", 1).astype(F32)

    *parts, gain_sums = back(
        me_arr,
        [gq, after(gkv, grad_w_late, early_got)],
        [(w_tok, span, 2), (w_tok, 2 * span, 0)],
        normed_a,
    )
    grad_gain_a = (gain_sums / gains[0:1])[0]
    inputs = own.astype(F32)
    grad_normed_a = added(reduce_last(*reduce_first(parts)))
    grad_tokens = (grad_res + rms_back(inputs, gains[0], grad_normed_a)).astype(LOW)

    def by_head(array):
        return array.reshape(array.shape[0], heads, -1)

    g_tok = jnp.concatenate([by_head(g_early[:, :span]), by_head(g_late[:, : 2 * span])], axis=2)
    g_state = jnp.concatenate(
        [by_head(g_late[:, 2 * span : 3 * span]), by_head(g_early[:, span : 3 * span])], axis=2
    )
    g_tout = g_early[:, 3 * span :].T.reshape(heads, HS, -1)
    g_sout = g_late[:, 3 * span : 4 * span].T.reshape(heads, HS, -1)

    squares = jnp.concatenate([jnp.sum(squares, axis=1), jnp.sum(branch_m * branch_m)[None]])
    slot = gtab[:, 0, :NBUCKET].reshape(-1)
    slots = lax.dynamic_update_slice_in_dim(
        jnp.zeros((size * slot.size,), F32), slot, me * slot.size, 0
    )
    tail = jnp.concatenate([slots, squares])
    tail = jnp.pad(tail, (0, width - tail.size))
    grad_decay = chain_small[1] * (decay * (1.0 - decay))[0]
    sums = sum_all(
        after(jnp.stack([grad_gain_a, grad_gain_m[0], chain_small[0], grad_decay, tail]), early_got)
    )
    place_at = (shard_pos * size + me) * cols
    mine = lax.dynamic_slice_in_dim(sums[:4], place_at, cols, 1)
    table_sum = lax.dynamic_slice_in_dim(sums[4], me * slot.size, slot.size, 0)
    table_sum = table_sum.reshape(heads, NBUCKET).T
    g_table = lax.dynamic_slice_in_dim(table_sum, shard_pos * bias_rows, bias_rows, 0)
    entries = own.size * shard_count * run_count * size
    first = size * slot.size
    rms_out = jnp.sqrt(sums[4, first : first + 3] / entries)

    return (
        output[None],
        grad_tokens[None],
        g_tok,
        g_state,
        g_tout,
        g_sout,
        g_in,
        g_out.T,
        g_table,
        g_late[:, 4 * span :].T,
        mine[:3],
        mine[3],
        rms_out,
    )


def solution(mesh):
    return jax.shard_map(
        shards,
        mesh=mesh,
        in_specs=(
            P("shard", ("context", "tensor"), None),
            P("shard", "context"),
            P("shard", "tensor", None),
            P("shard", "tensor", None),
            P("tensor", None, "shard"),
            P("tensor", None, "shard"),
            P("shard", "tensor"),
            P("tensor", "shard"),
            P("shard", "tensor"),
            P("tensor", "shard"),
            P(None, ("shard", "tensor")),
            P(("shard", "tensor")),
            P("shard", ("context", "tensor"), None),
        ),
        out_specs=(
            P("shard", ("context", "tensor"), None),
            P("shard", ("context", "tensor"), None),
            P("shard", "tensor", None),
            P("shard", "tensor", None),
            P("tensor", None, "shard"),
            P("tensor", None, "shard"),
            P("shard", "tensor"),
            P("tensor", "shard"),
            P("shard", "tensor"),
            P("tensor", "shard"),
            P(None, ("shard", "tensor")),
            P(("shard", "tensor")),
            P(),
        ),
        check_vma=False,
    )
```

```python
import functools

import jax
import jax.numpy as jnp
from jax import lax
from jax.experimental import pallas as pl
from jax.experimental.pallas import tpu as pltpu
from jax.sharding import PartitionSpec as P

HS = 128
BLK = 512
NBUCKET = 32
EDGES = (12, 16, 23, 32, 46, 64, 91)
LOW = jnp.bfloat16
F32 = jnp.float32
SCALE = HS ** (-0.5)
EPS = 1e-06
DIAG = 3 * BLK
SMALL = 16
PACE = 0.5


def mm(a, b, ca, cb):
    return lax.dot_general(a, b, (((ca,), (cb,)), ((), ())), preferred_element_type=F32)


def whole():
    return pl.BlockSpec(memory_space=pltpu.VMEM)


def columns(weight):
    _, width, index = weight
    return pl.BlockSpec((weight[0].shape[0], width), lambda *_: (0, index))


def scalars():
    return pl.BlockSpec(memory_space=pltpu.SMEM)


def params(grid_rank=0, mib=40):
    limit = mib * 1024 * 1024
    if grid_rank:
        return pltpu.CompilerParams(
            dimension_semantics=("arbitrary",) * grid_rank, vmem_limit_bytes=limit
        )
    return pltpu.CompilerParams(vmem_limit_bytes=limit)


def lasts(microseconds):
    return pl.CostEstimate(
        flops=int(microseconds * PACE * 1.1e9), bytes_accessed=int(microseconds * PACE * 3e6), transcendentals=0
    )


def rms_scale(v):
    return lax.rsqrt(jnp.mean(v * v, axis=-1, keepdims=True) + EPS)


def assemble_kernel(count, pos_ref, *refs):
    pieces, other_ref, outs = refs[:count], refs[count], refs[count + 1 :]
    part = pieces[0].shape[0]
    for s in range(count):
        base = (pos_ref[0] ^ s) * (2 * part)
        mine = pl.multiple_of(base + pos_ref[1] * part, part)
        theirs = pl.multiple_of(base + (1 - pos_ref[1]) * part, part)
        first = 0
        for out_ref in outs:
            last = first + out_ref.shape[1]
            out_ref[pl.ds(mine, part), :] = pieces[s][:, first:last]
            out_ref[pl.ds(theirs, part), :] = other_ref[s, :, first:last]
            first = last


def assemble(pos, pieces, other, widths):
    part, cols = pieces[0].shape
    rows = 2 * part * len(pieces)
    return pl.pallas_call(
        functools.partial(assemble_kernel, len(pieces)),
        out_shape=tuple(jax.ShapeDtypeStruct((rows, w), LOW) for w in widths),
        in_specs=[scalars()] + [whole()] * (len(pieces) + 1),
        out_specs=(whole(),) * len(widths),
        compiler_params=params(mib=16),
        cost_estimate=lasts(1.5),
        name="assemble",
    )(pos, *pieces, other)


def weight_grad_kernel(counts, extras, *refs):
    out_ref = refs[-1]
    at = 0
    first = 0
    for count in counts:
        right = refs[at + count]
        total = None
        row = 0
        for left in refs[at : at + count]:
            term = mm(left[...], right[row : row + left.shape[0], :], 0, 0)
            row += left.shape[0]
            total = term if total is None else total + term
        out_ref[:, first : first + right.shape[1]] = total.astype(LOW)
        first += right.shape[1]
        at += count + 1
    for extra in refs[at : at + extras]:
        out_ref[:, first : first + extra.shape[1]] = extra[...]
        first += extra.shape[1]


def weight_grad(pairs, extras=()):
    width = pairs[0][0][0].shape[1]
    tile = 256
    specs, args = [], []
    for lefts, right in pairs:
        specs += [pl.BlockSpec((left.shape[0], tile), lambda i: (0, i)) for left in lefts]
        specs.append(pl.BlockSpec(right.shape, lambda i: (0, 0)))
        args += list(lefts) + [right]
    specs += [pl.BlockSpec((tile, extra.shape[1]), lambda i: (i, 0)) for extra in extras]
    cols = sum(right.shape[1] for _, right in pairs) + sum(extra.shape[1] for extra in extras)
    return pl.pallas_call(
        functools.partial(weight_grad_kernel, [len(lefts) for lefts, _ in pairs], len(extras)),
        grid=(width // tile,),
        out_shape=jax.ShapeDtypeStruct((width, cols), LOW),
        in_specs=specs,
        out_specs=pl.BlockSpec((tile, cols), lambda i: (i, 0)),
        compiler_params=params(1, 20),
        cost_estimate=lasts(6),
        name="weight_grad",
    )(*args, *extras)


def token_proj_kernel(count, shards, blocks, me_ref, w_ref, *refs):
    pieces, small = refs[:count], refs[count : count + shards]
    q_ref, normed_ref, vec_ref, kv_ref, *kv_refs = refs[count + shards :]
    span = q_ref.shape[1]
    vectors = small[0][...].astype(F32)
    for piece in small[1:]:
        vectors = vectors + piece[...].astype(F32)
    vec_ref[...] = vectors
    gain = vectors[0:1]
    rows = pieces[0].shape[0] - SMALL
    for m in range(count):
        start = pl.multiple_of((me_ref[0] ^ m) * rows, rows)
        v = pieces[m][:rows, :].astype(F32)
        normed = (v * rms_scale(v) * gain).astype(LOW)
        normed_ref[pl.ds(start, rows), :] = normed
        kv_ref[pl.ds(start, rows), :] = mm(normed, w_ref[:, : 2 * span], 1, 0).astype(LOW)
        q_ref[pl.ds(start, rows), :] = mm(normed, w_ref[:, 2 * span :], 1, 0).astype(LOW)
    for b in range(blocks):
        kv_refs[b][...] = kv_ref[b * BLK : (b + 1) * BLK, :]


def token_proj(me, pieces, small, weight, blocks):
    width, cols = weight.shape
    span = cols // 3
    step = pieces[0].shape[0]
    rows = (step - SMALL) * len(pieces)
    return pl.pallas_call(
        functools.partial(token_proj_kernel, len(pieces), len(small), blocks),
        out_shape=(
            jax.ShapeDtypeStruct((rows, span), LOW),
            jax.ShapeDtypeStruct((rows, width), LOW),
            jax.ShapeDtypeStruct((SMALL, width), F32),
            jax.ShapeDtypeStruct((rows, 2 * span), LOW),
        )
        + (jax.ShapeDtypeStruct((BLK, 2 * span), LOW),) * blocks,
        in_specs=[scalars(), whole()] + [whole()] * (len(pieces) + len(small)),
        out_specs=(whole(),) * (4 + blocks),
        compiler_params=params(mib=56),
        cost_estimate=lasts(5),
        name="token_proj",
    )(me, weight, *pieces, *small)


def proj_kernel(count, weights, *refs):
    pieces, ws, outs = refs[:count], refs[count : count + weights], refs[count + weights :]
    rows = pieces[0].shape[0]
    for m in range(count):
        for w, out in zip(ws, outs, strict=True):
            out[m * rows : (m + 1) * rows, :] = mm(pieces[m][...], w[...], 1, 0).astype(LOW)


def proj(pieces, weights, mib=24):
    rows = pieces[0].shape[0] * len(pieces)
    return pl.pallas_call(
        functools.partial(proj_kernel, len(pieces), len(weights)),
        grid=(1,),
        out_shape=tuple(jax.ShapeDtypeStruct((rows, w[1]), LOW) for w in weights),
        in_specs=[whole()] * len(pieces) + [columns(w) for w in weights],
        out_specs=(whole(),) * len(weights),
        compiler_params=params(1, mib),
        cost_estimate=lasts(3),
        name="proj",
    )(*pieces, *[w[0] for w in weights])


def back_kernel(count, gained, size, me_ref, *refs):
    outs = refs[2 * count + gained : 2 * count + gained + size]
    total = None
    for i in range(count):
        term = mm(refs[i][...], refs[count + i][...], 1, 1)
        total = term if total is None else total + term
    step = pl.program_id(0)
    if gained:
        sums = jnp.sum(total * refs[2 * count][...].astype(F32), axis=0, keepdims=True)
        refs[-1][...] = sums + jnp.where(step == 0, 0.0, refs[-1][...])
    total = total.astype(LOW)
    for m in range(size):

        @pl.when(step == m)
        def _(m=m):
            outs[m][...] = total


def back(me, grads, weights, normed=None):
    rows, width = grads[0].shape[0], weights[0][0].shape[0]
    size = lax.axis_size("tensor")
    tile = rows // size
    extra = [] if normed is None else [normed]
    grid_spec = pltpu.PrefetchScalarGridSpec(
        num_scalar_prefetch=1,
        grid=(size,),
        in_specs=[pl.BlockSpec((tile, g.shape[1]), lambda i, me_ref: (i ^ me_ref[0], 0)) for g in grads]
        + [columns(w) for w in weights]
        + [pl.BlockSpec((tile, width), lambda i, me_ref: (i ^ me_ref[0], 0)) for _ in extra],
        out_specs=(pl.BlockSpec((tile, width), lambda i, me_ref: (0, 0)),) * size
        + (pl.BlockSpec((1, width), lambda i, me_ref: (0, 0)),) * len(extra),
    )
    return pl.pallas_call(
        functools.partial(back_kernel, len(grads), len(extra), size),
        grid_spec=grid_spec,
        out_shape=(jax.ShapeDtypeStruct((tile, width), LOW),) * size
        + (jax.ShapeDtypeStruct((1, width), F32),) * len(extra),
        compiler_params=params(1, 24),
        cost_estimate=lasts(3),
        name="back",
    )(me, *grads, *[w[0] for w in weights], *extra)


def branch_kernel(count, own_ref, gain_ref, *refs):
    parts, weights = refs[:count], refs[count : 2 * count]
    residual_ref, normed_ref, sums_ref = refs[2 * count :]
    branch = None
    for part, weight in zip(parts, weights, strict=True):
        term = mm(part[...], weight[...], 1, 1)
        branch = term if branch is None else branch + term
    own = own_ref[...].astype(F32)
    residual = own + branch
    residual_ref[...] = residual
    normed_ref[...] = (residual * rms_scale(residual) * gain_ref[...]).astype(LOW)
    sums_ref[0:1, :] = jnp.sum(own * own, axis=0, keepdims=True)
    sums_ref[1:2, :] = jnp.sum(branch * branch, axis=0, keepdims=True)


def branch_out(own, gain, parts, weights):
    rows, width = own.shape
    return pl.pallas_call(
        functools.partial(branch_kernel, len(parts)),
        out_shape=(
            jax.ShapeDtypeStruct((rows, width), F32),
            jax.ShapeDtypeStruct((rows, width), LOW),
            jax.ShapeDtypeStruct((2, width), F32),
        ),
        in_specs=[whole()] * (2 + 2 * len(parts)),
        out_specs=(whole(),) * 3,
        compiler_params=params(mib=12),
        cost_estimate=lasts(3),
        name="branch_out",
    )(own, gain, *parts, *weights)


def branch_back_kernel(count, sums, cot_ref, residual_ref, gain_ref, *refs):
    terms, weights, outs = refs[:sums], refs[sums : sums + count], refs[sums + count :]
    grad_ref, low_ref, gain_sum_ref, parts = outs[0], outs[1], outs[2], outs[3:]
    grad = terms[0][...].astype(F32)
    for term in terms[1:]:
        grad = grad + term[...].astype(F32)
    residual = residual_ref[...]
    r = rms_scale(residual)
    unit = residual * r
    gain_sum_ref[...] = jnp.sum(grad * unit, axis=0, keepdims=True)
    scaled = grad * gain_ref[...]
    grad = cot_ref[...].astype(F32) + r * (
        scaled - unit * jnp.mean(scaled * unit, axis=-1, keepdims=True)
    )
    grad_ref[...] = grad
    low = grad.astype(LOW)
    low_ref[...] = low
    for part, weight in zip(parts, weights, strict=True):
        part[...] = mm(low, weight[...], 1, 0).astype(LOW)


def branch_back(cot, residual, gain, terms, weights):
    rows, width = cot.shape
    span = weights[0].shape[1]
    return pl.pallas_call(
        functools.partial(branch_back_kernel, len(weights), len(terms)),
        out_shape=(
            jax.ShapeDtypeStruct((rows, width), F32),
            jax.ShapeDtypeStruct((rows, width), LOW),
            jax.ShapeDtypeStruct((1, width), F32),
        )
        + (jax.ShapeDtypeStruct((rows, span), LOW),) * len(weights),
        in_specs=[whole()] * (3 + len(terms) + len(weights)),
        out_specs=(whole(),) * (3 + len(weights)),
        compiler_params=params(mib=56),
        cost_estimate=lasts(2.5),
        name="branch_back",
    )(cot, residual, gain, *terms, *weights)


def gelu_parts(pre):
    half = 0.5 * (1.0 + lax.erf(pre * 0.7071067811865476))
    density = jnp.exp(pre * pre * -0.5) * 0.3989422804014327
    return half, density


def feed_kernel(count, w_ref, ghid_ref, *refs):
    pieces, (hidden_ref, gpre_ref), outs = refs[:count], refs[count : count + 2], refs[count + 2 :]
    rows = pieces[0].shape[0]
    for m in range(count):
        at = slice(m * rows, (m + 1) * rows)
        pre = mm(pieces[m][...], w_ref[...], 1, 0)
        half, density = gelu_parts(pre)
        hidden_ref[at, :] = (pre * half).astype(LOW)
        gpre = ((half + pre * density) * ghid_ref[at, :].astype(F32)).astype(LOW)
        gpre_ref[at, :] = gpre
        outs[m][...] = mm(gpre, w_ref[...], 1, 1).astype(LOW)


def feed(w_in, ghid, pieces):
    width, units = w_in[0].shape[0], w_in[1]
    own, count = pieces[0].shape[0], len(pieces)
    rows = own * count
    return pl.pallas_call(
        functools.partial(feed_kernel, count),
        grid=(1,),
        out_shape=(
            jax.ShapeDtypeStruct((rows, units), LOW),
            jax.ShapeDtypeStruct((rows, units), LOW),
        )
        + (jax.ShapeDtypeStruct((own, width), LOW),) * count,
        in_specs=[columns(w_in)] + [whole()] * (1 + count),
        out_specs=(whole(),) * (2 + count),
        compiler_params=params(1, 32),
        cost_estimate=lasts(7),
        name="feed",
    )(w_in[0], ghid, *pieces)


def column_softmax(scores):
    peak = jnp.max(scores, axis=0, keepdims=True)
    exponent = jnp.exp(scores - peak)
    return exponent * (1.0 / jnp.sum(exponent, axis=0, keepdims=True))


def chain_operands(count, brought, refs):
    kv, w = refs[:count], refs[count : 2 * count]
    if not brought:
        return kv, w, [(), ()] * count
    here, sems = refs[2 * count : 4 * count], refs[4 * count]
    copies = []
    for m in range(count):
        copies.append((pltpu.make_async_copy(w[m], here[count + m], sems.at[m]),))
        copies.append((pltpu.make_async_copy(kv[m], here[m], sems.at[count + m]),))
    for (copy,) in copies:
        copy.start()
    return here[:count], here[count:], copies


def chain_specs(kv, weights, brought):
    if not brought:
        return [whole()] * (2 * len(kv)), [], 24
    scratch = [pltpu.VMEM(array.shape, LOW) for array in list(kv) + list(weights)]
    scratch.append(pltpu.SemaphoreType.DMA((2 * len(kv),)))
    return [pl.BlockSpec(memory_space=pl.ANY)] * (2 * len(kv)), scratch, 56


def ready(copies):
    for copy in copies:
        copy.wait()


def chosen(flag_ref, mine_ref, got_ref):
    return jnp.where(flag_ref[0] != 0, got_ref[...].astype(F32), mine_ref[...])


def head_keys(kv, h):
    return kv[:, 2 * h * HS : (2 * h + 1) * HS]


def head_values(kv, h):
    return kv[:, (2 * h + 1) * HS : 2 * (h + 1) * HS]


def stacked(parts):
    return parts[0] if len(parts) == 1 else jnp.concatenate(parts, axis=0)


def chain_forward_kernel(
    count, heads, brought, flag_ref, gain_ref, dec_ref, mine_ref, got_ref, *refs
):
    outs = refs[2 * count : 2 * count + 5]
    state_ref, pair_ref, update_ref, next_ref, low_ref = outs
    kv, w, copies = chain_operands(count, brought, refs[: 2 * count] + refs[2 * count + 5 :])
    span = heads * HS
    dec = dec_ref[...]
    gain = gain_ref[...]
    state = chosen(flag_ref, mine_ref, got_ref)
    rows = state.shape[0]
    state_ref[...] = state
    normed = (state * rms_scale(state) * gain).astype(LOW)
    pair_ref[:rows, :] = normed
    queries = []
    for m in range(count):
        ready(copies[2 * m])
        queries.append(mm(normed, w[m][:, :span], 1, 0).astype(LOW))
    scores = []
    for m in range(count):
        ready(copies[2 * m + 1])
        for h in range(heads):
            scores.append(mm(head_keys(kv[m], h), queries[m][:, h * HS : (h + 1) * HS], 1, 1) * SCALE)
    weights = [column_softmax(score).astype(LOW) for score in scores]
    mixed = [
        stacked([mm(head_values(kv[m], h), weights[m * heads + h], 0, 0) for h in range(heads)])
        for m in range(count)
    ]
    update = None
    for m in range(count):
        term = mm(mixed[m].T.astype(LOW), w[m][:, span:], 1, 1)
        update = term if update is None else update + term
    update_ref[...] = update
    state = dec * state + (1.0 - dec) * update
    next_ref[...] = state
    low_ref[...] = state.astype(LOW)
    pair_ref[rows:, :] = (state * rms_scale(state) * gain).astype(LOW)


def chain_forward(flag, mine, got, gain, dec, kv, weights, brought):
    count = len(kv)
    rows, width = mine.shape
    heads = kv[0].shape[1] // (2 * HS)
    full = jax.ShapeDtypeStruct((rows, width), F32)
    specs, scratch, mib = chain_specs(kv, weights, brought)
    return pl.pallas_call(
        functools.partial(chain_forward_kernel, count, heads, brought),
        out_shape=(
            full,
            jax.ShapeDtypeStruct((2 * rows, width), LOW),
            full,
            full,
            jax.ShapeDtypeStruct((rows, width), LOW),
        ),
        in_specs=[scalars()] + [whole()] * 4 + specs,
        out_specs=(whole(),) * 5,
        scratch_shapes=scratch,
        compiler_params=params(mib=mib),
        cost_estimate=lasts(6.5),
        name="chain_forward",
    )(flag, gain, dec, mine, got, *kv, *weights)


def chain_backward_kernel(
    count, heads, terms, brought, flag_ref, gain_ref, dec_ref, state_ref, normed_ref, update_ref, mine_ref,
    got_ref, *refs
):
    gkv, refs = refs[:terms], refs[terms:]
    next_ref, low_ref, pair_ref, small_ref = refs[2 * count : 2 * count + 4]
    kv, w, copies = chain_operands(count, brought, refs[: 2 * count] + refs[2 * count + 4 :])
    span = heads * HS
    dec = dec_ref[...]
    gain = gain_ref[...]
    carry = chosen(flag_ref, mine_ref, got_ref)
    rows = carry.shape[0]
    state = state_ref[...]
    small_ref[1:2, :] = jnp.sum(carry * (state - update_ref[...]), axis=0, keepdims=True)
    gup = ((1.0 - dec) * carry).astype(LOW)
    pair_ref[rows:, :] = gup
    normed = normed_ref[...]
    queries, gmixes = [], []
    for m in range(count):
        ready(copies[2 * m])
        queries.append(mm(normed, w[m][:, :span], 1, 0).astype(LOW))
        gmixes.append(mm(gup, w[m][:, span:], 1, 0).astype(LOW))
    scores, grads = [], []
    for m in range(count):
        ready(copies[2 * m + 1])
        for h in range(heads):
            at = slice(h * HS, (h + 1) * HS)
            scores.append(mm(head_keys(kv[m], h), queries[m][:, at], 1, 1) * SCALE)
            grads.append(mm(head_values(kv[m], h), gmixes[m][:, at], 1, 1))
    lows = []
    for score, grad in zip(scores, grads, strict=True):
        weights = column_softmax(score)
        inner = jnp.sum(grad * weights, axis=0, keepdims=True)
        lows.append((weights * (grad - inner)).astype(LOW))
    grad_normed = gkv[0][...].astype(F32)
    for term in gkv[1:]:
        grad_normed = grad_normed + term[...].astype(F32)
    grad_queries = [
        stacked([mm(head_keys(kv[m], h), lows[m * heads + h], 0, 0) * SCALE for h in range(heads)])
        for m in range(count)
    ]
    for m in range(count):
        grad_normed = grad_normed + mm(grad_queries[m].T.astype(LOW), w[m][:, :span], 1, 1)
    r = rms_scale(state)
    unit = state * r
    scaled = grad_normed * gain
    small_ref[0:1, :] = jnp.sum(grad_normed * unit, axis=0, keepdims=True)
    carry = dec * carry + r * (scaled - unit * jnp.mean(scaled * unit, axis=-1, keepdims=True))
    next_ref[...] = carry
    low_ref[...] = carry.astype(LOW)
    pair_ref[:rows, :] = ((1.0 - dec) * carry).astype(LOW)


def chain_backward(flag, mine, got, gain, dec, state, normed, update, b, gkv, kv, weights, brought):
    count = len(kv)
    rows, width = state.shape
    heads = kv[0].shape[1] // (2 * HS)
    specs, scratch, mib = chain_specs(kv, weights, brought)
    return pl.pallas_call(
        functools.partial(chain_backward_kernel, count, heads, len(gkv), brought),
        grid=(1,),
        out_shape=(
            jax.ShapeDtypeStruct((rows, width), F32),
            jax.ShapeDtypeStruct((rows, width), LOW),
            jax.ShapeDtypeStruct((2 * rows, width), LOW),
            jax.ShapeDtypeStruct((2, width), F32),
        ),
        in_specs=[scalars()]
        + [whole()] * 3
        + [pl.BlockSpec((rows, width), lambda i: (b, 0))]
        + [whole()] * 3
        + [pl.BlockSpec((rows, width), lambda i: (b, 0)) for _ in gkv]
        + specs,
        out_specs=(whole(),) * 4,
        scratch_shapes=scratch,
        compiler_params=params(1, mib),
        cost_estimate=lasts(8.3),
        name="chain_backward",
    )(flag, gain, dec, state, normed, update, mine, got, *gkv, *kv, *weights)


def bucket_tile():
    lane = lax.broadcasted_iota(jnp.int32, (8, DIAG), 1)
    row = lax.broadcasted_iota(jnp.int32, (8, DIAG), 0)
    diff = lane - row
    diff = jnp.where(diff < 0, diff + DIAG, diff)
    offset = jnp.where(diff < BLK, diff, diff - DIAG) + BLK
    distance = jnp.abs(offset)
    far = jnp.full((8, DIAG), 8, jnp.int32)
    for edge in EDGES:
        far = far + (distance >= edge).astype(jnp.int32)
    near = jnp.where(distance < 8, distance, far)
    return jnp.where(offset >= 0, near, near + NBUCKET // 2)


def fill_bias(table_ref, h, bias_ref):
    bucket = bucket_tile()
    base = jnp.zeros((8, DIAG), F32)
    for k in range(NBUCKET):
        base = jnp.where(bucket == k, table_ref[h, k], base)
    for r in range(16):
        rolled = pltpu.roll(base, 8 * r, 1) if r else base
        wide = jnp.concatenate([rolled, rolled[:, :BLK]], axis=1)
        for k in range(2 * BLK // 128):
            start = (DIAG - 128 * k) % DIAG
            row = 8 * (16 * k + r)
            bias_ref[row : row + 8, :] = wide[:, start : start + BLK]


def collapse_bias(grad_ref, out_ref):
    total = jnp.zeros((8, DIAG), F32)
    for r in range(16):
        acc = [jnp.zeros((8, 128), F32)] * (DIAG // 128)
        for k in range(2 * BLK // 128):
            row = 8 * (16 * k + r)
            for c in range(BLK // 128):
                at = (c - k) % (DIAG // 128)
                acc[at] = acc[at] + grad_ref[row : row + 8, c * 128 : (c + 1) * 128]
        acc = jnp.concatenate(acc, axis=1)
        total = total + (pltpu.roll(acc, DIAG - 8 * r, 1) if r else acc)
    bucket = bucket_tile()
    lane = lax.broadcasted_iota(jnp.int32, (8, HS), 1)
    out = jnp.zeros((8, HS), F32)
    for k in range(NBUCKET):
        out = jnp.where(lane == k, jnp.sum(jnp.where(bucket == k, total, 0.0)), out)
    out_ref[...] = out


def current_mask(ids_ref):
    key = lax.broadcasted_iota(jnp.int32, (BLK, BLK), 0)
    query = lax.broadcasted_iota(jnp.int32, (BLK, BLK), 1)
    ids = ids_ref[...].astype(F32)
    column = jnp.broadcast_to(ids, (HS, BLK)).T[:, :1]
    return (key <= query) | ((column == ids) & (ids > 0.0))


def attend_kernel(
    run_ref, table_ref, q_ref, kc_ref, vc_ref, kp_ref, vp_ref, ko_ref, vo_ref, ks_ref, vs_ref,
    row_ref, out_ref, lse_ref, bias_ref, score_ref,
):
    h = pl.program_id(0)
    b = pl.program_id(1)

    @pl.when(b == 0)
    def _():
        fill_bias(table_ref, h, bias_ref)

    q = q_ref[...]
    first = b == 0
    keys = (
        ks_ref[...].reshape(BLK, HS),
        jnp.where(first, ko_ref[...], kp_ref[...]),
        kc_ref[...],
    )
    values = (
        vs_ref[...].reshape(BLK, HS),
        jnp.where(first, vo_ref[...], vp_ref[...]),
        vc_ref[...],
    )
    prior_ok = (run_ref[0] > 0) | (b > 0)
    score = mm(keys[0], q, 1, 1) * SCALE
    score_ref[0] = score
    peak = jnp.max(score, axis=0, keepdims=True)
    score = mm(keys[1], q, 1, 1) * SCALE + bias_ref[:BLK]
    score = jnp.where(prior_ok, score, -1e30)
    score_ref[1] = score
    peak = jnp.maximum(peak, jnp.max(score, axis=0, keepdims=True))
    score = mm(keys[2], q, 1, 1) * SCALE + bias_ref[BLK:]
    score = jnp.where(current_mask(row_ref), score, -1e30)
    score_ref[2] = score
    peak = jnp.maximum(peak, jnp.max(score, axis=0, keepdims=True))
    total = jnp.zeros((1, BLK), F32)
    for c in range(3):
        exponent = jnp.exp(score_ref[c] - peak)
        score_ref[c] = exponent
        total = total + jnp.sum(exponent, axis=0, keepdims=True)
    inverse = 1.0 / total
    mixed = jnp.zeros((HS, BLK), F32)
    for c in range(3):
        mixed = mixed + mm(values[c], (score_ref[c] * inverse).astype(LOW), 0, 0)
    out_ref[...] = mixed.T.astype(LOW)
    lse_ref[...] = peak + jnp.log(total)


def attend_specs(heads, pieces, part, blocks):
    def at(col):
        return pl.BlockSpec((BLK, HS), lambda h, b: (b, col(h)))

    def before(col):
        return pl.BlockSpec((BLK, HS), lambda h, b: (jnp.maximum(b - 1, 0), col(h)))

    def outer(col):
        return pl.BlockSpec((BLK, HS), lambda h, b: (0, col(h)))

    def state(col):
        return pl.BlockSpec((pieces, None, part, HS), lambda h, b: (0, b, 0, col(h)))

    key, value = (lambda h: 2 * h), (lambda h: 2 * h + 1)
    return [
        scalars(),
        scalars(),
        at(lambda h: h),
        at(key),
        at(value),
        before(key),
        before(value),
        outer(key),
        outer(value),
        state(lambda h: 2 * h),
        state(lambda h: 2 * h + 1),
        pl.BlockSpec((None, 1, BLK), lambda h, b: (b, 0, 0)),
    ]


def attend(run, table, q, kv, outer, sproj, ids_row):
    rows = q.shape[0]
    heads = q.shape[1] // HS
    pieces, blocks, part, _ = sproj.shape
    return pl.pallas_call(
        attend_kernel,
        grid=(heads, blocks),
        out_shape=(
            jax.ShapeDtypeStruct((rows, heads * HS), LOW),
            jax.ShapeDtypeStruct((heads, blocks, 1, BLK), F32),
        ),
        in_specs=attend_specs(heads, pieces, part, blocks),
        out_specs=(
            pl.BlockSpec((BLK, HS), lambda h, b: (b, h)),
            pl.BlockSpec((None, None, 1, BLK), lambda h, b: (h, b, 0, 0)),
        ),
        scratch_shapes=[pltpu.VMEM((2 * BLK, BLK), F32), pltpu.VMEM((3, BLK, BLK), F32)],
        compiler_params=params(2, 20),
        cost_estimate=lasts(9.7),
        name="attend",
    )(run, table, q, kv, kv, kv, kv, outer, outer, sproj, sproj, ids_row)


def attend_back_kernel(
    run_ref, table_ref, q_ref, kc_ref, vc_ref, kp_ref, vp_ref, ko_ref, vo_ref, ks_ref, vs_ref,
    row_ref, gmix_ref, lse_ref,
    gq_ref, gcur_ref, gprev_ref, gs_ref, gtab_ref,
    bias_ref, gbias_ref, prob_ref, gprob_ref,
):
    h = pl.program_id(0)
    b = pl.program_id(1)

    @pl.when(b == 0)
    def _():
        fill_bias(table_ref, h, bias_ref)
        gbias_ref[...] = jnp.zeros_like(gbias_ref)

    q = q_ref[...]
    gmix = gmix_ref[...]
    lse = lse_ref[...]
    first = b == 0
    keys = (
        ks_ref[...].reshape(BLK, HS),
        jnp.where(first, ko_ref[...], kp_ref[...]),
        kc_ref[...],
    )
    values = (
        vs_ref[...].reshape(BLK, HS),
        jnp.where(first, vo_ref[...], vp_ref[...]),
        vc_ref[...],
    )
    prior_ok = (run_ref[0] > 0) | (b > 0)
    inner = jnp.zeros((1, BLK), F32)
    grad_values = []
    for c in range(3):
        score = mm(keys[c], q, 1, 1) * SCALE
        if c == 1:
            score = jnp.where(prior_ok, score + bias_ref[:BLK], -1e30)
        if c == 2:
            score = jnp.where(current_mask(row_ref), score + bias_ref[BLK:], -1e30)
        prob = jnp.exp(score - lse)
        prob_ref[c] = prob
        grad_values.append(mm(prob.astype(LOW), gmix, 1, 0))
        grad_prob = mm(values[c], gmix, 1, 1)
        gprob_ref[c] = grad_prob
        inner = inner + jnp.sum(prob * grad_prob, axis=0, keepdims=True)
    grad_q = jnp.zeros((HS, BLK), F32)
    grad_keys = []
    for c in range(3):
        grad_score = (prob_ref[c] * (gprob_ref[c] - inner)).astype(LOW)
        if c > 0:
            gbias_ref[(c - 1) * BLK : c * BLK, :] += grad_score.astype(F32)
        grad_keys.append(mm(grad_score, q, 1, 0) * SCALE)
        grad_q = grad_q + mm(keys[c], grad_score, 0, 0)
    gq_ref[...] = (grad_q * SCALE).T.astype(LOW)
    part = gs_ref.shape[0], gs_ref.shape[1], HS
    gs_ref[:, :, :HS] = grad_keys[0].astype(LOW).reshape(part)
    gs_ref[:, :, HS:] = grad_values[0].astype(LOW).reshape(part)
    gprev_ref[:, :HS] = grad_keys[1].astype(LOW)
    gprev_ref[:, HS:] = grad_values[1].astype(LOW)
    gcur_ref[:, :HS] = grad_keys[2].astype(LOW)
    gcur_ref[:, HS:] = grad_values[2].astype(LOW)

    @pl.when(b == pl.num_programs(1) - 1)
    def _():
        collapse_bias(gbias_ref, gtab_ref)


def attend_back(run, table, q, kv, outer, sproj, ids_row, gmix, lse):
    rows = q.shape[0]
    heads = q.shape[1] // HS
    pieces, blocks, part, _ = sproj.shape

    def at():
        return pl.BlockSpec((BLK, HS), lambda h, b: (b, h))

    side = jax.ShapeDtypeStruct((rows, heads * 2 * HS), LOW)
    pair = pl.BlockSpec((BLK, 2 * HS), lambda h, b: (b, h))
    return pl.pallas_call(
        attend_back_kernel,
        grid=(heads, blocks),
        out_shape=(
            jax.ShapeDtypeStruct((rows, heads * HS), LOW),
            side,
            side,
            jax.ShapeDtypeStruct((pieces, blocks, part, heads * 2 * HS), LOW),
            jax.ShapeDtypeStruct((heads, 8, HS), F32),
        ),
        in_specs=attend_specs(heads, pieces, part, blocks)
        + [at(), pl.BlockSpec((None, None, 1, BLK), lambda h, b: (h, b, 0, 0))],
        out_specs=(
            at(),
            pair,
            pair,
            pl.BlockSpec((pieces, None, part, 2 * HS), lambda h, b: (0, b, 0, h)),
            pl.BlockSpec((None, 8, HS), lambda h, b: (h, 0, 0)),
        ),
        scratch_shapes=[
            pltpu.VMEM((2 * BLK, BLK), F32),
            pltpu.VMEM((2 * BLK, BLK), F32),
            pltpu.VMEM((3, BLK, BLK), F32),
            pltpu.VMEM((3, BLK, BLK), F32),
        ],
        compiler_params=params(2, 56),
        cost_estimate=lasts(16),
        name="attend_back",
    )(run, table, q, kv, kv, kv, kv, outer, outer, sproj, sproj, ids_row, gmix, lse)


def state_back_kernel(
    sq_ref, k_ref, v_ref, gmix_ref, gcur_ref, gnext_ref, gouter_ref,
    gkv_ref, gsq_ref, smix_ref,
):
    b = pl.program_id(1)
    last = b == pl.num_programs(1) - 1
    pieces, part = sq_ref.shape[0], sq_ref.shape[1]
    sq = sq_ref[...].reshape(BLK, HS)
    gmix = gmix_ref[...].reshape(BLK, HS)
    k, v = k_ref[...], v_ref[...]
    weights = column_softmax(mm(k, sq, 1, 1) * SCALE)
    low = weights.astype(LOW)
    grad_w = mm(v, gmix, 1, 1)
    inner = jnp.sum(grad_w * weights, axis=0, keepdims=True)
    grad_s = (weights * (grad_w - inner)).astype(LOW)
    grad_k = mm(grad_s, sq, 1, 0) * SCALE
    grad_v = mm(low, gmix, 1, 0)
    grad_q = mm(k, grad_s, 0, 0) * SCALE
    smix = mm(v, low, 0, 0)
    rest = gcur_ref[...].astype(F32) + jnp.where(last, gouter_ref[...], gnext_ref[...]).astype(F32)
    gkv_ref[:, :HS] = (rest[:, :HS] + grad_k).astype(LOW)
    gkv_ref[:, HS:] = (rest[:, HS:] + grad_v).astype(LOW)
    gsq_ref[...] = grad_q.T.astype(LOW).reshape(pieces, part, HS)
    smix_ref[...] = smix.T.astype(LOW).reshape(pieces, part, HS)


def state_back(sq, kv, gmix, gcur, gprev, outer):
    rows = gcur.shape[0]
    heads = gcur.shape[1] // (2 * HS)
    pieces, blocks, part, _ = sq.shape

    def at(col=lambda h: h):
        return pl.BlockSpec((BLK, HS), lambda h, b: (b, col(h)))

    def state():
        return pl.BlockSpec((pieces, None, part, HS), lambda h, b: (0, b, 0, h))

    side = jax.ShapeDtypeStruct((pieces, blocks, part, heads * HS), LOW)
    return pl.pallas_call(
        state_back_kernel,
        grid=(heads, blocks),
        out_shape=(jax.ShapeDtypeStruct((rows, heads * 2 * HS), LOW), side, side),
        in_specs=[
            state(),
            at(lambda h: 2 * h),
            at(lambda h: 2 * h + 1),
            state(),
            pl.BlockSpec((BLK, 2 * HS), lambda h, b: (b, h)),
            pl.BlockSpec((BLK, 2 * HS), lambda h, b: (jnp.minimum(b + 1, blocks - 1), h)),
            pl.BlockSpec((BLK, 2 * HS), lambda h, b: (0, h)),
        ],
        out_specs=(
            pl.BlockSpec((BLK, 2 * HS), lambda h, b: (b, h)),
            state(),
            state(),
        ),
        compiler_params=params(2, 16),
        cost_estimate=lasts(6.5),
        name="state_back",
    )(sq, kv, kv, gmix, gcur, gprev, outer)


def passed_along(array, axis, by):
    size = lax.axis_size(axis)
    pairs = [(i, i + by) for i in range(size) if 0 <= i + by < size]
    return lax.ppermute(array, axis, pairs)


def swap(array, axis, bits):
    return lax.ppermute(array, axis, [(i, i ^ bits) for i in range(lax.axis_size(axis))])


def far_pieces(array):
    return [array] + [swap(array, "tensor", m) for m in range(2, lax.axis_size("tensor"), 2)]


def chip_pieces(pieces, *fillers):
    out = []
    for j, piece in enumerate(pieces):
        if j and fillers:
            piece = after(piece, *fillers)
        out += [piece, swap(piece, "tensor", 1)]
    return out


def gather_rel(array, *fillers):
    return chip_pieces(far_pieces(array), *fillers)


def reduce_first(parts):
    size = len(parts)
    got = [swap(parts[m + 1], "tensor", 1) for m in range(0, size, 2)]
    sends = [
        (parts[m].astype(F32) + got[m // 2].astype(F32)).astype(LOW) for m in range(2, size, 2)
    ]
    return [parts[0], got[0]], sends


def reduce_last(own, sends, filler=None):
    terms = list(own)
    for j, send in enumerate(sends, 1):
        term = swap(send, "tensor", 2 * j)
        terms.append(term if filler is None else after(term, filler))
    return terms


def added(terms):
    return sum(term.astype(F32) for term in terms)


def exchange_rel(parts):
    return [part if m == 0 else swap(part, "tensor", m) for m, part in enumerate(parts)]


def cut(array, me):
    size = lax.axis_size("tensor")
    rows = array.shape[0] // size
    return [lax.dynamic_slice_in_dim(array, (me ^ m) * rows, rows, 0) for m in range(size)]


def place(pieces, me):
    rows = pieces[0].shape[0]
    out = jnp.zeros((rows * len(pieces),) + pieces[0].shape[1:], pieces[0].dtype)
    for m, piece in enumerate(pieces):
        out = lax.dynamic_update_slice_in_dim(out, piece, (me ^ m) * rows, 0)
    return out


def sum_all(array, *before_last):
    for axis in ("tensor", "shard", "context"):
        if axis == "context":
            array = after(array, *before_last)
        bits = 1
        while bits < lax.axis_size(axis):
            array = array + swap(array, axis, bits)
            bits *= 2
    return array


def rms_back(v, gain, grad):
    r = rms_scale(v)
    unit = v * r
    scaled = grad * gain
    return r * (scaled - unit * jnp.mean(scaled * unit, axis=-1, keepdims=True))


def dot(a, b, ca, cb):
    return lax.dot_general(a, b, (((ca,), (cb,)), ((), ())), preferred_element_type=F32)


def after(array, *others):
    return lax.optimization_barrier((array,) + others)[0]


def half_rows(local, run):
    part = local.shape[0] // 2
    return lax.dynamic_slice_in_dim(local, run * part, part, 0)


def shard_pieces(array):
    return [array if s == 0 else swap(array, "shard", s) for s in range(lax.axis_size("shard"))]


def scatter_rows(grad):
    return lax.psum_scatter(grad, "shard", scatter_dimension=0, tiled=True)


def shards(
    tokens,
    piece_ids,
    tok_qkv,
    state_qkv,
    tok_out,
    state_out,
    mlp_in,
    mlp_out,
    rel_bias,
    init_state,
    norm_gains,
    decay_param,
    cotangent,
):
    size = lax.axis_size("tensor")
    shard_count = lax.axis_size("shard")
    me = lax.axis_index("tensor")
    shard_pos = lax.axis_index("shard")
    run_pos = lax.axis_index("context")
    run_count = lax.axis_size("context")
    me_arr = me.astype(jnp.int32)[None]
    run_arr = run_pos.astype(jnp.int32)[None]
    pos = jnp.stack([shard_pos, run_pos]).astype(jnp.int32)
    own = tokens[0]
    own_rows, width = own.shape
    rows = own_rows * size
    blocks = rows // BLK
    heads = tok_qkv.shape[1]
    part = init_state.shape[0]
    span = heads * HS

    cols = norm_gains.shape[1]
    bias_rows = rel_bias.shape[0]
    slot_size = NBUCKET * heads
    small = jnp.zeros((SMALL, width), LOW)
    small = lax.dynamic_update_slice(
        small, jnp.concatenate([norm_gains, decay_param[None]], 0), (0, (shard_pos * size + me) * cols)
    )
    small = lax.dynamic_update_slice(
        small, rel_bias.reshape(1, -1), (4, me * slot_size + shard_pos * bias_rows * heads)
    )

    local_chain = jnp.concatenate(
        [state_qkv[:, :, :HS].reshape(-1, span), state_out.reshape(span, -1).T, init_state.T], axis=1
    )
    chain_pieces = shard_pieces(half_rows(local_chain, run_pos))
    local_tok = jnp.concatenate(
        [tok_qkv[:, :, HS:].reshape(-1, 2 * span), tok_qkv[:, :, :HS].reshape(-1, span)], axis=1
    )
    token_far = far_pieces(jnp.concatenate([own, small], axis=0))
    local_tok = after(local_tok, *token_far[1:], *chain_pieces)
    w_tok = lax.all_gather(local_tok, "shard", axis=0, tiled=True)
    token_pieces = chip_pieces(token_far, *chain_pieces)
    chain_other = swap(jnp.stack(chain_pieces), "context", 1)
    chain_own, start = assemble(pos, chain_pieces, chain_other, (2 * span, part))
    chip_own = swap(chain_own, "tensor", 1)
    small = sum(piece[own_rows:].astype(F32) for piece in token_pieces).astype(LOW)
    small_pieces = shard_pieces(after(small, chip_own))
    start = start.astype(F32).T
    small_pieces = [after(piece, start) for piece in small_pieces]
    w_sq, w_sout = (chain_own, span, 0), (chain_own, span, 1)

    chain_w = [chain_own, chip_own] + gather_rel(chain_own)[2:]

    local_side = jnp.concatenate(
        [state_qkv[:, :, HS:].reshape(-1, 2 * span), tok_out.reshape(span, -1).T], axis=1
    )
    local_mlp = jnp.concatenate([mlp_in, mlp_out.T], axis=1)

    w_side = lax.all_gather(after(local_side, chain_own), "shard", axis=0, tiled=True)
    w_skv, w_tout = (w_side, 2 * span, 0), w_side[:, 2 * span :]

    q, normed_a, vectors, kv, *kv_blocks = token_proj(
        me_arr, token_pieces, small_pieces, after(w_tok, *chain_w[2::2]), blocks
    )
    gains = vectors[:3]
    decay = jax.nn.sigmoid(vectors[3:4])
    table = lax.dynamic_slice_in_dim(vectors[4], me * slot_size, slot_size, 0)
    table = table.reshape(NBUCKET, heads).T
    kv_pieces = [gather_rel(kv_blocks[0])]

    w_mlp = lax.all_gather(after(local_mlp, q), "shard", axis=0, tiled=True)

    ids_row = piece_ids.reshape(blocks, 1, BLK)
    zero_arr = jnp.zeros((1,), jnp.int32)
    gain_s = gains[2:3]
    got, flag = jnp.zeros((part, width), LOW), zero_arr
    for round_index in range(run_count):
        state = start
        states, normeds, updates = [], [], []
        for b in range(blocks):
            if b == len(kv_pieces):
                kv_pieces.append(gather_rel(after(kv_blocks[b], *kv_pieces[-1][2::2]), state))
            if round_index + b == run_count:
                state = after(state, outer, *tout_far)
            state, pair, update, following, low = chain_forward(
                zero_arr if b else flag, state, got, gain_s, decay, kv_pieces[b], chain_w,
                round_index > 0,
            )
            if round_index + b == 0:
                outer = passed_along(after(kv_blocks[-1], low), "context", 1)
            states.append(state)
            normeds.append(pair)
            updates.append(update)
            state = following
        if round_index + 1 < run_count:
            got, flag = passed_along(low, "context", 1), run_arr
            if round_index == 0:
                grad_far = far_pieces(after(cotangent[0], *kv_pieces[-1][2::2]))
                tout_far = far_pieces(after(w_tout, *grad_far))
                got = after(got, *grad_far)
    units = mlp_in.shape[1]
    w_in, w_out = (w_mlp, units, 0), (w_mlp, units, 1)
    normed_s = stacked([pair for pair in normeds[::2]])[: blocks * part]
    state_pieces = gather_rel(normed_s, updates[-1])
    sq, skv = proj(state_pieces, [w_sq, w_skv])
    sq = sq.reshape(size, blocks, part, span)
    skv = skv.reshape(size, blocks, part, 2 * span)

    mixed, lse = attend(run_arr, table, q, kv, outer, skv, ids_row)
    grad_pieces = chip_pieces(grad_far, mixed)
    tout_pieces = chip_pieces(tout_far, mixed)
    mixed_parts = cut(mixed, me)
    residual, normed_m, squares = branch_out(own, gains[1:2], exchange_rel(mixed_parts), tout_pieces)

    (grad_hidden,) = proj([after(piece, normed_m) for piece in grad_pieces], [w_out])
    mlp_pieces = gather_rel(normed_m, grad_hidden)
    hidden, grad_pre, *parts = feed(w_in, grad_hidden, mlp_pieces)
    sums, sends = reduce_first(parts)
    grad_w_mlp = weight_grad([(mlp_pieces, after(grad_pre, *sends)), (grad_pieces, hidden)])
    terms = reduce_last(sums, sends, grad_w_mlp)
    mlp_mine = scatter_rows(after(grad_w_mlp, *terms))

    grad_res, grad_branch, grad_gain_m, *gmix_parts = branch_back(
        cotangent[0], residual, gains[1:2], terms, tout_pieces
    )
    gmix = place(exchange_rel(gmix_parts), me)
    gq, gcur, gprev, gs, gtab = attend_back(
        run_arr, table, q, kv, outer, skv, ids_row, gmix, lse
    )
    branch_pieces = gather_rel(after(grad_branch, gmix), gq)
    gs = after(gs, branch_pieces[-2])
    outer_back = passed_along(gprev[:BLK], "context", -1)

    gs = gs.reshape(-1, 2 * span)
    sums, sends = reduce_first(back(zero_arr, [gs], [w_skv]))
    parts = back(zero_arr, [after(hidden, *sends)], [w_out])
    state_terms = reduce_last(sums, sends, parts[0])
    state_terms[0] = after(state_terms[0], outer_back)
    sums, sends = reduce_first(parts)
    branch_m = reduce_last(sums, [after(send, *state_terms) for send in sends])

    got, flag = jnp.zeros((part, width), LOW), zero_arr
    not_last = (run_pos != run_count - 1).astype(jnp.int32)[None]
    for round_index in range(run_count):
        carry = jnp.zeros_like(start)
        gups = [None] * blocks
        chain_small = jnp.zeros((2, width), F32)
        for b in reversed(range(blocks)):
            carry, low, pair, row_sums = chain_backward(
                flag if b == blocks - 1 else zero_arr, carry, got, gain_s, decay, states[b], normed_s,
                updates[b], b, state_terms, kv_pieces[b], chain_w, round_index > 0,
            )
            chain_small = chain_small + row_sums
            gups[b] = pair
        if round_index + 1 < run_count:
            got, flag = passed_along(low, "context", -1), not_last
            if round_index == 0:
                grad_w_early = weight_grad(
                    [
                        ([normed_a], after(gq, carry)),
                        (state_pieces, gs),
                        (branch_pieces, jnp.concatenate(mixed_parts, axis=0)),
                    ]
                )
                got = came = after(got, grad_w_early, *branch_m)
    gup_all = stacked([gups[b] for b in range(blocks - 1, 0, -2)][::-1])
    grad_start = jnp.where(run_pos == 0, carry, 0.0).astype(LOW)
    branch_m = added(branch_m)
    output = (residual + branch_m).astype(LOW)
    mlp_halves = [after(mlp_mine[:, i * units : (i + 1) * units], gup_all) for i in range(2)]
    mlp_got = [swap(mlp_halves[0], "context", 1)]
    gup_pieces = gather_rel(gup_all, carry, mlp_got[0])
    early_mine = scatter_rows(after(grad_w_early, came))
    (gsmix,) = proj(gup_pieces, [w_sout])
    gsmix = gsmix.reshape(size, blocks, part, span)
    gkv, gsq, smix = state_back(sq, kv, gsmix, gcur, gprev, outer_back)
    grad_w_late = weight_grad(
        [([normed_a], gkv), (state_pieces, gsq.reshape(-1, span)), (gup_pieces, smix.reshape(-1, span))],
        [grad_start.T],
    )
    mlp_got.append(swap(after(mlp_halves[1], grad_w_late), "context", 1))
    early_got = swap(after(early_mine, grad_w_late), "context", 1)
    late_mine = scatter_rows(grad_w_late)
    g_in, g_out = (
        half.astype(F32) + other.astype(F32) for half, other in zip(mlp_halves, mlp_got, strict=True)
    )
    g_early = early_mine.astype(F32) + early_got.astype(F32)
    g_late = late_mine.astype(F32) + swap(late_mine, "context", 1).astype(F32)

    *parts, gain_sums = back(
        me_arr,
        [gq, after(gkv, grad_w_late)],
        [(w_tok, span, 2), (w_tok, 2 * span, 0)],
        normed_a,
    )
    grad_gain_a = (gain_sums / gains[0:1])[0]
    inputs = own.astype(F32)
    terms = reduce_last(*reduce_first(parts))
    grad_normed_a = added(terms)
    grad_tokens = (grad_res + rms_back(inputs, gains[0], grad_normed_a)).astype(LOW)

    def by_head(array):
        return array.reshape(array.shape[0], heads, -1)

    g_tok = jnp.concatenate([by_head(g_early[:, :span]), by_head(g_late[:, : 2 * span])], axis=2)
    g_state = jnp.concatenate(
        [by_head(g_late[:, 2 * span : 3 * span]), by_head(g_early[:, span : 3 * span])], axis=2
    )
    g_tout = g_early[:, 3 * span :].T.reshape(heads, HS, -1)
    g_sout = g_late[:, 3 * span : 4 * span].T.reshape(heads, HS, -1)

    squares = jnp.concatenate([jnp.sum(squares, axis=1), jnp.sum(branch_m * branch_m)[None]])
    slot = gtab[:, 0, :NBUCKET].reshape(-1)
    slots = lax.dynamic_update_slice_in_dim(
        jnp.zeros((size * slot.size,), F32), slot, me * slot.size, 0
    )
    tail = jnp.concatenate([slots, squares])
    tail = jnp.pad(tail, (0, width - tail.size))
    grad_decay = chain_small[1] * (decay * (1.0 - decay))[0]
    sums = sum_all(
        jnp.stack([grad_gain_a, grad_gain_m[0], chain_small[0], grad_decay, tail]),
        early_got,
        mlp_got[1],
        *terms,
    )
    place_at = (shard_pos * size + me) * cols
    mine = lax.dynamic_slice_in_dim(sums[:4], place_at, cols, 1)
    table_sum = lax.dynamic_slice_in_dim(sums[4], me * slot.size, slot.size, 0)
    table_sum = table_sum.reshape(heads, NBUCKET).T
    g_table = lax.dynamic_slice_in_dim(table_sum, shard_pos * bias_rows, bias_rows, 0)
    entries = own.size * shard_count * run_count * size
    first = size * slot.size
    rms_out = jnp.sqrt(sums[4, first : first + 3] / entries)

    return (
        output[None],
        grad_tokens[None],
        g_tok,
        g_state,
        g_tout,
        g_sout,
        g_in,
        g_out.T,
        g_table,
        g_late[:, 4 * span :].T,
        mine[:3],
        mine[3],
        rms_out,
    )


def solution(mesh):
    return jax.shard_map(
        shards,
        mesh=mesh,
        in_specs=(
            P("shard", ("context", "tensor"), None),
            P("shard", "context"),
            P("shard", "tensor", None),
            P("shard", "tensor", None),
            P("tensor", None, "shard"),
            P("tensor", None, "shard"),
            P("shard", "tensor"),
            P("tensor", "shard"),
            P("shard", "tensor"),
            P("tensor", "shard"),
            P(None, ("shard", "tensor")),
            P(("shard", "tensor")),
            P("shard", ("context", "tensor"), None),
        ),
        out_specs=(
            P("shard", ("context", "tensor"), None),
            P("shard", ("context", "tensor"), None),
            P("shard", "tensor", None),
            P("shard", "tensor", None),
            P("tensor", None, "shard"),
            P("tensor", None, "shard"),
            P("shard", "tensor"),
            P("tensor", "shard"),
            P("shard", "tensor"),
            P("tensor", "shard"),
            P(None, ("shard", "tensor")),
            P(("shard", "tensor")),
            P(),
        ),
        check_vma=False,
    )
```

```python
import functools

import jax
import jax.numpy as jnp
from jax import lax
from jax.experimental import pallas as pl
from jax.experimental.pallas import tpu as pltpu
from jax.sharding import PartitionSpec as P

HS = 128
BLK = 512
NBUCKET = 32
EDGES = (12, 16, 23, 32, 46, 64, 91)
LOW = jnp.bfloat16
F32 = jnp.float32
SCALE = HS ** (-0.5)
EPS = 1e-06
DIAG = 3 * BLK
SMALL = 16
PACE = 0.5


def mm(a, b, ca, cb):
    return lax.dot_general(a, b, (((ca,), (cb,)), ((), ())), preferred_element_type=F32)


def whole():
    return pl.BlockSpec(memory_space=pltpu.VMEM)


def columns(weight):
    _, width, index = weight
    return pl.BlockSpec((weight[0].shape[0], width), lambda *_: (0, index))


def scalars():
    return pl.BlockSpec(memory_space=pltpu.SMEM)


def params(grid_rank=0, mib=40):
    limit = mib * 1024 * 1024
    if grid_rank:
        return pltpu.CompilerParams(
            dimension_semantics=("arbitrary",) * grid_rank, vmem_limit_bytes=limit
        )
    return pltpu.CompilerParams(vmem_limit_bytes=limit)


def lasts(microseconds):
    return pl.CostEstimate(
        flops=int(microseconds * PACE * 1.1e9), bytes_accessed=int(microseconds * PACE * 3e6), transcendentals=0
    )


def rms_scale(v):
    return lax.rsqrt(jnp.mean(v * v, axis=-1, keepdims=True) + EPS)


def assemble_kernel(count, pos_ref, *refs):
    pieces, other_ref, outs = refs[:count], refs[count], refs[count + 1 :]
    part = pieces[0].shape[0]
    for s in range(count):
        base = (pos_ref[0] ^ s) * (2 * part)
        mine = pl.multiple_of(base + pos_ref[1] * part, part)
        theirs = pl.multiple_of(base + (1 - pos_ref[1]) * part, part)
        first = 0
        for out_ref in outs:
            last = first + out_ref.shape[1]
            out_ref[pl.ds(mine, part), :] = pieces[s][:, first:last]
            out_ref[pl.ds(theirs, part), :] = other_ref[s, :, first:last]
            first = last


def assemble(pos, pieces, other, widths):
    part, cols = pieces[0].shape
    rows = 2 * part * len(pieces)
    return pl.pallas_call(
        functools.partial(assemble_kernel, len(pieces)),
        out_shape=tuple(jax.ShapeDtypeStruct((rows, w), LOW) for w in widths),
        in_specs=[scalars()] + [whole()] * (len(pieces) + 1),
        out_specs=(whole(),) * len(widths),
        compiler_params=params(mib=16),
        cost_estimate=lasts(1.5),
        name="assemble",
    )(pos, *pieces, other)


def weight_grad_kernel(counts, extras, *refs):
    out_ref = refs[-1]
    at = 0
    first = 0
    for count in counts:
        right = refs[at + count]
        total = None
        row = 0
        for left in refs[at : at + count]:
            term = mm(left[...], right[row : row + left.shape[0], :], 0, 0)
            row += left.shape[0]
            total = term if total is None else total + term
        out_ref[:, first : first + right.shape[1]] = total.astype(LOW)
        first += right.shape[1]
        at += count + 1
    for extra in refs[at : at + extras]:
        out_ref[:, first : first + extra.shape[1]] = extra[...]
        first += extra.shape[1]


def weight_grad(pairs, extras=()):
    width = pairs[0][0][0].shape[1]
    tile = 256
    specs, args = [], []
    for lefts, right in pairs:
        specs += [pl.BlockSpec((left.shape[0], tile), lambda i: (0, i)) for left in lefts]
        specs.append(pl.BlockSpec(right.shape, lambda i: (0, 0)))
        args += list(lefts) + [right]
    specs += [pl.BlockSpec((tile, extra.shape[1]), lambda i: (i, 0)) for extra in extras]
    cols = sum(right.shape[1] for _, right in pairs) + sum(extra.shape[1] for extra in extras)
    return pl.pallas_call(
        functools.partial(weight_grad_kernel, [len(lefts) for lefts, _ in pairs], len(extras)),
        grid=(width // tile,),
        out_shape=jax.ShapeDtypeStruct((width, cols), LOW),
        in_specs=specs,
        out_specs=pl.BlockSpec((tile, cols), lambda i: (i, 0)),
        compiler_params=params(1, 20),
        cost_estimate=lasts(6),
        name="weight_grad",
    )(*args, *extras)


def token_proj_kernel(count, shards, blocks, me_ref, w_ref, *refs):
    pieces, small = refs[:count], refs[count : count + shards]
    q_ref, normed_ref, vec_ref, kv_ref, *kv_refs = refs[count + shards :]
    span = q_ref.shape[1]
    vectors = small[0][...].astype(F32)
    for piece in small[1:]:
        vectors = vectors + piece[...].astype(F32)
    vec_ref[...] = vectors
    gain = vectors[0:1]
    rows = pieces[0].shape[0] - SMALL
    for m in range(count):
        start = pl.multiple_of((me_ref[0] ^ m) * rows, rows)
        v = pieces[m][:rows, :].astype(F32)
        normed = (v * rms_scale(v) * gain).astype(LOW)
        normed_ref[pl.ds(start, rows), :] = normed
        kv_ref[pl.ds(start, rows), :] = mm(normed, w_ref[:, : 2 * span], 1, 0).astype(LOW)
        q_ref[pl.ds(start, rows), :] = mm(normed, w_ref[:, 2 * span :], 1, 0).astype(LOW)
    for b in range(blocks):
        kv_refs[b][...] = kv_ref[b * BLK : (b + 1) * BLK, :]


def token_proj(me, pieces, small, weight, blocks):
    width, cols = weight.shape
    span = cols // 3
    step = pieces[0].shape[0]
    rows = (step - SMALL) * len(pieces)
    return pl.pallas_call(
        functools.partial(token_proj_kernel, len(pieces), len(small), blocks),
        out_shape=(
            jax.ShapeDtypeStruct((rows, span), LOW),
            jax.ShapeDtypeStruct((rows, width), LOW),
            jax.ShapeDtypeStruct((SMALL, width), F32),
            jax.ShapeDtypeStruct((rows, 2 * span), LOW),
        )
        + (jax.ShapeDtypeStruct((BLK, 2 * span), LOW),) * blocks,
        in_specs=[scalars(), whole()] + [whole()] * (len(pieces) + len(small)),
        out_specs=(whole(),) * (4 + blocks),
        compiler_params=params(mib=56),
        cost_estimate=lasts(5),
        name="token_proj",
    )(me, weight, *pieces, *small)


def proj_kernel(count, weights, *refs):
    pieces, ws, outs = refs[:count], refs[count : count + weights], refs[count + weights :]
    rows = pieces[0].shape[0]
    for m in range(count):
        for w, out in zip(ws, outs, strict=True):
            out[m * rows : (m + 1) * rows, :] = mm(pieces[m][...], w[...], 1, 0).astype(LOW)


def proj(pieces, weights, mib=24):
    rows = pieces[0].shape[0] * len(pieces)
    return pl.pallas_call(
        functools.partial(proj_kernel, len(pieces), len(weights)),
        grid=(1,),
        out_shape=tuple(jax.ShapeDtypeStruct((rows, w[1]), LOW) for w in weights),
        in_specs=[whole()] * len(pieces) + [columns(w) for w in weights],
        out_specs=(whole(),) * len(weights),
        compiler_params=params(1, mib),
        cost_estimate=lasts(3),
        name="proj",
    )(*pieces, *[w[0] for w in weights])


def back_kernel(count, gained, size, me_ref, *refs):
    outs = refs[2 * count + gained : 2 * count + gained + size]
    total = None
    for i in range(count):
        term = mm(refs[i][...], refs[count + i][...], 1, 1)
        total = term if total is None else total + term
    step = pl.program_id(0)
    if gained:
        sums = jnp.sum(total * refs[2 * count][...].astype(F32), axis=0, keepdims=True)
        refs[-1][...] = sums + jnp.where(step == 0, 0.0, refs[-1][...])
    total = total.astype(LOW)
    for m in range(size):

        @pl.when(step == m)
        def _(m=m):
            outs[m][...] = total


def back(me, grads, weights, normed=None):
    rows, width = grads[0].shape[0], weights[0][0].shape[0]
    size = lax.axis_size("tensor")
    tile = rows // size
    extra = [] if normed is None else [normed]
    grid_spec = pltpu.PrefetchScalarGridSpec(
        num_scalar_prefetch=1,
        grid=(size,),
        in_specs=[pl.BlockSpec((tile, g.shape[1]), lambda i, me_ref: (i ^ me_ref[0], 0)) for g in grads]
        + [columns(w) for w in weights]
        + [pl.BlockSpec((tile, width), lambda i, me_ref: (i ^ me_ref[0], 0)) for _ in extra],
        out_specs=(pl.BlockSpec((tile, width), lambda i, me_ref: (0, 0)),) * size
        + (pl.BlockSpec((1, width), lambda i, me_ref: (0, 0)),) * len(extra),
    )
    return pl.pallas_call(
        functools.partial(back_kernel, len(grads), len(extra), size),
        grid_spec=grid_spec,
        out_shape=(jax.ShapeDtypeStruct((tile, width), LOW),) * size
        + (jax.ShapeDtypeStruct((1, width), F32),) * len(extra),
        compiler_params=params(1, 24),
        cost_estimate=lasts(3),
        name="back",
    )(me, *grads, *[w[0] for w in weights], *extra)


def branch_kernel(count, own_ref, gain_ref, *refs):
    parts, weights = refs[:count], refs[count : 2 * count]
    residual_ref, normed_ref, sums_ref = refs[2 * count :]
    branch = None
    for part, weight in zip(parts, weights, strict=True):
        term = mm(part[...], weight[...], 1, 1)
        branch = term if branch is None else branch + term
    own = own_ref[...].astype(F32)
    residual = own + branch
    residual_ref[...] = residual
    normed_ref[...] = (residual * rms_scale(residual) * gain_ref[...]).astype(LOW)
    sums_ref[0:1, :] = jnp.sum(own * own, axis=0, keepdims=True)
    sums_ref[1:2, :] = jnp.sum(branch * branch, axis=0, keepdims=True)


def branch_out(own, gain, parts, weights):
    rows, width = own.shape
    return pl.pallas_call(
        functools.partial(branch_kernel, len(parts)),
        out_shape=(
            jax.ShapeDtypeStruct((rows, width), F32),
            jax.ShapeDtypeStruct((rows, width), LOW),
            jax.ShapeDtypeStruct((2, width), F32),
        ),
        in_specs=[whole()] * (2 + 2 * len(parts)),
        out_specs=(whole(),) * 3,
        compiler_params=params(mib=56),
        cost_estimate=lasts(3),
        name="branch_out",
    )(own, gain, *parts, *weights)


def branch_back_kernel(count, sums, cot_ref, residual_ref, gain_ref, *refs):
    terms, weights, outs = refs[:sums], refs[sums : sums + count], refs[sums + count :]
    grad_ref, low_ref, gain_sum_ref, parts = outs[0], outs[1], outs[2], outs[3:]
    grad = terms[0][...].astype(F32)
    for term in terms[1:]:
        grad = grad + term[...].astype(F32)
    residual = residual_ref[...]
    r = rms_scale(residual)
    unit = residual * r
    gain_sum_ref[...] = jnp.sum(grad * unit, axis=0, keepdims=True)
    scaled = grad * gain_ref[...]
    grad = cot_ref[...].astype(F32) + r * (
        scaled - unit * jnp.mean(scaled * unit, axis=-1, keepdims=True)
    )
    grad_ref[...] = grad
    low = grad.astype(LOW)
    low_ref[...] = low
    for part, weight in zip(parts, weights, strict=True):
        part[...] = mm(low, weight[...], 1, 0).astype(LOW)


def branch_back(cot, residual, gain, terms, weights):
    rows, width = cot.shape
    span = weights[0].shape[1]
    return pl.pallas_call(
        functools.partial(branch_back_kernel, len(weights), len(terms)),
        out_shape=(
            jax.ShapeDtypeStruct((rows, width), F32),
            jax.ShapeDtypeStruct((rows, width), LOW),
            jax.ShapeDtypeStruct((1, width), F32),
        )
        + (jax.ShapeDtypeStruct((rows, span), LOW),) * len(weights),
        in_specs=[whole()] * (3 + len(terms) + len(weights)),
        out_specs=(whole(),) * (3 + len(weights)),
        compiler_params=params(mib=56),
        cost_estimate=lasts(2.5),
        name="branch_back",
    )(cot, residual, gain, *terms, *weights)


def gelu_parts(pre):
    half = 0.5 * (1.0 + lax.erf(pre * 0.7071067811865476))
    density = jnp.exp(pre * pre * -0.5) * 0.3989422804014327
    return half, density


def feed_kernel(count, w_ref, ghid_ref, *refs):
    pieces, (hidden_ref, gpre_ref), outs = refs[:count], refs[count : count + 2], refs[count + 2 :]
    rows = pieces[0].shape[0]
    for m in range(count):
        at = slice(m * rows, (m + 1) * rows)
        pre = mm(pieces[m][...], w_ref[...], 1, 0)
        half, density = gelu_parts(pre)
        hidden_ref[at, :] = (pre * half).astype(LOW)
        gpre = ((half + pre * density) * ghid_ref[at, :].astype(F32)).astype(LOW)
        gpre_ref[at, :] = gpre
        outs[m][...] = mm(gpre, w_ref[...], 1, 1).astype(LOW)


def feed(w_in, ghid, pieces):
    width, units = w_in[0].shape[0], w_in[1]
    own, count = pieces[0].shape[0], len(pieces)
    rows = own * count
    return pl.pallas_call(
        functools.partial(feed_kernel, count),
        grid=(1,),
        out_shape=(
            jax.ShapeDtypeStruct((rows, units), LOW),
            jax.ShapeDtypeStruct((rows, units), LOW),
        )
        + (jax.ShapeDtypeStruct((own, width), LOW),) * count,
        in_specs=[columns(w_in)] + [whole()] * (1 + count),
        out_specs=(whole(),) * (2 + count),
        compiler_params=params(1, 32),
        cost_estimate=lasts(7),
        name="feed",
    )(w_in[0], ghid, *pieces)


def column_softmax(scores):
    peak = jnp.max(scores, axis=0, keepdims=True)
    exponent = jnp.exp(scores - peak)
    return exponent * (1.0 / jnp.sum(exponent, axis=0, keepdims=True))


def chain_operands(count, brought, refs):
    kv, w = refs[:count], refs[count : 2 * count]
    if not brought:
        return kv, w, [(), ()] * count
    here, sems = refs[2 * count : 4 * count], refs[4 * count]
    copies = []
    for m in range(count):
        copies.append((pltpu.make_async_copy(w[m], here[count + m], sems.at[m]),))
        copies.append((pltpu.make_async_copy(kv[m], here[m], sems.at[count + m]),))
    for (copy,) in copies:
        copy.start()
    return here[:count], here[count:], copies


def chain_specs(kv, weights, brought):
    if not brought:
        return [whole()] * (2 * len(kv)), [], 24
    scratch = [pltpu.VMEM(array.shape, LOW) for array in list(kv) + list(weights)]
    scratch.append(pltpu.SemaphoreType.DMA((2 * len(kv),)))
    return [pl.BlockSpec(memory_space=pl.ANY)] * (2 * len(kv)), scratch, 56


def ready(copies):
    for copy in copies:
        copy.wait()


def chosen(flag_ref, mine_ref, got_ref):
    return jnp.where(flag_ref[0] != 0, got_ref[...].astype(F32), mine_ref[...])


def head_keys(kv, h):
    return kv[:, 2 * h * HS : (2 * h + 1) * HS]


def head_values(kv, h):
    return kv[:, (2 * h + 1) * HS : 2 * (h + 1) * HS]


def stacked(parts):
    return parts[0] if len(parts) == 1 else jnp.concatenate(parts, axis=0)


def chain_forward_kernel(
    count, heads, brought, flag_ref, gain_ref, dec_ref, mine_ref, got_ref, *refs
):
    outs = refs[2 * count : 2 * count + 5]
    state_ref, pair_ref, update_ref, next_ref, low_ref = outs
    kv, w, copies = chain_operands(count, brought, refs[: 2 * count] + refs[2 * count + 5 :])
    span = heads * HS
    dec = dec_ref[...]
    gain = gain_ref[...]
    state = chosen(flag_ref, mine_ref, got_ref)
    rows = state.shape[0]
    state_ref[...] = state
    normed = (state * rms_scale(state) * gain).astype(LOW)
    pair_ref[:rows, :] = normed
    queries = []
    for m in range(count):
        ready(copies[2 * m])
        queries.append(mm(normed, w[m][:, :span], 1, 0).astype(LOW))
    scores = []
    for m in range(count):
        ready(copies[2 * m + 1])
        for h in range(heads):
            scores.append(mm(head_keys(kv[m], h), queries[m][:, h * HS : (h + 1) * HS], 1, 1) * SCALE)
    weights = [column_softmax(score).astype(LOW) for score in scores]
    mixed = [
        stacked([mm(head_values(kv[m], h), weights[m * heads + h], 0, 0) for h in range(heads)])
        for m in range(count)
    ]
    update = None
    for m in range(count):
        term = mm(mixed[m].T.astype(LOW), w[m][:, span:], 1, 1)
        update = term if update is None else update + term
    update_ref[...] = update
    state = dec * state + (1.0 - dec) * update
    next_ref[...] = state
    low_ref[...] = state.astype(LOW)
    pair_ref[rows:, :] = (state * rms_scale(state) * gain).astype(LOW)


def chain_forward(flag, mine, got, gain, dec, kv, weights, brought):
    count = len(kv)
    rows, width = mine.shape
    heads = kv[0].shape[1] // (2 * HS)
    full = jax.ShapeDtypeStruct((rows, width), F32)
    specs, scratch, mib = chain_specs(kv, weights, brought)
    return pl.pallas_call(
        functools.partial(chain_forward_kernel, count, heads, brought),
        out_shape=(
            full,
            jax.ShapeDtypeStruct((2 * rows, width), LOW),
            full,
            full,
            jax.ShapeDtypeStruct((rows, width), LOW),
        ),
        in_specs=[scalars()] + [whole()] * 4 + specs,
        out_specs=(whole(),) * 5,
        scratch_shapes=scratch,
        compiler_params=params(mib=mib),
        cost_estimate=lasts(6.5),
        name="chain_forward",
    )(flag, gain, dec, mine, got, *kv, *weights)


def chain_backward_kernel(
    count, heads, terms, brought, flag_ref, gain_ref, dec_ref, state_ref, normed_ref, update_ref, mine_ref,
    got_ref, *refs
):
    gkv, refs = refs[:terms], refs[terms:]
    next_ref, low_ref, pair_ref, small_ref = refs[2 * count : 2 * count + 4]
    kv, w, copies = chain_operands(count, brought, refs[: 2 * count] + refs[2 * count + 4 :])
    span = heads * HS
    dec = dec_ref[...]
    gain = gain_ref[...]
    carry = chosen(flag_ref, mine_ref, got_ref)
    rows = carry.shape[0]
    state = state_ref[...]
    small_ref[1:2, :] = jnp.sum(carry * (state - update_ref[...]), axis=0, keepdims=True)
    gup = ((1.0 - dec) * carry).astype(LOW)
    pair_ref[rows:, :] = gup
    normed = normed_ref[...]
    queries, gmixes = [], []
    for m in range(count):
        ready(copies[2 * m])
        queries.append(mm(normed, w[m][:, :span], 1, 0).astype(LOW))
        gmixes.append(mm(gup, w[m][:, span:], 1, 0).astype(LOW))
    scores, grads = [], []
    for m in range(count):
        ready(copies[2 * m + 1])
        for h in range(heads):
            at = slice(h * HS, (h + 1) * HS)
            scores.append(mm(head_keys(kv[m], h), queries[m][:, at], 1, 1) * SCALE)
            grads.append(mm(head_values(kv[m], h), gmixes[m][:, at], 1, 1))
    lows = []
    for score, grad in zip(scores, grads, strict=True):
        weights = column_softmax(score)
        inner = jnp.sum(grad * weights, axis=0, keepdims=True)
        lows.append((weights * (grad - inner)).astype(LOW))
    grad_normed = gkv[0][...].astype(F32)
    for term in gkv[1:]:
        grad_normed = grad_normed + term[...].astype(F32)
    grad_queries = [
        stacked([mm(head_keys(kv[m], h), lows[m * heads + h], 0, 0) * SCALE for h in range(heads)])
        for m in range(count)
    ]
    for m in range(count):
        grad_normed = grad_normed + mm(grad_queries[m].T.astype(LOW), w[m][:, :span], 1, 1)
    r = rms_scale(state)
    unit = state * r
    scaled = grad_normed * gain
    small_ref[0:1, :] = jnp.sum(grad_normed * unit, axis=0, keepdims=True)
    carry = dec * carry + r * (scaled - unit * jnp.mean(scaled * unit, axis=-1, keepdims=True))
    next_ref[...] = carry
    low_ref[...] = carry.astype(LOW)
    pair_ref[:rows, :] = ((1.0 - dec) * carry).astype(LOW)


def chain_backward(flag, mine, got, gain, dec, state, normed, update, b, gkv, kv, weights, brought):
    count = len(kv)
    rows, width = state.shape
    heads = kv[0].shape[1] // (2 * HS)
    specs, scratch, mib = chain_specs(kv, weights, brought)
    return pl.pallas_call(
        functools.partial(chain_backward_kernel, count, heads, len(gkv), brought),
        grid=(1,),
        out_shape=(
            jax.ShapeDtypeStruct((rows, width), F32),
            jax.ShapeDtypeStruct((rows, width), LOW),
            jax.ShapeDtypeStruct((2 * rows, width), LOW),
            jax.ShapeDtypeStruct((2, width), F32),
        ),
        in_specs=[scalars()]
        + [whole()] * 3
        + [pl.BlockSpec((rows, width), lambda i: (b, 0))]
        + [whole()] * 3
        + [pl.BlockSpec((rows, width), lambda i: (b, 0)) for _ in gkv]
        + specs,
        out_specs=(whole(),) * 4,
        scratch_shapes=scratch,
        compiler_params=params(1, mib),
        cost_estimate=lasts(8.3),
        name="chain_backward",
    )(flag, gain, dec, state, normed, update, mine, got, *gkv, *kv, *weights)


def bucket_tile():
    lane = lax.broadcasted_iota(jnp.int32, (8, DIAG), 1)
    row = lax.broadcasted_iota(jnp.int32, (8, DIAG), 0)
    diff = lane - row
    diff = jnp.where(diff < 0, diff + DIAG, diff)
    offset = jnp.where(diff < BLK, diff, diff - DIAG) + BLK
    distance = jnp.abs(offset)
    far = jnp.full((8, DIAG), 8, jnp.int32)
    for edge in EDGES:
        far = far + (distance >= edge).astype(jnp.int32)
    near = jnp.where(distance < 8, distance, far)
    return jnp.where(offset >= 0, near, near + NBUCKET // 2)


def fill_bias(table_ref, h, bias_ref):
    bucket = bucket_tile()
    base = jnp.zeros((8, DIAG), F32)
    for k in range(NBUCKET):
        base = jnp.where(bucket == k, table_ref[h, k], base)
    for r in range(16):
        rolled = pltpu.roll(base, 8 * r, 1) if r else base
        wide = jnp.concatenate([rolled, rolled[:, :BLK]], axis=1)
        for k in range(2 * BLK // 128):
            start = (DIAG - 128 * k) % DIAG
            row = 8 * (16 * k + r)
            bias_ref[row : row + 8, :] = wide[:, start : start + BLK]


def collapse_bias(grad_ref, out_ref):
    total = jnp.zeros((8, DIAG), F32)
    for r in range(16):
        acc = [jnp.zeros((8, 128), F32)] * (DIAG // 128)
        for k in range(2 * BLK // 128):
            row = 8 * (16 * k + r)
            for c in range(BLK // 128):
                at = (c - k) % (DIAG // 128)
                acc[at] = acc[at] + grad_ref[row : row + 8, c * 128 : (c + 1) * 128]
        acc = jnp.concatenate(acc, axis=1)
        total = total + (pltpu.roll(acc, DIAG - 8 * r, 1) if r else acc)
    bucket = bucket_tile()
    lane = lax.broadcasted_iota(jnp.int32, (8, HS), 1)
    out = jnp.zeros((8, HS), F32)
    for k in range(NBUCKET):
        out = jnp.where(lane == k, jnp.sum(jnp.where(bucket == k, total, 0.0)), out)
    out_ref[...] = out


def current_mask(ids_ref):
    key = lax.broadcasted_iota(jnp.int32, (BLK, BLK), 0)
    query = lax.broadcasted_iota(jnp.int32, (BLK, BLK), 1)
    ids = ids_ref[...].astype(F32)
    column = jnp.broadcast_to(ids, (HS, BLK)).T[:, :1]
    return (key <= query) | ((column == ids) & (ids > 0.0))


def attend_kernel(
    run_ref, table_ref, q_ref, kc_ref, vc_ref, kp_ref, vp_ref, ko_ref, vo_ref, ks_ref, vs_ref,
    row_ref, out_ref, lse_ref, bias_ref, score_ref,
):
    h = pl.program_id(0)
    b = pl.program_id(1)

    @pl.when(b == 0)
    def _():
        fill_bias(table_ref, h, bias_ref)

    q = q_ref[...]
    first = b == 0
    keys = (
        ks_ref[...].reshape(BLK, HS),
        jnp.where(first, ko_ref[...], kp_ref[...]),
        kc_ref[...],
    )
    values = (
        vs_ref[...].reshape(BLK, HS),
        jnp.where(first, vo_ref[...], vp_ref[...]),
        vc_ref[...],
    )
    prior_ok = (run_ref[0] > 0) | (b > 0)
    score = mm(keys[0], q, 1, 1) * SCALE
    score_ref[0] = score
    peak = jnp.max(score, axis=0, keepdims=True)
    score = mm(keys[1], q, 1, 1) * SCALE + bias_ref[:BLK]
    score = jnp.where(prior_ok, score, -1e30)
    score_ref[1] = score
    peak = jnp.maximum(peak, jnp.max(score, axis=0, keepdims=True))
    score = mm(keys[2], q, 1, 1) * SCALE + bias_ref[BLK:]
    score = jnp.where(current_mask(row_ref), score, -1e30)
    score_ref[2] = score
    peak = jnp.maximum(peak, jnp.max(score, axis=0, keepdims=True))
    total = jnp.zeros((1, BLK), F32)
    for c in range(3):
        exponent = jnp.exp(score_ref[c] - peak)
        score_ref[c] = exponent
        total = total + jnp.sum(exponent, axis=0, keepdims=True)
    inverse = 1.0 / total
    mixed = jnp.zeros((HS, BLK), F32)
    for c in range(3):
        mixed = mixed + mm(values[c], (score_ref[c] * inverse).astype(LOW), 0, 0)
    out_ref[...] = mixed.T.astype(LOW)
    lse_ref[...] = peak + jnp.log(total)


def attend_specs(heads, pieces, part, blocks):
    def at(col):
        return pl.BlockSpec((BLK, HS), lambda h, b: (b, col(h)))

    def before(col):
        return pl.BlockSpec((BLK, HS), lambda h, b: (jnp.maximum(b - 1, 0), col(h)))

    def outer(col):
        return pl.BlockSpec((BLK, HS), lambda h, b: (0, col(h)))

    def state(col):
        return pl.BlockSpec((pieces, None, part, HS), lambda h, b: (0, b, 0, col(h)))

    key, value = (lambda h: 2 * h), (lambda h: 2 * h + 1)
    return [
        scalars(),
        scalars(),
        at(lambda h: h),
        at(key),
        at(value),
        before(key),
        before(value),
        outer(key),
        outer(value),
        state(lambda h: 2 * h),
        state(lambda h: 2 * h + 1),
        pl.BlockSpec((None, 1, BLK), lambda h, b: (b, 0, 0)),
    ]


def attend(run, table, q, kv, outer, sproj, ids_row):
    rows = q.shape[0]
    heads = q.shape[1] // HS
    pieces, blocks, part, _ = sproj.shape
    return pl.pallas_call(
        attend_kernel,
        grid=(heads, blocks),
        out_shape=(
            jax.ShapeDtypeStruct((rows, heads * HS), LOW),
            jax.ShapeDtypeStruct((heads, blocks, 1, BLK), F32),
        ),
        in_specs=attend_specs(heads, pieces, part, blocks),
        out_specs=(
            pl.BlockSpec((BLK, HS), lambda h, b: (b, h)),
            pl.BlockSpec((None, None, 1, BLK), lambda h, b: (h, b, 0, 0)),
        ),
        scratch_shapes=[pltpu.VMEM((2 * BLK, BLK), F32), pltpu.VMEM((3, BLK, BLK), F32)],
        compiler_params=params(2, 20),
        cost_estimate=lasts(9.7),
        name="attend",
    )(run, table, q, kv, kv, kv, kv, outer, outer, sproj, sproj, ids_row)


def attend_back_kernel(
    run_ref, table_ref, q_ref, kc_ref, vc_ref, kp_ref, vp_ref, ko_ref, vo_ref, ks_ref, vs_ref,
    row_ref, gmix_ref, lse_ref,
    gq_ref, gcur_ref, gprev_ref, gs_ref, gtab_ref,
    bias_ref, gbias_ref, prob_ref, gprob_ref,
):
    h = pl.program_id(0)
    b = pl.program_id(1)

    @pl.when(b == 0)
    def _():
        fill_bias(table_ref, h, bias_ref)
        gbias_ref[...] = jnp.zeros_like(gbias_ref)

    q = q_ref[...]
    gmix = gmix_ref[...]
    lse = lse_ref[...]
    first = b == 0
    keys = (
        ks_ref[...].reshape(BLK, HS),
        jnp.where(first, ko_ref[...], kp_ref[...]),
        kc_ref[...],
    )
    values = (
        vs_ref[...].reshape(BLK, HS),
        jnp.where(first, vo_ref[...], vp_ref[...]),
        vc_ref[...],
    )
    prior_ok = (run_ref[0] > 0) | (b > 0)
    inner = jnp.zeros((1, BLK), F32)
    grad_values = []
    for c in range(3):
        score = mm(keys[c], q, 1, 1) * SCALE
        if c == 1:
            score = jnp.where(prior_ok, score + bias_ref[:BLK], -1e30)
        if c == 2:
            score = jnp.where(current_mask(row_ref), score + bias_ref[BLK:], -1e30)
        prob = jnp.exp(score - lse)
        prob_ref[c] = prob
        grad_values.append(mm(prob.astype(LOW), gmix, 1, 0))
        grad_prob = mm(values[c], gmix, 1, 1)
        gprob_ref[c] = grad_prob
        inner = inner + jnp.sum(prob * grad_prob, axis=0, keepdims=True)
    grad_q = jnp.zeros((HS, BLK), F32)
    grad_keys = []
    for c in range(3):
        grad_score = (prob_ref[c] * (gprob_ref[c] - inner)).astype(LOW)
        if c > 0:
            gbias_ref[(c - 1) * BLK : c * BLK, :] += grad_score.astype(F32)
        grad_keys.append(mm(grad_score, q, 1, 0) * SCALE)
        grad_q = grad_q + mm(keys[c], grad_score, 0, 0)
    gq_ref[...] = (grad_q * SCALE).T.astype(LOW)
    part = gs_ref.shape[0], gs_ref.shape[1], HS
    gs_ref[:, :, :HS] = grad_keys[0].astype(LOW).reshape(part)
    gs_ref[:, :, HS:] = grad_values[0].astype(LOW).reshape(part)
    gprev_ref[:, :HS] = grad_keys[1].astype(LOW)
    gprev_ref[:, HS:] = grad_values[1].astype(LOW)
    gcur_ref[:, :HS] = grad_keys[2].astype(LOW)
    gcur_ref[:, HS:] = grad_values[2].astype(LOW)

    @pl.when(b == pl.num_programs(1) - 1)
    def _():
        collapse_bias(gbias_ref, gtab_ref)


def attend_back(run, table, q, kv, outer, sproj, ids_row, gmix, lse):
    rows = q.shape[0]
    heads = q.shape[1] // HS
    pieces, blocks, part, _ = sproj.shape

    def at():
        return pl.BlockSpec((BLK, HS), lambda h, b: (b, h))

    side = jax.ShapeDtypeStruct((rows, heads * 2 * HS), LOW)
    pair = pl.BlockSpec((BLK, 2 * HS), lambda h, b: (b, h))
    return pl.pallas_call(
        attend_back_kernel,
        grid=(heads, blocks),
        out_shape=(
            jax.ShapeDtypeStruct((rows, heads * HS), LOW),
            side,
            side,
            jax.ShapeDtypeStruct((pieces, blocks, part, heads * 2 * HS), LOW),
            jax.ShapeDtypeStruct((heads, 8, HS), F32),
        ),
        in_specs=attend_specs(heads, pieces, part, blocks)
        + [at(), pl.BlockSpec((None, None, 1, BLK), lambda h, b: (h, b, 0, 0))],
        out_specs=(
            at(),
            pair,
            pair,
            pl.BlockSpec((pieces, None, part, 2 * HS), lambda h, b: (0, b, 0, h)),
            pl.BlockSpec((None, 8, HS), lambda h, b: (h, 0, 0)),
        ),
        scratch_shapes=[
            pltpu.VMEM((2 * BLK, BLK), F32),
            pltpu.VMEM((2 * BLK, BLK), F32),
            pltpu.VMEM((3, BLK, BLK), F32),
            pltpu.VMEM((3, BLK, BLK), F32),
        ],
        compiler_params=params(2, 56),
        cost_estimate=lasts(16),
        name="attend_back",
    )(run, table, q, kv, kv, kv, kv, outer, outer, sproj, sproj, ids_row, gmix, lse)


def state_back_kernel(
    sq_ref, k_ref, v_ref, gmix_ref, gcur_ref, gnext_ref, gouter_ref,
    gkv_ref, gsq_ref, smix_ref,
):
    b = pl.program_id(1)
    last = b == pl.num_programs(1) - 1
    pieces, part = sq_ref.shape[0], sq_ref.shape[1]
    sq = sq_ref[...].reshape(BLK, HS)
    gmix = gmix_ref[...].reshape(BLK, HS)
    k, v = k_ref[...], v_ref[...]
    weights = column_softmax(mm(k, sq, 1, 1) * SCALE)
    low = weights.astype(LOW)
    grad_w = mm(v, gmix, 1, 1)
    inner = jnp.sum(grad_w * weights, axis=0, keepdims=True)
    grad_s = (weights * (grad_w - inner)).astype(LOW)
    grad_k = mm(grad_s, sq, 1, 0) * SCALE
    grad_v = mm(low, gmix, 1, 0)
    grad_q = mm(k, grad_s, 0, 0) * SCALE
    smix = mm(v, low, 0, 0)
    rest = gcur_ref[...].astype(F32) + jnp.where(last, gouter_ref[...], gnext_ref[...]).astype(F32)
    gkv_ref[:, :HS] = (rest[:, :HS] + grad_k).astype(LOW)
    gkv_ref[:, HS:] = (rest[:, HS:] + grad_v).astype(LOW)
    gsq_ref[...] = grad_q.T.astype(LOW).reshape(pieces, part, HS)
    smix_ref[...] = smix.T.astype(LOW).reshape(pieces, part, HS)


def state_back(sq, kv, gmix, gcur, gprev, outer):
    rows = gcur.shape[0]
    heads = gcur.shape[1] // (2 * HS)
    pieces, blocks, part, _ = sq.shape

    def at(col=lambda h: h):
        return pl.BlockSpec((BLK, HS), lambda h, b: (b, col(h)))

    def state():
        return pl.BlockSpec((pieces, None, part, HS), lambda h, b: (0, b, 0, h))

    side = jax.ShapeDtypeStruct((pieces, blocks, part, heads * HS), LOW)
    return pl.pallas_call(
        state_back_kernel,
        grid=(heads, blocks),
        out_shape=(jax.ShapeDtypeStruct((rows, heads * 2 * HS), LOW), side, side),
        in_specs=[
            state(),
            at(lambda h: 2 * h),
            at(lambda h: 2 * h + 1),
            state(),
            pl.BlockSpec((BLK, 2 * HS), lambda h, b: (b, h)),
            pl.BlockSpec((BLK, 2 * HS), lambda h, b: (jnp.minimum(b + 1, blocks - 1), h)),
            pl.BlockSpec((BLK, 2 * HS), lambda h, b: (0, h)),
        ],
        out_specs=(
            pl.BlockSpec((BLK, 2 * HS), lambda h, b: (b, h)),
            state(),
            state(),
        ),
        compiler_params=params(2, 16),
        cost_estimate=lasts(6.5),
        name="state_back",
    )(sq, kv, kv, gmix, gcur, gprev, outer)


def passed_along(array, axis, by):
    size = lax.axis_size(axis)
    pairs = [(i, i + by) for i in range(size) if 0 <= i + by < size]
    return lax.ppermute(array, axis, pairs)


def swap(array, axis, bits):
    return lax.ppermute(array, axis, [(i, i ^ bits) for i in range(lax.axis_size(axis))])


def far_pieces(array):
    return [array] + [swap(array, "tensor", m) for m in range(2, lax.axis_size("tensor"), 2)]


def chip_pieces(pieces, *fillers):
    out = []
    for j, piece in enumerate(pieces):
        if j and fillers:
            piece = after(piece, *fillers)
        out += [piece, swap(piece, "tensor", 1)]
    return out


def gather_rel(array, *fillers):
    return chip_pieces(far_pieces(array), *fillers)


def reduce_first(parts):
    size = len(parts)
    got = [swap(parts[m + 1], "tensor", 1) for m in range(0, size, 2)]
    sends = [
        (parts[m].astype(F32) + got[m // 2].astype(F32)).astype(LOW) for m in range(2, size, 2)
    ]
    return [parts[0], got[0]], sends


def reduce_last(own, sends, filler=None):
    terms = list(own)
    for j, send in enumerate(sends, 1):
        term = swap(send, "tensor", 2 * j)
        terms.append(term if filler is None else after(term, filler))
    return terms


def added(terms):
    return sum(term.astype(F32) for term in terms)


def exchange_rel(parts):
    return [part if m == 0 else swap(part, "tensor", m) for m, part in enumerate(parts)]


def cut(array, me):
    size = lax.axis_size("tensor")
    rows = array.shape[0] // size
    return [lax.dynamic_slice_in_dim(array, (me ^ m) * rows, rows, 0) for m in range(size)]


def place(pieces, me):
    rows = pieces[0].shape[0]
    out = jnp.zeros((rows * len(pieces),) + pieces[0].shape[1:], pieces[0].dtype)
    for m, piece in enumerate(pieces):
        out = lax.dynamic_update_slice_in_dim(out, piece, (me ^ m) * rows, 0)
    return out


def sum_all(array, *before_last):
    for axis in ("tensor", "shard", "context"):
        if axis == "context":
            array = after(array, *before_last)
        bits = 1
        while bits < lax.axis_size(axis):
            array = array + swap(array, axis, bits)
            bits *= 2
    return array


def rms_back(v, gain, grad):
    r = rms_scale(v)
    unit = v * r
    scaled = grad * gain
    return r * (scaled - unit * jnp.mean(scaled * unit, axis=-1, keepdims=True))


def dot(a, b, ca, cb):
    return lax.dot_general(a, b, (((ca,), (cb,)), ((), ())), preferred_element_type=F32)


def after(array, *others):
    return lax.optimization_barrier((array,) + others)[0]


def half_rows(local, run):
    part = local.shape[0] // 2
    return lax.dynamic_slice_in_dim(local, run * part, part, 0)


def shard_pieces(array):
    return [array if s == 0 else swap(array, "shard", s) for s in range(lax.axis_size("shard"))]


def scatter_rows(grad):
    return lax.psum_scatter(grad, "shard", scatter_dimension=0, tiled=True)


def shards(
    tokens,
    piece_ids,
    tok_qkv,
    state_qkv,
    tok_out,
    state_out,
    mlp_in,
    mlp_out,
    rel_bias,
    init_state,
    norm_gains,
    decay_param,
    cotangent,
):
    size = lax.axis_size("tensor")
    shard_count = lax.axis_size("shard")
    me = lax.axis_index("tensor")
    shard_pos = lax.axis_index("shard")
    run_pos = lax.axis_index("context")
    run_count = lax.axis_size("context")
    me_arr = me.astype(jnp.int32)[None]
    run_arr = run_pos.astype(jnp.int32)[None]
    pos = jnp.stack([shard_pos, run_pos]).astype(jnp.int32)
    own = tokens[0]
    own_rows, width = own.shape
    rows = own_rows * size
    blocks = rows // BLK
    heads = tok_qkv.shape[1]
    part = init_state.shape[0]
    span = heads * HS

    cols = norm_gains.shape[1]
    bias_rows = rel_bias.shape[0]
    slot_size = NBUCKET * heads
    small = jnp.zeros((SMALL, width), LOW)
    small = lax.dynamic_update_slice(
        small, jnp.concatenate([norm_gains, decay_param[None]], 0), (0, (shard_pos * size + me) * cols)
    )
    small = lax.dynamic_update_slice(
        small, rel_bias.reshape(1, -1), (4, me * slot_size + shard_pos * bias_rows * heads)
    )

    local_chain = jnp.concatenate(
        [state_qkv[:, :, :HS].reshape(-1, span), state_out.reshape(span, -1).T, init_state.T], axis=1
    )
    chain_pieces = shard_pieces(half_rows(local_chain, run_pos))
    local_tok = jnp.concatenate(
        [tok_qkv[:, :, HS:].reshape(-1, 2 * span), tok_qkv[:, :, :HS].reshape(-1, span)], axis=1
    )
    token_far = far_pieces(jnp.concatenate([own, small], axis=0))
    local_tok = after(local_tok, *token_far[1:], *chain_pieces)
    w_tok = lax.all_gather(local_tok, "shard", axis=0, tiled=True)
    token_pieces = chip_pieces(token_far, *chain_pieces)
    chain_other = swap(jnp.stack(chain_pieces), "context", 1)
    chain_own, start = assemble(pos, chain_pieces, chain_other, (2 * span, part))
    chip_own = swap(chain_own, "tensor", 1)
    small = sum(piece[own_rows:].astype(F32) for piece in token_pieces).astype(LOW)
    small_pieces = shard_pieces(after(small, chip_own))
    start = start.astype(F32).T
    small_pieces = [after(piece, start) for piece in small_pieces]
    w_sq, w_sout = (chain_own, span, 0), (chain_own, span, 1)

    chain_w = [chain_own, chip_own] + gather_rel(chain_own)[2:]

    local_side = jnp.concatenate(
        [state_qkv[:, :, HS:].reshape(-1, 2 * span), tok_out.reshape(span, -1).T], axis=1
    )
    local_mlp = jnp.concatenate([mlp_in, mlp_out.T], axis=1)

    w_side = lax.all_gather(after(local_side, chain_own), "shard", axis=0, tiled=True)
    w_skv, w_tout = (w_side, 2 * span, 0), w_side[:, 2 * span :]

    q, normed_a, vectors, kv, *kv_blocks = token_proj(
        me_arr, token_pieces, small_pieces, after(w_tok, *chain_w[2::2]), blocks
    )
    gains = vectors[:3]
    decay = jax.nn.sigmoid(vectors[3:4])
    table = lax.dynamic_slice_in_dim(vectors[4], me * slot_size, slot_size, 0)
    table = table.reshape(NBUCKET, heads).T
    kv_pieces = [gather_rel(kv_blocks[0])]

    w_mlp = lax.all_gather(after(local_mlp, q), "shard", axis=0, tiled=True)

    ids_row = piece_ids.reshape(blocks, 1, BLK)
    zero_arr = jnp.zeros((1,), jnp.int32)
    gain_s = gains[2:3]
    got, flag = jnp.zeros((part, width), LOW), zero_arr
    for round_index in range(run_count):
        state = start
        states, normeds, updates = [], [], []
        for b in range(blocks):
            if b == len(kv_pieces):
                kv_pieces.append(gather_rel(after(kv_blocks[b], *kv_pieces[-1][2::2]), state))
            if round_index + b == run_count:
                state = after(state, outer, *tout_far)
            state, pair, update, following, low = chain_forward(
                zero_arr if b else flag, state, got, gain_s, decay, kv_pieces[b], chain_w,
                round_index > 0,
            )
            if round_index + b == 0:
                outer = passed_along(after(kv_blocks[-1], low), "context", 1)
            states.append(state)
            normeds.append(pair)
            updates.append(update)
            state = following
        if round_index + 1 < run_count:
            got, flag = passed_along(low, "context", 1), run_arr
            if round_index == 0:
                grad_far = far_pieces(after(cotangent[0], *kv_pieces[-1][2::2]))
                tout_far = far_pieces(after(w_tout, *grad_far))
                got = after(got, *grad_far)
    units = mlp_in.shape[1]
    w_in, w_out = (w_mlp, units, 0), (w_mlp, units, 1)
    normed_s = stacked([pair for pair in normeds[::2]])[: blocks * part]
    state_pieces = gather_rel(normed_s, updates[-1])
    sq, skv = proj(state_pieces, [w_sq, w_skv])
    sq = sq.reshape(size, blocks, part, span)
    skv = skv.reshape(size, blocks, part, 2 * span)

    mixed, lse = attend(run_arr, table, q, kv, outer, skv, ids_row)
    grad_pieces = chip_pieces(grad_far, mixed)
    tout_pieces = chip_pieces(tout_far, mixed)
    mixed_parts = cut(mixed, me)
    residual, normed_m, squares = branch_out(own, gains[1:2], exchange_rel(mixed_parts), tout_pieces)

    (grad_hidden,) = proj([after(piece, normed_m) for piece in grad_pieces], [w_out])
    mlp_pieces = gather_rel(normed_m, grad_hidden)
    hidden, grad_pre, *parts = feed(w_in, grad_hidden, mlp_pieces)
    sums, sends = reduce_first(parts)
    grad_w_mlp = weight_grad([(mlp_pieces, after(grad_pre, *sends)), (grad_pieces, hidden)])
    terms = reduce_last(sums, sends, grad_w_mlp)
    mlp_mine = scatter_rows(after(grad_w_mlp, *terms))

    grad_res, grad_branch, grad_gain_m, *gmix_parts = branch_back(
        cotangent[0], residual, gains[1:2], terms, tout_pieces
    )
    gmix = place(exchange_rel(gmix_parts), me)
    gq, gcur, gprev, gs, gtab = attend_back(
        run_arr, table, q, kv, outer, skv, ids_row, gmix, lse
    )
    branch_pieces = gather_rel(after(grad_branch, gmix), gq)
    gs = after(gs, branch_pieces[-2])
    outer_back = passed_along(gprev[:BLK], "context", -1)

    gs = gs.reshape(-1, 2 * span)
    sums, sends = reduce_first(back(zero_arr, [gs], [w_skv]))
    parts = back(zero_arr, [after(hidden, *sends)], [w_out])
    state_terms = reduce_last(sums, sends, parts[0])
    state_terms[0] = after(state_terms[0], outer_back)
    sums, sends = reduce_first(parts)
    branch_m = reduce_last(sums, [after(send, *state_terms) for send in sends])

    got, flag = jnp.zeros((part, width), LOW), zero_arr
    not_last = (run_pos != run_count - 1).astype(jnp.int32)[None]
    for round_index in range(run_count):
        carry = jnp.zeros_like(start)
        gups = [None] * blocks
        chain_small = jnp.zeros((2, width), F32)
        for b in reversed(range(blocks)):
            carry, low, pair, row_sums = chain_backward(
                flag if b == blocks - 1 else zero_arr, carry, got, gain_s, decay, states[b], normed_s,
                updates[b], b, state_terms, kv_pieces[b], chain_w, round_index > 0,
            )
            chain_small = chain_small + row_sums
            gups[b] = pair
        if round_index + 1 < run_count:
            got, flag = passed_along(low, "context", -1), not_last
            if round_index == 0:
                grad_w_early = weight_grad(
                    [
                        ([normed_a], after(gq, carry)),
                        (state_pieces, gs),
                        (branch_pieces, jnp.concatenate(mixed_parts, axis=0)),
                    ]
                )
                got = came = after(got, grad_w_early, *branch_m)
    gup_all = stacked([gups[b] for b in range(blocks - 1, 0, -2)][::-1])
    grad_start = jnp.where(run_pos == 0, carry, 0.0).astype(LOW)
    branch_m = added(branch_m)
    output = (residual + branch_m).astype(LOW)
    mlp_halves = [after(mlp_mine[:, i * units : (i + 1) * units], gup_all) for i in range(2)]
    mlp_got = [swap(mlp_halves[0], "context", 1)]
    gup_pieces = gather_rel(gup_all, carry, mlp_got[0])
    early_mine = scatter_rows(after(grad_w_early, came))
    (gsmix,) = proj(gup_pieces, [w_sout])
    gsmix = gsmix.reshape(size, blocks, part, span)
    gkv, gsq, smix = state_back(sq, kv, gsmix, gcur, gprev, outer_back)
    grad_w_late = weight_grad(
        [([normed_a], gkv), (state_pieces, gsq.reshape(-1, span)), (gup_pieces, smix.reshape(-1, span))],
        [grad_start.T],
    )
    mlp_got.append(swap(after(mlp_halves[1], grad_w_late), "context", 1))
    early_got = swap(after(early_mine, grad_w_late), "context", 1)
    late_mine = scatter_rows(grad_w_late)
    g_in, g_out = (
        half.astype(F32) + other.astype(F32) for half, other in zip(mlp_halves, mlp_got, strict=True)
    )
    g_early = early_mine.astype(F32) + early_got.astype(F32)
    g_late = late_mine.astype(F32) + swap(late_mine, "context", 1).astype(F32)

    *parts, gain_sums = back(
        me_arr,
        [gq, after(gkv, grad_w_late)],
        [(w_tok, span, 2), (w_tok, 2 * span, 0)],
        normed_a,
    )
    grad_gain_a = (gain_sums / gains[0:1])[0]
    inputs = own.astype(F32)
    terms = reduce_last(*reduce_first(parts))
    grad_normed_a = added(terms)
    grad_tokens = (grad_res + rms_back(inputs, gains[0], grad_normed_a)).astype(LOW)

    def by_head(array):
        return array.reshape(array.shape[0], heads, -1)

    g_tok = jnp.concatenate([by_head(g_early[:, :span]), by_head(g_late[:, : 2 * span])], axis=2)
    g_state = jnp.concatenate(
        [by_head(g_late[:, 2 * span : 3 * span]), by_head(g_early[:, span : 3 * span])], axis=2
    )
    g_tout = g_early[:, 3 * span :].T.reshape(heads, HS, -1)
    g_sout = g_late[:, 3 * span : 4 * span].T.reshape(heads, HS, -1)

    squares = jnp.concatenate([jnp.sum(squares, axis=1), jnp.sum(branch_m * branch_m)[None]])
    slot = gtab[:, 0, :NBUCKET].reshape(-1)
    slots = lax.dynamic_update_slice_in_dim(
        jnp.zeros((size * slot.size,), F32), slot, me * slot.size, 0
    )
    tail = jnp.concatenate([slots, squares])
    tail = jnp.pad(tail, (0, width - tail.size))
    grad_decay = chain_small[1] * (decay * (1.0 - decay))[0]
    sums = sum_all(
        jnp.stack([grad_gain_a, grad_gain_m[0], chain_small[0], grad_decay, tail]),
        early_got,
        mlp_got[1],
        *terms,
    )
    place_at = (shard_pos * size + me) * cols
    mine = lax.dynamic_slice_in_dim(sums[:4], place_at, cols, 1)
    table_sum = lax.dynamic_slice_in_dim(sums[4], me * slot.size, slot.size, 0)
    table_sum = table_sum.reshape(heads, NBUCKET).T
    g_table = lax.dynamic_slice_in_dim(table_sum, shard_pos * bias_rows, bias_rows, 0)
    entries = own.size * shard_count * run_count * size
    first = size * slot.size
    rms_out = jnp.sqrt(sums[4, first : first + 3] / entries)

    return (
        output[None],
        grad_tokens[None],
        g_tok,
        g_state,
        g_tout,
        g_sout,
        g_in,
        g_out.T,
        g_table,
        g_late[:, 4 * span :].T,
        mine[:3],
        mine[3],
        rms_out,
    )


def solution(mesh):
    return jax.shard_map(
        shards,
        mesh=mesh,
        in_specs=(
            P("shard", ("context", "tensor"), None),
            P("shard", "context"),
            P("shard", "tensor", None),
            P("shard", "tensor", None),
            P("tensor", None, "shard"),
            P("tensor", None, "shard"),
            P("shard", "tensor"),
            P("tensor", "shard"),
            P("shard", "tensor"),
            P("tensor", "shard"),
            P(None, ("shard", "tensor")),
            P(("shard", "tensor")),
            P("shard", ("context", "tensor"), None),
        ),
        out_specs=(
            P("shard", ("context", "tensor"), None),
            P("shard", ("context", "tensor"), None),
            P("shard", "tensor", None),
            P("shard", "tensor", None),
            P("tensor", None, "shard"),
            P("tensor", None, "shard"),
            P("shard", "tensor"),
            P("tensor", "shard"),
            P("shard", "tensor"),
            P("tensor", "shard"),
            P(None, ("shard", "tensor")),
            P(("shard", "tensor")),
            P(),
        ),
        check_vma=False,
    )
```

```python
import functools

import jax
import jax.numpy as jnp
from jax import lax
from jax.experimental import pallas as pl
from jax.experimental.pallas import tpu as pltpu
from jax.sharding import PartitionSpec as P

HS = 128
BLK = 512
NBUCKET = 32
EDGES = (12, 16, 23, 32, 46, 64, 91)
LOW = jnp.bfloat16
F32 = jnp.float32
SCALE = HS ** (-0.5)
EPS = 1e-06
DIAG = 3 * BLK
SMALL = 16
PACE = 0.5


def mm(a, b, ca, cb):
    return lax.dot_general(a, b, (((ca,), (cb,)), ((), ())), preferred_element_type=F32)


def whole():
    return pl.BlockSpec(memory_space=pltpu.VMEM)


def columns(weight):
    _, width, index = weight
    return pl.BlockSpec((weight[0].shape[0], width), lambda *_: (0, index))


def scalars():
    return pl.BlockSpec(memory_space=pltpu.SMEM)


def params(grid_rank=0, mib=40):
    limit = mib * 1024 * 1024
    if grid_rank:
        return pltpu.CompilerParams(
            dimension_semantics=("arbitrary",) * grid_rank, vmem_limit_bytes=limit
        )
    return pltpu.CompilerParams(vmem_limit_bytes=limit)


def lasts(microseconds):
    return pl.CostEstimate(
        flops=int(microseconds * PACE * 1.1e9), bytes_accessed=int(microseconds * PACE * 3e6), transcendentals=0
    )


def rms_scale(v):
    return lax.rsqrt(jnp.mean(v * v, axis=-1, keepdims=True) + EPS)


def assemble_kernel(count, pos_ref, *refs):
    pieces, other_ref, outs = refs[:count], refs[count], refs[count + 1 :]
    part = pieces[0].shape[0]
    for s in range(count):
        base = (pos_ref[0] ^ s) * (2 * part)
        mine = pl.multiple_of(base + pos_ref[1] * part, part)
        theirs = pl.multiple_of(base + (1 - pos_ref[1]) * part, part)
        first = 0
        for out_ref in outs:
            last = first + out_ref.shape[1]
            out_ref[pl.ds(mine, part), :] = pieces[s][:, first:last]
            out_ref[pl.ds(theirs, part), :] = other_ref[s, :, first:last]
            first = last


def assemble(pos, pieces, other, widths):
    part, cols = pieces[0].shape
    rows = 2 * part * len(pieces)
    return pl.pallas_call(
        functools.partial(assemble_kernel, len(pieces)),
        out_shape=tuple(jax.ShapeDtypeStruct((rows, w), LOW) for w in widths),
        in_specs=[scalars()] + [whole()] * (len(pieces) + 1),
        out_specs=(whole(),) * len(widths),
        compiler_params=params(mib=16),
        cost_estimate=lasts(1.5),
        name="assemble",
    )(pos, *pieces, other)


def weight_grad_kernel(counts, extras, *refs):
    out_ref = refs[-1]
    at = 0
    first = 0
    for count in counts:
        right = refs[at + count]
        total = None
        row = 0
        for left in refs[at : at + count]:
            term = mm(left[...], right[row : row + left.shape[0], :], 0, 0)
            row += left.shape[0]
            total = term if total is None else total + term
        out_ref[:, first : first + right.shape[1]] = total.astype(LOW)
        first += right.shape[1]
        at += count + 1
    for extra in refs[at : at + extras]:
        out_ref[:, first : first + extra.shape[1]] = extra[...]
        first += extra.shape[1]


def weight_grad(pairs, extras=()):
    width = pairs[0][0][0].shape[1]
    tile = 256
    specs, args = [], []
    for lefts, right in pairs:
        specs += [pl.BlockSpec((left.shape[0], tile), lambda i: (0, i)) for left in lefts]
        specs.append(pl.BlockSpec(right.shape, lambda i: (0, 0)))
        args += list(lefts) + [right]
    specs += [pl.BlockSpec((tile, extra.shape[1]), lambda i: (i, 0)) for extra in extras]
    cols = sum(right.shape[1] for _, right in pairs) + sum(extra.shape[1] for extra in extras)
    return pl.pallas_call(
        functools.partial(weight_grad_kernel, [len(lefts) for lefts, _ in pairs], len(extras)),
        grid=(width // tile,),
        out_shape=jax.ShapeDtypeStruct((width, cols), LOW),
        in_specs=specs,
        out_specs=pl.BlockSpec((tile, cols), lambda i: (i, 0)),
        compiler_params=params(1, 32),
        cost_estimate=lasts(6),
        name="weight_grad",
    )(*args, *extras)


def token_proj_kernel(count, shards, blocks, me_ref, w_ref, *refs):
    pieces, small = refs[:count], refs[count : count + shards]
    q_ref, normed_ref, vec_ref, kv_ref, *kv_refs = refs[count + shards :]
    span = q_ref.shape[1]
    vectors = small[0][...].astype(F32)
    for piece in small[1:]:
        vectors = vectors + piece[...].astype(F32)
    vec_ref[...] = vectors
    gain = vectors[0:1]
    rows = pieces[0].shape[0] - SMALL
    for m in range(count):
        start = pl.multiple_of((me_ref[0] ^ m) * rows, rows)
        v = pieces[m][:rows, :].astype(F32)
        normed = (v * rms_scale(v) * gain).astype(LOW)
        normed_ref[pl.ds(start, rows), :] = normed
        kv_ref[pl.ds(start, rows), :] = mm(normed, w_ref[:, : 2 * span], 1, 0).astype(LOW)
        q_ref[pl.ds(start, rows), :] = mm(normed, w_ref[:, 2 * span :], 1, 0).astype(LOW)
    for b in range(blocks):
        kv_refs[b][...] = kv_ref[b * BLK : (b + 1) * BLK, :]


def token_proj(me, pieces, small, weight, blocks):
    width, cols = weight.shape
    span = cols // 3
    step = pieces[0].shape[0]
    rows = (step - SMALL) * len(pieces)
    return pl.pallas_call(
        functools.partial(token_proj_kernel, len(pieces), len(small), blocks),
        out_shape=(
            jax.ShapeDtypeStruct((rows, span), LOW),
            jax.ShapeDtypeStruct((rows, width), LOW),
            jax.ShapeDtypeStruct((SMALL, width), F32),
            jax.ShapeDtypeStruct((rows, 2 * span), LOW),
        )
        + (jax.ShapeDtypeStruct((BLK, 2 * span), LOW),) * blocks,
        in_specs=[scalars(), whole()] + [whole()] * (len(pieces) + len(small)),
        out_specs=(whole(),) * (4 + blocks),
        compiler_params=params(mib=56),
        cost_estimate=lasts(5),
        name="token_proj",
    )(me, weight, *pieces, *small)


def proj_kernel(count, weights, *refs):
    pieces, ws, outs = refs[:count], refs[count : count + weights], refs[count + weights :]
    rows = pieces[0].shape[0]
    for m in range(count):
        for w, out in zip(ws, outs, strict=True):
            out[m * rows : (m + 1) * rows, :] = mm(pieces[m][...], w[...], 1, 0).astype(LOW)


def proj(pieces, weights, mib=24):
    rows = pieces[0].shape[0] * len(pieces)
    return pl.pallas_call(
        functools.partial(proj_kernel, len(pieces), len(weights)),
        grid=(1,),
        out_shape=tuple(jax.ShapeDtypeStruct((rows, w[1]), LOW) for w in weights),
        in_specs=[whole()] * len(pieces) + [columns(w) for w in weights],
        out_specs=(whole(),) * len(weights),
        compiler_params=params(1, mib),
        cost_estimate=lasts(3),
        name="proj",
    )(*pieces, *[w[0] for w in weights])


def back_kernel(count, gained, size, me_ref, *refs):
    outs = refs[2 * count + gained : 2 * count + gained + size]
    total = None
    for i in range(count):
        term = mm(refs[i][...], refs[count + i][...], 1, 1)
        total = term if total is None else total + term
    step = pl.program_id(0)
    if gained:
        sums = jnp.sum(total * refs[2 * count][...].astype(F32), axis=0, keepdims=True)
        refs[-1][...] = sums + jnp.where(step == 0, 0.0, refs[-1][...])
    total = total.astype(LOW)
    for m in range(size):

        @pl.when(step == m)
        def _(m=m):
            outs[m][...] = total


def back(me, grads, weights, normed=None):
    rows, width = grads[0].shape[0], weights[0][0].shape[0]
    size = lax.axis_size("tensor")
    tile = rows // size
    extra = [] if normed is None else [normed]
    grid_spec = pltpu.PrefetchScalarGridSpec(
        num_scalar_prefetch=1,
        grid=(size,),
        in_specs=[pl.BlockSpec((tile, g.shape[1]), lambda i, me_ref: (i ^ me_ref[0], 0)) for g in grads]
        + [columns(w) for w in weights]
        + [pl.BlockSpec((tile, width), lambda i, me_ref: (i ^ me_ref[0], 0)) for _ in extra],
        out_specs=(pl.BlockSpec((tile, width), lambda i, me_ref: (0, 0)),) * size
        + (pl.BlockSpec((1, width), lambda i, me_ref: (0, 0)),) * len(extra),
    )
    return pl.pallas_call(
        functools.partial(back_kernel, len(grads), len(extra), size),
        grid_spec=grid_spec,
        out_shape=(jax.ShapeDtypeStruct((tile, width), LOW),) * size
        + (jax.ShapeDtypeStruct((1, width), F32),) * len(extra),
        compiler_params=params(1, 24),
        cost_estimate=lasts(3),
        name="back",
    )(me, *grads, *[w[0] for w in weights], *extra)


def branch_kernel(count, own_ref, gain_ref, *refs):
    parts, weights = refs[:count], refs[count : 2 * count]
    residual_ref, normed_ref, sums_ref = refs[2 * count :]
    branch = None
    for part, weight in zip(parts, weights, strict=True):
        term = mm(part[...], weight[...], 1, 1)
        branch = term if branch is None else branch + term
    own = own_ref[...].astype(F32)
    residual = own + branch
    residual_ref[...] = residual
    normed_ref[...] = (residual * rms_scale(residual) * gain_ref[...]).astype(LOW)
    sums_ref[0:1, :] = jnp.sum(own * own, axis=0, keepdims=True)
    sums_ref[1:2, :] = jnp.sum(branch * branch, axis=0, keepdims=True)


def branch_out(own, gain, parts, weights):
    rows, width = own.shape
    return pl.pallas_call(
        functools.partial(branch_kernel, len(parts)),
        out_shape=(
            jax.ShapeDtypeStruct((rows, width), F32),
            jax.ShapeDtypeStruct((rows, width), LOW),
            jax.ShapeDtypeStruct((2, width), F32),
        ),
        in_specs=[whole()] * (2 + 2 * len(parts)),
        out_specs=(whole(),) * 3,
        compiler_params=params(mib=56),
        cost_estimate=lasts(3),
        name="branch_out",
    )(own, gain, *parts, *weights)


def branch_back_kernel(count, sums, cot_ref, residual_ref, gain_ref, *refs):
    terms, weights, outs = refs[:sums], refs[sums : sums + count], refs[sums + count :]
    grad_ref, low_ref, gain_sum_ref, parts = outs[0], outs[1], outs[2], outs[3:]
    grad = terms[0][...].astype(F32)
    for term in terms[1:]:
        grad = grad + term[...].astype(F32)
    residual = residual_ref[...]
    r = rms_scale(residual)
    unit = residual * r
    gain_sum_ref[...] = jnp.sum(grad * unit, axis=0, keepdims=True)
    scaled = grad * gain_ref[...]
    grad = cot_ref[...].astype(F32) + r * (
        scaled - unit * jnp.mean(scaled * unit, axis=-1, keepdims=True)
    )
    grad_ref[...] = grad
    low = grad.astype(LOW)
    low_ref[...] = low
    for part, weight in zip(parts, weights, strict=True):
        part[...] = mm(low, weight[...], 1, 0).astype(LOW)


def branch_back(cot, residual, gain, terms, weights):
    rows, width = cot.shape
    span = weights[0].shape[1]
    return pl.pallas_call(
        functools.partial(branch_back_kernel, len(weights), len(terms)),
        out_shape=(
            jax.ShapeDtypeStruct((rows, width), F32),
            jax.ShapeDtypeStruct((rows, width), LOW),
            jax.ShapeDtypeStruct((1, width), F32),
        )
        + (jax.ShapeDtypeStruct((rows, span), LOW),) * len(weights),
        in_specs=[whole()] * (3 + len(terms) + len(weights)),
        out_specs=(whole(),) * (3 + len(weights)),
        compiler_params=params(mib=56),
        cost_estimate=lasts(2.5),
        name="branch_back",
    )(cot, residual, gain, *terms, *weights)


def gelu_parts(pre):
    half = 0.5 * (1.0 + lax.erf(pre * 0.7071067811865476))
    density = jnp.exp(pre * pre * -0.5) * 0.3989422804014327
    return half, density


def feed_kernel(count, w_ref, ghid_ref, *refs):
    pieces, (hidden_ref, gpre_ref), outs = refs[:count], refs[count : count + 2], refs[count + 2 :]
    rows = pieces[0].shape[0]
    for m in range(count):
        at = slice(m * rows, (m + 1) * rows)
        pre = mm(pieces[m][...], w_ref[...], 1, 0)
        half, density = gelu_parts(pre)
        hidden_ref[at, :] = (pre * half).astype(LOW)
        gpre = ((half + pre * density) * ghid_ref[at, :].astype(F32)).astype(LOW)
        gpre_ref[at, :] = gpre
        outs[m][...] = mm(gpre, w_ref[...], 1, 1).astype(LOW)


def feed(w_in, ghid, pieces):
    width, units = w_in[0].shape[0], w_in[1]
    own, count = pieces[0].shape[0], len(pieces)
    rows = own * count
    return pl.pallas_call(
        functools.partial(feed_kernel, count),
        grid=(1,),
        out_shape=(
            jax.ShapeDtypeStruct((rows, units), LOW),
            jax.ShapeDtypeStruct((rows, units), LOW),
        )
        + (jax.ShapeDtypeStruct((own, width), LOW),) * count,
        in_specs=[columns(w_in)] + [whole()] * (1 + count),
        out_specs=(whole(),) * (2 + count),
        compiler_params=params(1, 32),
        cost_estimate=lasts(7),
        name="feed",
    )(w_in[0], ghid, *pieces)


def column_softmax(scores):
    peak = jnp.max(scores, axis=0, keepdims=True)
    exponent = jnp.exp(scores - peak)
    return exponent * (1.0 / jnp.sum(exponent, axis=0, keepdims=True))


def chain_operands(count, brought, refs):
    kv, w = refs[:count], refs[count : 2 * count]
    if not brought:
        return kv, w, [(), ()] * count
    here, sems = refs[2 * count : 4 * count], refs[4 * count]
    copies = []
    for m in range(count):
        copies.append((pltpu.make_async_copy(w[m], here[count + m], sems.at[m]),))
        copies.append((pltpu.make_async_copy(kv[m], here[m], sems.at[count + m]),))
    for (copy,) in copies:
        copy.start()
    return here[:count], here[count:], copies


def chain_specs(kv, weights, brought):
    if not brought:
        return [whole()] * (2 * len(kv)), [], 24
    scratch = [pltpu.VMEM(array.shape, LOW) for array in list(kv) + list(weights)]
    scratch.append(pltpu.SemaphoreType.DMA((2 * len(kv),)))
    return [pl.BlockSpec(memory_space=pl.ANY)] * (2 * len(kv)), scratch, 56


def ready(copies):
    for copy in copies:
        copy.wait()


def chosen(flag_ref, mine_ref, got_ref):
    return jnp.where(flag_ref[0] != 0, got_ref[...].astype(F32), mine_ref[...])


def head_keys(kv, h):
    return kv[:, 2 * h * HS : (2 * h + 1) * HS]


def head_values(kv, h):
    return kv[:, (2 * h + 1) * HS : 2 * (h + 1) * HS]


def stacked(parts):
    return parts[0] if len(parts) == 1 else jnp.concatenate(parts, axis=0)


def chain_forward_kernel(
    count, heads, brought, flag_ref, gain_ref, dec_ref, mine_ref, got_ref, *refs
):
    outs = refs[2 * count : 2 * count + 5]
    state_ref, pair_ref, update_ref, next_ref, low_ref = outs
    kv, w, copies = chain_operands(count, brought, refs[: 2 * count] + refs[2 * count + 5 :])
    span = heads * HS
    dec = dec_ref[...]
    gain = gain_ref[...]
    state = chosen(flag_ref, mine_ref, got_ref)
    rows = state.shape[0]
    state_ref[...] = state
    normed = (state * rms_scale(state) * gain).astype(LOW)
    pair_ref[:rows, :] = normed
    queries = []
    for m in range(count):
        ready(copies[2 * m])
        queries.append(mm(normed, w[m][:, :span], 1, 0).astype(LOW))
    scores = []
    for m in range(count):
        ready(copies[2 * m + 1])
        for h in range(heads):
            scores.append(mm(head_keys(kv[m], h), queries[m][:, h * HS : (h + 1) * HS], 1, 1) * SCALE)
    weights = [column_softmax(score).astype(LOW) for score in scores]
    mixed = [
        stacked([mm(head_values(kv[m], h), weights[m * heads + h], 0, 0) for h in range(heads)])
        for m in range(count)
    ]
    update = None
    for m in range(count):
        term = mm(mixed[m].T.astype(LOW), w[m][:, span:], 1, 1)
        update = term if update is None else update + term
    update_ref[...] = update
    state = dec * state + (1.0 - dec) * update
    next_ref[...] = state
    low_ref[...] = state.astype(LOW)
    pair_ref[rows:, :] = (state * rms_scale(state) * gain).astype(LOW)


def chain_forward(flag, mine, got, gain, dec, kv, weights, brought):
    count = len(kv)
    rows, width = mine.shape
    heads = kv[0].shape[1] // (2 * HS)
    full = jax.ShapeDtypeStruct((rows, width), F32)
    specs, scratch, mib = chain_specs(kv, weights, brought)
    return pl.pallas_call(
        functools.partial(chain_forward_kernel, count, heads, brought),
        out_shape=(
            full,
            jax.ShapeDtypeStruct((2 * rows, width), LOW),
            full,
            full,
            jax.ShapeDtypeStruct((rows, width), LOW),
        ),
        in_specs=[scalars()] + [whole()] * 4 + specs,
        out_specs=(whole(),) * 5,
        scratch_shapes=scratch,
        compiler_params=params(mib=mib),
        cost_estimate=lasts(6.5),
        name="chain_forward",
    )(flag, gain, dec, mine, got, *kv, *weights)


def chain_backward_kernel(
    count, heads, terms, brought, flag_ref, gain_ref, dec_ref, state_ref, normed_ref, update_ref, mine_ref,
    got_ref, *refs
):
    gkv, refs = refs[:terms], refs[terms:]
    next_ref, low_ref, pair_ref, small_ref = refs[2 * count : 2 * count + 4]
    kv, w, copies = chain_operands(count, brought, refs[: 2 * count] + refs[2 * count + 4 :])
    span = heads * HS
    dec = dec_ref[...]
    gain = gain_ref[...]
    carry = chosen(flag_ref, mine_ref, got_ref)
    rows = carry.shape[0]
    state = state_ref[...]
    small_ref[1:2, :] = jnp.sum(carry * (state - update_ref[...]), axis=0, keepdims=True)
    gup = ((1.0 - dec) * carry).astype(LOW)
    pair_ref[rows:, :] = gup
    normed = normed_ref[...]
    queries, gmixes = [], []
    for m in range(count):
        ready(copies[2 * m])
        queries.append(mm(normed, w[m][:, :span], 1, 0).astype(LOW))
        gmixes.append(mm(gup, w[m][:, span:], 1, 0).astype(LOW))
    scores, grads = [], []
    for m in range(count):
        ready(copies[2 * m + 1])
        for h in range(heads):
            at = slice(h * HS, (h + 1) * HS)
            scores.append(mm(head_keys(kv[m], h), queries[m][:, at], 1, 1) * SCALE)
            grads.append(mm(head_values(kv[m], h), gmixes[m][:, at], 1, 1))
    lows = []
    for score, grad in zip(scores, grads, strict=True):
        weights = column_softmax(score)
        inner = jnp.sum(grad * weights, axis=0, keepdims=True)
        lows.append((weights * (grad - inner)).astype(LOW))
    grad_normed = gkv[0][...].astype(F32)
    for term in gkv[1:]:
        grad_normed = grad_normed + term[...].astype(F32)
    grad_queries = [
        stacked([mm(head_keys(kv[m], h), lows[m * heads + h], 0, 0) * SCALE for h in range(heads)])
        for m in range(count)
    ]
    for m in range(count):
        grad_normed = grad_normed + mm(grad_queries[m].T.astype(LOW), w[m][:, :span], 1, 1)
    r = rms_scale(state)
    unit = state * r
    scaled = grad_normed * gain
    small_ref[0:1, :] = jnp.sum(grad_normed * unit, axis=0, keepdims=True)
    carry = dec * carry + r * (scaled - unit * jnp.mean(scaled * unit, axis=-1, keepdims=True))
    next_ref[...] = carry
    low_ref[...] = carry.astype(LOW)
    pair_ref[:rows, :] = ((1.0 - dec) * carry).astype(LOW)


def chain_backward(flag, mine, got, gain, dec, state, normed, update, b, gkv, kv, weights, brought):
    count = len(kv)
    rows, width = state.shape
    heads = kv[0].shape[1] // (2 * HS)
    specs, scratch, mib = chain_specs(kv, weights, brought)
    return pl.pallas_call(
        functools.partial(chain_backward_kernel, count, heads, len(gkv), brought),
        grid=(1,),
        out_shape=(
            jax.ShapeDtypeStruct((rows, width), F32),
            jax.ShapeDtypeStruct((rows, width), LOW),
            jax.ShapeDtypeStruct((2 * rows, width), LOW),
            jax.ShapeDtypeStruct((2, width), F32),
        ),
        in_specs=[scalars()]
        + [whole()] * 3
        + [pl.BlockSpec((rows, width), lambda i: (b, 0))]
        + [whole()] * 3
        + [pl.BlockSpec((rows, width), lambda i: (b, 0)) for _ in gkv]
        + specs,
        out_specs=(whole(),) * 4,
        scratch_shapes=scratch,
        compiler_params=params(1, mib),
        cost_estimate=lasts(8.3),
        name="chain_backward",
    )(flag, gain, dec, state, normed, update, mine, got, *gkv, *kv, *weights)


def bucket_tile():
    lane = lax.broadcasted_iota(jnp.int32, (8, DIAG), 1)
    row = lax.broadcasted_iota(jnp.int32, (8, DIAG), 0)
    diff = lane - row
    diff = jnp.where(diff < 0, diff + DIAG, diff)
    offset = jnp.where(diff < BLK, diff, diff - DIAG) + BLK
    distance = jnp.abs(offset)
    far = jnp.full((8, DIAG), 8, jnp.int32)
    for edge in EDGES:
        far = far + (distance >= edge).astype(jnp.int32)
    near = jnp.where(distance < 8, distance, far)
    return jnp.where(offset >= 0, near, near + NBUCKET // 2)


def fill_bias(table_ref, h, bias_ref):
    bucket = bucket_tile()
    base = jnp.zeros((8, DIAG), F32)
    for k in range(NBUCKET):
        base = jnp.where(bucket == k, table_ref[h, k], base)
    for r in range(16):
        rolled = pltpu.roll(base, 8 * r, 1) if r else base
        wide = jnp.concatenate([rolled, rolled[:, :BLK]], axis=1)
        for k in range(2 * BLK // 128):
            start = (DIAG - 128 * k) % DIAG
            row = 8 * (16 * k + r)
            bias_ref[row : row + 8, :] = wide[:, start : start + BLK]


def collapse_bias(grad_ref, out_ref):
    total = jnp.zeros((8, DIAG), F32)
    for r in range(16):
        acc = [jnp.zeros((8, 128), F32)] * (DIAG // 128)
        for k in range(2 * BLK // 128):
            row = 8 * (16 * k + r)
            for c in range(BLK // 128):
                at = (c - k) % (DIAG // 128)
                acc[at] = acc[at] + grad_ref[row : row + 8, c * 128 : (c + 1) * 128]
        acc = jnp.concatenate(acc, axis=1)
        total = total + (pltpu.roll(acc, DIAG - 8 * r, 1) if r else acc)
    bucket = bucket_tile()
    lane = lax.broadcasted_iota(jnp.int32, (8, HS), 1)
    out = jnp.zeros((8, HS), F32)
    for k in range(NBUCKET):
        out = jnp.where(lane == k, jnp.sum(jnp.where(bucket == k, total, 0.0)), out)
    out_ref[...] = out


def current_mask(ids_ref):
    key = lax.broadcasted_iota(jnp.int32, (BLK, BLK), 0)
    query = lax.broadcasted_iota(jnp.int32, (BLK, BLK), 1)
    ids = ids_ref[...].astype(F32)
    column = jnp.broadcast_to(ids, (HS, BLK)).T[:, :1]
    return (key <= query) | ((column == ids) & (ids > 0.0))


def attend_kernel(
    run_ref, table_ref, q_ref, kc_ref, vc_ref, kp_ref, vp_ref, ko_ref, vo_ref, ks_ref, vs_ref,
    row_ref, out_ref, lse_ref, bias_ref, score_ref,
):
    h = pl.program_id(0)
    b = pl.program_id(1)

    @pl.when(b == 0)
    def _():
        fill_bias(table_ref, h, bias_ref)

    q = q_ref[...]
    first = b == 0
    keys = (
        ks_ref[...].reshape(BLK, HS),
        jnp.where(first, ko_ref[...], kp_ref[...]),
        kc_ref[...],
    )
    values = (
        vs_ref[...].reshape(BLK, HS),
        jnp.where(first, vo_ref[...], vp_ref[...]),
        vc_ref[...],
    )
    prior_ok = (run_ref[0] > 0) | (b > 0)
    score = mm(keys[0], q, 1, 1) * SCALE
    score_ref[0] = score
    peak = jnp.max(score, axis=0, keepdims=True)
    score = mm(keys[1], q, 1, 1) * SCALE + bias_ref[:BLK]
    score = jnp.where(prior_ok, score, -1e30)
    score_ref[1] = score
    peak = jnp.maximum(peak, jnp.max(score, axis=0, keepdims=True))
    score = mm(keys[2], q, 1, 1) * SCALE + bias_ref[BLK:]
    score = jnp.where(current_mask(row_ref), score, -1e30)
    score_ref[2] = score
    peak = jnp.maximum(peak, jnp.max(score, axis=0, keepdims=True))
    total = jnp.zeros((1, BLK), F32)
    for c in range(3):
        exponent = jnp.exp(score_ref[c] - peak)
        score_ref[c] = exponent
        total = total + jnp.sum(exponent, axis=0, keepdims=True)
    inverse = 1.0 / total
    mixed = jnp.zeros((HS, BLK), F32)
    for c in range(3):
        mixed = mixed + mm(values[c], (score_ref[c] * inverse).astype(LOW), 0, 0)
    out_ref[...] = mixed.T.astype(LOW)
    lse_ref[...] = peak + jnp.log(total)


def attend_specs(heads, pieces, part, blocks):
    def at(col):
        return pl.BlockSpec((BLK, HS), lambda h, b: (b, col(h)))

    def before(col):
        return pl.BlockSpec((BLK, HS), lambda h, b: (jnp.maximum(b - 1, 0), col(h)))

    def outer(col):
        return pl.BlockSpec((BLK, HS), lambda h, b: (0, col(h)))

    def state(col):
        return pl.BlockSpec((pieces, None, part, HS), lambda h, b: (0, b, 0, col(h)))

    key, value = (lambda h: 2 * h), (lambda h: 2 * h + 1)
    return [
        scalars(),
        scalars(),
        at(lambda h: h),
        at(key),
        at(value),
        before(key),
        before(value),
        outer(key),
        outer(value),
        state(lambda h: 2 * h),
        state(lambda h: 2 * h + 1),
        pl.BlockSpec((None, 1, BLK), lambda h, b: (b, 0, 0)),
    ]


def attend(run, table, q, kv, outer, sproj, ids_row):
    rows = q.shape[0]
    heads = q.shape[1] // HS
    pieces, blocks, part, _ = sproj.shape
    return pl.pallas_call(
        attend_kernel,
        grid=(heads, blocks),
        out_shape=(
            jax.ShapeDtypeStruct((rows, heads * HS), LOW),
            jax.ShapeDtypeStruct((heads, blocks, 1, BLK), F32),
        ),
        in_specs=attend_specs(heads, pieces, part, blocks),
        out_specs=(
            pl.BlockSpec((BLK, HS), lambda h, b: (b, h)),
            pl.BlockSpec((None, None, 1, BLK), lambda h, b: (h, b, 0, 0)),
        ),
        scratch_shapes=[pltpu.VMEM((2 * BLK, BLK), F32), pltpu.VMEM((3, BLK, BLK), F32)],
        compiler_params=params(2, 20),
        cost_estimate=lasts(9.7),
        name="attend",
    )(run, table, q, kv, kv, kv, kv, outer, outer, sproj, sproj, ids_row)


def attend_back_kernel(
    run_ref, table_ref, q_ref, kc_ref, vc_ref, kp_ref, vp_ref, ko_ref, vo_ref, ks_ref, vs_ref,
    row_ref, gmix_ref, lse_ref,
    gq_ref, gcur_ref, gprev_ref, gs_ref, gtab_ref,
    bias_ref, gbias_ref, prob_ref, gprob_ref,
):
    h = pl.program_id(0)
    b = pl.program_id(1)

    @pl.when(b == 0)
    def _():
        fill_bias(table_ref, h, bias_ref)
        gbias_ref[...] = jnp.zeros_like(gbias_ref)

    q = q_ref[...]
    gmix = gmix_ref[...]
    lse = lse_ref[...]
    first = b == 0
    keys = (
        ks_ref[...].reshape(BLK, HS),
        jnp.where(first, ko_ref[...], kp_ref[...]),
        kc_ref[...],
    )
    values = (
        vs_ref[...].reshape(BLK, HS),
        jnp.where(first, vo_ref[...], vp_ref[...]),
        vc_ref[...],
    )
    prior_ok = (run_ref[0] > 0) | (b > 0)
    inner = jnp.zeros((1, BLK), F32)
    grad_values = []
    for c in range(3):
        score = mm(keys[c], q, 1, 1) * SCALE
        if c == 1:
            score = jnp.where(prior_ok, score + bias_ref[:BLK], -1e30)
        if c == 2:
            score = jnp.where(current_mask(row_ref), score + bias_ref[BLK:], -1e30)
        prob = jnp.exp(score - lse)
        prob_ref[c] = prob
        grad_values.append(mm(prob.astype(LOW), gmix, 1, 0))
        grad_prob = mm(values[c], gmix, 1, 1)
        gprob_ref[c] = grad_prob
        inner = inner + jnp.sum(prob * grad_prob, axis=0, keepdims=True)
    grad_q = jnp.zeros((HS, BLK), F32)
    grad_keys = []
    for c in range(3):
        grad_score = (prob_ref[c] * (gprob_ref[c] - inner)).astype(LOW)
        if c > 0:
            gbias_ref[(c - 1) * BLK : c * BLK, :] += grad_score.astype(F32)
        grad_keys.append(mm(grad_score, q, 1, 0) * SCALE)
        grad_q = grad_q + mm(keys[c], grad_score, 0, 0)
    gq_ref[...] = (grad_q * SCALE).T.astype(LOW)
    part = gs_ref.shape[0], gs_ref.shape[1], HS
    gs_ref[:, :, :HS] = grad_keys[0].astype(LOW).reshape(part)
    gs_ref[:, :, HS:] = grad_values[0].astype(LOW).reshape(part)
    gprev_ref[:, :HS] = grad_keys[1].astype(LOW)
    gprev_ref[:, HS:] = grad_values[1].astype(LOW)
    gcur_ref[:, :HS] = grad_keys[2].astype(LOW)
    gcur_ref[:, HS:] = grad_values[2].astype(LOW)

    @pl.when(b == pl.num_programs(1) - 1)
    def _():
        collapse_bias(gbias_ref, gtab_ref)


def attend_back(run, table, q, kv, outer, sproj, ids_row, gmix, lse):
    rows = q.shape[0]
    heads = q.shape[1] // HS
    pieces, blocks, part, _ = sproj.shape

    def at():
        return pl.BlockSpec((BLK, HS), lambda h, b: (b, h))

    side = jax.ShapeDtypeStruct((rows, heads * 2 * HS), LOW)
    pair = pl.BlockSpec((BLK, 2 * HS), lambda h, b: (b, h))
    return pl.pallas_call(
        attend_back_kernel,
        grid=(heads, blocks),
        out_shape=(
            jax.ShapeDtypeStruct((rows, heads * HS), LOW),
            side,
            side,
            jax.ShapeDtypeStruct((pieces, blocks, part, heads * 2 * HS), LOW),
            jax.ShapeDtypeStruct((heads, 8, HS), F32),
        ),
        in_specs=attend_specs(heads, pieces, part, blocks)
        + [at(), pl.BlockSpec((None, None, 1, BLK), lambda h, b: (h, b, 0, 0))],
        out_specs=(
            at(),
            pair,
            pair,
            pl.BlockSpec((pieces, None, part, 2 * HS), lambda h, b: (0, b, 0, h)),
            pl.BlockSpec((None, 8, HS), lambda h, b: (h, 0, 0)),
        ),
        scratch_shapes=[
            pltpu.VMEM((2 * BLK, BLK), F32),
            pltpu.VMEM((2 * BLK, BLK), F32),
            pltpu.VMEM((3, BLK, BLK), F32),
            pltpu.VMEM((3, BLK, BLK), F32),
        ],
        compiler_params=params(2, 56),
        cost_estimate=lasts(16),
        name="attend_back",
    )(run, table, q, kv, kv, kv, kv, outer, outer, sproj, sproj, ids_row, gmix, lse)


def state_back_kernel(
    sq_ref, k_ref, v_ref, gmix_ref, gcur_ref, gnext_ref, gouter_ref,
    gkv_ref, gsq_ref, smix_ref,
):
    b = pl.program_id(1)
    last = b == pl.num_programs(1) - 1
    pieces, part = sq_ref.shape[0], sq_ref.shape[1]
    sq = sq_ref[...].reshape(BLK, HS)
    gmix = gmix_ref[...].reshape(BLK, HS)
    k, v = k_ref[...], v_ref[...]
    weights = column_softmax(mm(k, sq, 1, 1) * SCALE)
    low = weights.astype(LOW)
    grad_w = mm(v, gmix, 1, 1)
    inner = jnp.sum(grad_w * weights, axis=0, keepdims=True)
    grad_s = (weights * (grad_w - inner)).astype(LOW)
    grad_k = mm(grad_s, sq, 1, 0) * SCALE
    grad_v = mm(low, gmix, 1, 0)
    grad_q = mm(k, grad_s, 0, 0) * SCALE
    smix = mm(v, low, 0, 0)
    rest = gcur_ref[...].astype(F32) + jnp.where(last, gouter_ref[...], gnext_ref[...]).astype(F32)
    gkv_ref[:, :HS] = (rest[:, :HS] + grad_k).astype(LOW)
    gkv_ref[:, HS:] = (rest[:, HS:] + grad_v).astype(LOW)
    gsq_ref[...] = grad_q.T.astype(LOW).reshape(pieces, part, HS)
    smix_ref[...] = smix.T.astype(LOW).reshape(pieces, part, HS)


def state_back(sq, kv, gmix, gcur, gprev, outer):
    rows = gcur.shape[0]
    heads = gcur.shape[1] // (2 * HS)
    pieces, blocks, part, _ = sq.shape

    def at(col=lambda h: h):
        return pl.BlockSpec((BLK, HS), lambda h, b: (b, col(h)))

    def state():
        return pl.BlockSpec((pieces, None, part, HS), lambda h, b: (0, b, 0, h))

    side = jax.ShapeDtypeStruct((pieces, blocks, part, heads * HS), LOW)
    return pl.pallas_call(
        state_back_kernel,
        grid=(heads, blocks),
        out_shape=(jax.ShapeDtypeStruct((rows, heads * 2 * HS), LOW), side, side),
        in_specs=[
            state(),
            at(lambda h: 2 * h),
            at(lambda h: 2 * h + 1),
            state(),
            pl.BlockSpec((BLK, 2 * HS), lambda h, b: (b, h)),
            pl.BlockSpec((BLK, 2 * HS), lambda h, b: (jnp.minimum(b + 1, blocks - 1), h)),
            pl.BlockSpec((BLK, 2 * HS), lambda h, b: (0, h)),
        ],
        out_specs=(
            pl.BlockSpec((BLK, 2 * HS), lambda h, b: (b, h)),
            state(),
            state(),
        ),
        compiler_params=params(2, 16),
        cost_estimate=lasts(6.5),
        name="state_back",
    )(sq, kv, kv, gmix, gcur, gprev, outer)


def passed_along(array, axis, by):
    size = lax.axis_size(axis)
    pairs = [(i, i + by) for i in range(size) if 0 <= i + by < size]
    return lax.ppermute(array, axis, pairs)


def swap(array, axis, bits):
    return lax.ppermute(array, axis, [(i, i ^ bits) for i in range(lax.axis_size(axis))])


def far_pieces(array):
    return [array] + [swap(array, "tensor", m) for m in range(2, lax.axis_size("tensor"), 2)]


def chip_pieces(pieces, *fillers):
    out = []
    for j, piece in enumerate(pieces):
        if j and fillers:
            piece = after(piece, *fillers)
        out += [piece, swap(piece, "tensor", 1)]
    return out


def gather_rel(array, *fillers):
    return chip_pieces(far_pieces(array), *fillers)


def reduce_first(parts):
    size = len(parts)
    got = [swap(parts[m + 1], "tensor", 1) for m in range(0, size, 2)]
    sends = [
        (parts[m].astype(F32) + got[m // 2].astype(F32)).astype(LOW) for m in range(2, size, 2)
    ]
    return [parts[0], got[0]], sends


def reduce_last(own, sends, filler=None):
    terms = list(own)
    for j, send in enumerate(sends, 1):
        term = swap(send, "tensor", 2 * j)
        terms.append(term if filler is None else after(term, filler))
    return terms


def added(terms):
    return sum(term.astype(F32) for term in terms)


def exchange_rel(parts):
    return [part if m == 0 else swap(part, "tensor", m) for m, part in enumerate(parts)]


def cut(array, me):
    size = lax.axis_size("tensor")
    rows = array.shape[0] // size
    return [lax.dynamic_slice_in_dim(array, (me ^ m) * rows, rows, 0) for m in range(size)]


def place(pieces, me):
    rows = pieces[0].shape[0]
    out = jnp.zeros((rows * len(pieces),) + pieces[0].shape[1:], pieces[0].dtype)
    for m, piece in enumerate(pieces):
        out = lax.dynamic_update_slice_in_dim(out, piece, (me ^ m) * rows, 0)
    return out


def sum_all(array, *before_last):
    for axis in ("tensor", "shard", "context"):
        if axis == "context":
            array = after(array, *before_last)
        bits = 1
        while bits < lax.axis_size(axis):
            array = array + swap(array, axis, bits)
            bits *= 2
    return array


def rms_back(v, gain, grad):
    r = rms_scale(v)
    unit = v * r
    scaled = grad * gain
    return r * (scaled - unit * jnp.mean(scaled * unit, axis=-1, keepdims=True))


def dot(a, b, ca, cb):
    return lax.dot_general(a, b, (((ca,), (cb,)), ((), ())), preferred_element_type=F32)


def after(array, *others):
    return lax.optimization_barrier((array,) + others)[0]


def half_rows(local, run):
    part = local.shape[0] // 2
    return lax.dynamic_slice_in_dim(local, run * part, part, 0)


def shard_pieces(array):
    return [array if s == 0 else swap(array, "shard", s) for s in range(lax.axis_size("shard"))]


def scatter_rows(grad):
    return lax.psum_scatter(grad, "shard", scatter_dimension=0, tiled=True)


def shards(
    tokens,
    piece_ids,
    tok_qkv,
    state_qkv,
    tok_out,
    state_out,
    mlp_in,
    mlp_out,
    rel_bias,
    init_state,
    norm_gains,
    decay_param,
    cotangent,
):
    size = lax.axis_size("tensor")
    shard_count = lax.axis_size("shard")
    me = lax.axis_index("tensor")
    shard_pos = lax.axis_index("shard")
    run_pos = lax.axis_index("context")
    run_count = lax.axis_size("context")
    me_arr = me.astype(jnp.int32)[None]
    run_arr = run_pos.astype(jnp.int32)[None]
    pos = jnp.stack([shard_pos, run_pos]).astype(jnp.int32)
    own = tokens[0]
    own_rows, width = own.shape
    rows = own_rows * size
    blocks = rows // BLK
    heads = tok_qkv.shape[1]
    part = init_state.shape[0]
    span = heads * HS

    cols = norm_gains.shape[1]
    bias_rows = rel_bias.shape[0]
    slot_size = NBUCKET * heads
    small = jnp.zeros((SMALL, width), LOW)
    small = lax.dynamic_update_slice(
        small, jnp.concatenate([norm_gains, decay_param[None]], 0), (0, (shard_pos * size + me) * cols)
    )
    small = lax.dynamic_update_slice(
        small, rel_bias.reshape(1, -1), (4, me * slot_size + shard_pos * bias_rows * heads)
    )

    local_chain = jnp.concatenate(
        [state_qkv[:, :, :HS].reshape(-1, span), state_out.reshape(span, -1).T, init_state.T], axis=1
    )
    chain_pieces = shard_pieces(half_rows(local_chain, run_pos))
    local_tok = jnp.concatenate(
        [tok_qkv[:, :, HS:].reshape(-1, 2 * span), tok_qkv[:, :, :HS].reshape(-1, span)], axis=1
    )
    token_far = far_pieces(jnp.concatenate([own, small], axis=0))
    local_tok = after(local_tok, *token_far[1:], *chain_pieces)
    w_tok = lax.all_gather(local_tok, "shard", axis=0, tiled=True)
    token_pieces = chip_pieces(token_far, *chain_pieces)
    chain_other = swap(jnp.stack(chain_pieces), "context", 1)
    chain_own, start = assemble(pos, chain_pieces, chain_other, (2 * span, part))
    chip_own = swap(chain_own, "tensor", 1)
    small = sum(piece[own_rows:].astype(F32) for piece in token_pieces).astype(LOW)
    small_pieces = shard_pieces(after(small, chip_own))
    start = start.astype(F32).T
    small_pieces = [after(piece, start) for piece in small_pieces]
    w_sq, w_sout = (chain_own, span, 0), (chain_own, span, 1)

    chain_w = [chain_own, chip_own] + gather_rel(chain_own)[2:]

    local_side = jnp.concatenate(
        [state_qkv[:, :, HS:].reshape(-1, 2 * span), tok_out.reshape(span, -1).T], axis=1
    )
    local_mlp = jnp.concatenate([mlp_in, mlp_out.T], axis=1)

    w_side = lax.all_gather(after(local_side, chain_own), "shard", axis=0, tiled=True)
    w_skv, w_tout = (w_side, 2 * span, 0), w_side[:, 2 * span :]

    q, normed_a, vectors, kv, *kv_blocks = token_proj(
        me_arr, token_pieces, small_pieces, after(w_tok, *chain_w[2::2]), blocks
    )
    gains = vectors[:3]
    decay = jax.nn.sigmoid(vectors[3:4])
    table = lax.dynamic_slice_in_dim(vectors[4], me * slot_size, slot_size, 0)
    table = table.reshape(NBUCKET, heads).T
    kv_pieces = [gather_rel(kv_blocks[0])]

    w_mlp = lax.all_gather(after(local_mlp, q), "shard", axis=0, tiled=True)

    ids_row = piece_ids.reshape(blocks, 1, BLK)
    zero_arr = jnp.zeros((1,), jnp.int32)
    gain_s = gains[2:3]
    got, flag = jnp.zeros((part, width), LOW), zero_arr
    for round_index in range(run_count):
        state = start
        states, normeds, updates = [], [], []
        for b in range(blocks):
            if b == len(kv_pieces):
                kv_pieces.append(gather_rel(after(kv_blocks[b], *kv_pieces[-1][2::2]), state))
            if round_index + b == run_count:
                state = after(state, outer, *tout_far)
            state, pair, update, following, low = chain_forward(
                zero_arr if b else flag, state, got, gain_s, decay, kv_pieces[b], chain_w,
                round_index > 0,
            )
            if round_index + b == 0:
                outer = passed_along(after(kv_blocks[-1], low), "context", 1)
            states.append(state)
            normeds.append(pair)
            updates.append(update)
            state = following
        if round_index + 1 < run_count:
            got, flag = passed_along(low, "context", 1), run_arr
            if round_index == 0:
                grad_far = far_pieces(after(cotangent[0], *kv_pieces[-1][2::2]))
                tout_far = far_pieces(after(w_tout, *grad_far))
                got = after(got, *grad_far)
    units = mlp_in.shape[1]
    w_in, w_out = (w_mlp, units, 0), (w_mlp, units, 1)
    normed_s = stacked([pair for pair in normeds[::2]])[: blocks * part]
    state_pieces = gather_rel(normed_s, updates[-1])
    sq, skv = proj(state_pieces, [w_sq, w_skv])
    sq = sq.reshape(size, blocks, part, span)
    skv = skv.reshape(size, blocks, part, 2 * span)

    mixed, lse = attend(run_arr, table, q, kv, outer, skv, ids_row)
    grad_pieces = chip_pieces(grad_far, mixed)
    tout_pieces = chip_pieces(tout_far, mixed)
    mixed_parts = cut(mixed, me)
    residual, normed_m, squares = branch_out(own, gains[1:2], exchange_rel(mixed_parts), tout_pieces)

    (grad_hidden,) = proj([after(piece, normed_m) for piece in grad_pieces], [w_out])
    mlp_pieces = gather_rel(normed_m, grad_hidden)
    hidden, grad_pre, *parts = feed(w_in, grad_hidden, mlp_pieces)
    sums, sends = reduce_first(parts)
    grad_w_mlp = weight_grad([(mlp_pieces, after(grad_pre, *sends)), (grad_pieces, hidden)])
    terms = reduce_last(sums, sends, grad_w_mlp)
    mlp_mine = scatter_rows(after(grad_w_mlp, *terms))

    grad_res, grad_branch, grad_gain_m, *gmix_parts = branch_back(
        cotangent[0], residual, gains[1:2], terms, tout_pieces
    )
    gmix = place(exchange_rel(gmix_parts), me)
    gq, gcur, gprev, gs, gtab = attend_back(
        run_arr, table, q, kv, outer, skv, ids_row, gmix, lse
    )
    branch_pieces = gather_rel(after(grad_branch, gmix), gq)
    gs = after(gs, branch_pieces[-2])
    outer_back = passed_along(gprev[:BLK], "context", -1)

    gs = gs.reshape(-1, 2 * span)
    sums, sends = reduce_first(back(zero_arr, [gs], [w_skv]))
    parts = back(zero_arr, [after(hidden, *sends)], [w_out])
    state_terms = reduce_last(sums, sends, parts[0])
    state_terms[0] = after(state_terms[0], outer_back)
    sums, sends = reduce_first(parts)
    branch_m = reduce_last(sums, [after(send, *state_terms) for send in sends])

    got, flag = jnp.zeros((part, width), LOW), zero_arr
    not_last = (run_pos != run_count - 1).astype(jnp.int32)[None]
    for round_index in range(run_count):
        carry = jnp.zeros_like(start)
        gups = [None] * blocks
        chain_small = jnp.zeros((2, width), F32)
        for b in reversed(range(blocks)):
            carry, low, pair, row_sums = chain_backward(
                flag if b == blocks - 1 else zero_arr, carry, got, gain_s, decay, states[b], normed_s,
                updates[b], b, state_terms, kv_pieces[b], chain_w, round_index > 0,
            )
            chain_small = chain_small + row_sums
            gups[b] = pair
        if round_index + 1 < run_count:
            got, flag = passed_along(low, "context", -1), not_last
            if round_index == 0:
                grad_w_early = weight_grad(
                    [
                        ([normed_a], after(gq, carry)),
                        (state_pieces, gs),
                        (branch_pieces, jnp.concatenate(mixed_parts, axis=0)),
                    ]
                )
                got = came = after(got, grad_w_early, *branch_m)
    gup_all = stacked([gups[b] for b in range(blocks - 1, 0, -2)][::-1])
    grad_start = jnp.where(run_pos == 0, carry, 0.0).astype(LOW)
    branch_m = added(branch_m)
    output = (residual + branch_m).astype(LOW)
    mlp_halves = [after(mlp_mine[:, i * units : (i + 1) * units], gup_all) for i in range(2)]
    mlp_got = [swap(mlp_halves[0], "context", 1)]
    gup_pieces = gather_rel(gup_all, carry, mlp_got[0])
    early_mine = scatter_rows(after(grad_w_early, came))
    (gsmix,) = proj(gup_pieces, [w_sout])
    gsmix = gsmix.reshape(size, blocks, part, span)
    gkv, gsq, smix = state_back(sq, kv, gsmix, gcur, gprev, outer_back)
    grad_w_late = weight_grad(
        [([normed_a], gkv), (state_pieces, gsq.reshape(-1, span)), (gup_pieces, smix.reshape(-1, span))],
        [grad_start.T],
    )
    mlp_got.append(swap(after(mlp_halves[1], grad_w_late), "context", 1))
    early_got = swap(after(early_mine, grad_w_late), "context", 1)
    late_mine = scatter_rows(grad_w_late)
    g_in, g_out = (
        half.astype(F32) + other.astype(F32) for half, other in zip(mlp_halves, mlp_got, strict=True)
    )
    g_early = early_mine.astype(F32) + early_got.astype(F32)
    g_late = late_mine.astype(F32) + swap(late_mine, "context", 1).astype(F32)

    *parts, gain_sums = back(
        me_arr,
        [gq, after(gkv, grad_w_late)],
        [(w_tok, span, 2), (w_tok, 2 * span, 0)],
        normed_a,
    )
    grad_gain_a = (gain_sums / gains[0:1])[0]
    inputs = own.astype(F32)
    terms = reduce_last(*reduce_first(parts))
    grad_normed_a = added(terms)
    grad_tokens = (grad_res + rms_back(inputs, gains[0], grad_normed_a)).astype(LOW)

    def by_head(array):
        return array.reshape(array.shape[0], heads, -1)

    g_tok = jnp.concatenate([by_head(g_early[:, :span]), by_head(g_late[:, : 2 * span])], axis=2)
    g_state = jnp.concatenate(
        [by_head(g_late[:, 2 * span : 3 * span]), by_head(g_early[:, span : 3 * span])], axis=2
    )
    g_tout = g_early[:, 3 * span :].T.reshape(heads, HS, -1)
    g_sout = g_late[:, 3 * span : 4 * span].T.reshape(heads, HS, -1)

    squares = jnp.concatenate([jnp.sum(squares, axis=1), jnp.sum(branch_m * branch_m)[None]])
    slot = gtab[:, 0, :NBUCKET].reshape(-1)
    slots = lax.dynamic_update_slice_in_dim(
        jnp.zeros((size * slot.size,), F32), slot, me * slot.size, 0
    )
    tail = jnp.concatenate([slots, squares])
    tail = jnp.pad(tail, (0, width - tail.size))
    grad_decay = chain_small[1] * (decay * (1.0 - decay))[0]
    sums = sum_all(
        jnp.stack([grad_gain_a, grad_gain_m[0], chain_small[0], grad_decay, tail]),
        early_got,
        mlp_got[1],
        *terms,
    )
    place_at = (shard_pos * size + me) * cols
    mine = lax.dynamic_slice_in_dim(sums[:4], place_at, cols, 1)
    table_sum = lax.dynamic_slice_in_dim(sums[4], me * slot.size, slot.size, 0)
    table_sum = table_sum.reshape(heads, NBUCKET).T
    g_table = lax.dynamic_slice_in_dim(table_sum, shard_pos * bias_rows, bias_rows, 0)
    entries = own.size * shard_count * run_count * size
    first = size * slot.size
    rms_out = jnp.sqrt(sums[4, first : first + 3] / entries)

    return (
        output[None],
        grad_tokens[None],
        g_tok,
        g_state,
        g_tout,
        g_sout,
        g_in,
        g_out.T,
        g_table,
        g_late[:, 4 * span :].T,
        mine[:3],
        mine[3],
        rms_out,
    )


def solution(mesh):
    return jax.shard_map(
        shards,
        mesh=mesh,
        in_specs=(
            P("shard", ("context", "tensor"), None),
            P("shard", "context"),
            P("shard", "tensor", None),
            P("shard", "tensor", None),
            P("tensor", None, "shard"),
            P("tensor", None, "shard"),
            P("shard", "tensor"),
            P("tensor", "shard"),
            P("shard", "tensor"),
            P("tensor", "shard"),
            P(None, ("shard", "tensor")),
            P(("shard", "tensor")),
            P("shard", ("context", "tensor"), None),
        ),
        out_specs=(
            P("shard", ("context", "tensor"), None),
            P("shard", ("context", "tensor"), None),
            P("shard", "tensor", None),
            P("shard", "tensor", None),
            P("tensor", None, "shard"),
            P("tensor", None, "shard"),
            P("shard", "tensor"),
            P("tensor", "shard"),
            P("shard", "tensor"),
            P("tensor", "shard"),
            P(None, ("shard", "tensor")),
            P(("shard", "tensor")),
            P(),
        ),
        check_vma=False,
    )
```
